32 devices in a mesh: dp: 8 (over z, x), table: 4 (over y, core).
Axes of the slice: x: 2, y: 2, z: 4, core: 2. Of those that a mesh axis runs over, the one named last changes fastest.
Arguments:
- feature_high: int32 [20, 2048], P(None, 'dp'), may hold values from 0 to 2047
- feature_low: int32 [20, 2048], P(None, 'dp'), may hold values from 0 to 2047
- labels: int32 [2048], P('dp'), may hold values 0 or 1
- weights: float32 [4194304], P(('dp', 'table')), may hold values from -0.6 to 0.6
- history_steps: float32 [8, 4194304], P(None, ('dp', 'table')), may hold values from -46 to 46
- history_diffs: float32 [8, 4194304], P(None, ('dp', 'table')), may hold values from -198 to 198, as said below
Outputs:
- direction: float32 [4194304], P(('dp', 'table'))
The draws below stay inside these ranges and needn't reach their ends.
Inputs may be any that keep to these rules, and one draw needn't show every extreme that they name: Each entry of history_diffs has the sign of the matching entry of history_steps and 0.2 to 4.3 times its magnitude.
All inputs are finite; a program needn't handle non-finite values. No bound on the sum of `labels` on one device may be relied on, other than what follows from the above.
Results may differ from the reference program's by a relative error of at most 0.0001.
Values sent between devices are 32-bit elements; how exact they have to be, the bound alone decides.
A program may use at most 64 MiB of HBM per device.

```python
import jax
import jax.numpy as jnp

TABLE = 4194304
SLOTS = 20
HASHES = 4
MEM = 8
EX_DEV = 256
EXAMPLES = 2048


def feature_pair(key):
    base_key = jax.random.fold_in(key, 31)
    keys = jax.random.split(base_key, 9)
    dp_count = EXAMPLES // EX_DEV
    block_width = TABLE // (dp_count * 4)
    spread_count = max(1, block_width // 2053)
    tops = jax.random.randint(keys[0], (SLOTS, EXAMPLES), 1, 2049)
    raw_high = jax.random.randint(keys[1], (SLOTS, EXAMPLES), 0, tops)
    odd_mult = 2 * jax.random.randint(keys[2], (SLOTS, 1), 0, 1024) + 1
    offset = jax.random.randint(keys[3], (SLOTS, 1), 0, 2048)
    high = (raw_high * odd_mult + offset) % 2048
    low = jax.random.randint(keys[4], (SLOTS, EXAMPLES), 0, 2048)
    chosen_device = jax.random.randint(keys[5], (), 0, dp_count)
    target_block = jax.random.randint(keys[6], (), 0, dp_count * 4)
    example = jnp.arange(EXAMPLES, dtype=jnp.int32)[None, :]
    picked = jax.random.randint(keys[7], (1, EXAMPLES), 0, 2) == 1
    crowded = (example // EX_DEV == chosen_device) & picked
    slot_index = jnp.arange(SLOTS, dtype=jnp.int32)[:, None]
    block_start = target_block * block_width
    remainder = (block_start - high * 40503 % TABLE - slot_index * 1543) % TABLE
    first_low = (remainder + 2052) // 2053
    nudge = jax.random.randint(keys[8], (SLOTS, EXAMPLES), 0, spread_count)
    aimed = (first_low + nudge) % 2048
    low = jnp.where(crowded, aimed, low)
    return (high.astype(jnp.int32), low.astype(jnp.int32))


def draw_feature_high(key, part):
    return feature_pair(key)[0]


def draw_feature_low(key, part):
    return feature_pair(key)[1]


def history_pair(key):
    base_key = jax.random.fold_in(key, 77)
    first, second, third, fourth = jax.random.split(base_key, 4)
    spot = jnp.arange(TABLE, dtype=jnp.float32)[None, :] / (TABLE - 1)
    order = jax.random.permutation(fourth, MEM)
    top_row = order[:, None] == MEM - 1
    column = jnp.arange(TABLE, dtype=jnp.int32)[None, :]
    base = jnp.clip(jax.random.normal(first, (MEM, TABLE), jnp.float32), -4.0, 4.0)
    ramp = 1.0 + 2.0 * spot
    steps = base * ramp
    plant_up = top_row & (column == TABLE - 1)
    plant_down = top_row & (column == TABLE - 2)
    steps = jnp.where(plant_up, 46.0, jnp.where(plant_down, -46.0, steps))
    factor = jnp.exp(jax.random.uniform(second, (MEM, TABLE), jnp.float32, jnp.log(0.5), jnp.log(4.0)))
    factor = factor + 0.3 * jax.random.uniform(third, (MEM, TABLE), jnp.float32, -1.0, 1.0)
    factor = jnp.where(plant_up | plant_down, 4.3, factor)
    return (steps, steps * factor)


def draw_history_steps(key, part):
    return history_pair(key)[0]


def draw_history_diffs(key, part):
    return history_pair(key)[1]


def plant(result, own_key, smallest, top_value):
    extent = result.shape
    place = [jax.random.randint(jax.random.fold_in(own_key, axis), (), 0, extent[axis]) for axis in range(len(extent))]
    result = result.at[tuple(place)].set(smallest)
    longest = extent.index(max(extent))
    place[longest] = (place[longest] + 1) % extent[longest]
    return result.at[tuple(place)].set(top_value)


def block_scale(stream_key, extent, cuts, least, top_value):
    level = 1.0
    for position, parts in cuts:
        draws = jax.random.uniform(jax.random.fold_in(jax.random.fold_in(stream_key, 6), position), (parts,), jnp.float32, least / len(cuts), top_value / len(cuts))
        level = level * jnp.repeat(jnp.exp(draws), extent[position] // parts).reshape((-1,) + (1,) * (len(extent) - 1 - position))
    return level


def bell_draw(own_key, dims, width, bound, cuts=(), kind=jnp.bfloat16):
    gain = block_scale(own_key, dims, cuts, -0.22, 0.18) if cuts else 1.0
    result = jax.random.normal(own_key, dims, jnp.float32) * width * gain
    return jnp.minimum(jnp.maximum(result, -bound), bound).astype(kind)


def setup_inputs(seed: int = 0) -> dict:
    seeds = jax.random.split(jax.random.key(seed), 7)
    return {
        "feature_high": draw_feature_high(jax.random.fold_in(seeds[6], 71), 0),
        "feature_low": draw_feature_low(jax.random.fold_in(seeds[6], 71), 0),
        "labels": plant((jax.random.randint(seeds[2], (EXAMPLES,), 0, 4) < 1).astype(jnp.int32), jax.random.fold_in(seeds[2], 1), 0, 1),
        "weights": bell_draw(seeds[3], (TABLE,), 0.1, 0.6, ((0, 32),), jnp.float32),
        "history_steps": draw_history_steps(jax.random.fold_in(seeds[6], 71), 0),
        "history_diffs": draw_history_diffs(jax.random.fold_in(seeds[6], 71), 0),
    }


high_mult = (40503, 96469, 255361, 362443)
low_mult = (2053, 6151, 12289, 98317)
slot_mult = (1543, 3079, 769, 3457)
shifts = (0, 1048573, 2097143, 3145727)
l2_weight = 1.0


def hashed(feature_high, feature_low, number):
    slot_index = jnp.arange(feature_high.shape[0], dtype=jnp.int32)[:, None]
    part_high = (feature_high * high_mult[number]) % TABLE
    part_low = (feature_low * low_mult[number]) % TABLE
    return ((part_high + part_low + slot_index * slot_mult[number] + shifts[number]) % TABLE).astype(jnp.int32)


def reference(feature_high, feature_low, labels, weights, history_steps, history_diffs):
    margin = jnp.zeros((feature_high.shape[1],), jnp.float32)
    for number in range(HASHES):
        indices = hashed(feature_high, feature_low, number)
        margin = margin + jnp.sum(weights[indices], axis=0)
    residual = jax.nn.sigmoid(margin) - labels.astype(jnp.float32)
    gradient = jnp.zeros((TABLE,), jnp.float32)
    for number in range(HASHES):
        indices = hashed(feature_high, feature_low, number)
        spread = jnp.broadcast_to(residual[None, :], indices.shape)
        gradient = gradient.at[indices.reshape(-1)].add(spread.reshape(-1))
    gradient = gradient + l2_weight * weights
    inverse = [1.0 / jnp.sum(history_steps[which] * history_diffs[which]) for which in range(MEM)]
    current = gradient
    alphas = [None] * MEM
    for which in reversed(range(MEM)):
        alphas[which] = inverse[which] * jnp.sum(history_steps[which] * current)
        current = current - alphas[which] * history_diffs[which]
    newest = MEM - 1
    scaling = jnp.sum(history_steps[newest] * history_diffs[newest]) / jnp.sum(history_diffs[newest] * history_diffs[newest])
    current = scaling * current
    for which in range(MEM):
        correction = inverse[which] * jnp.sum(history_diffs[which] * current)
        current = current + (alphas[which] - correction) * history_steps[which]
    return -current
```

```python
import functools

import jax
import jax.numpy as jnp
from jax import lax
from jax.experimental import pallas as pl
from jax.experimental.pallas import tpu as pltpu
from jax.sharding import PartitionSpec as P

HASHES = 4
LANES = 128
BLOCK = 16
GROUP = 4
DEPTH = 24
CAP = 40
WIDE = 8
UNROLL = 1

high_mult = (40503, 96469, 255361, 362443)
low_mult = (2053, 6151, 12289, 98317)
slot_mult = (1543, 3079, 769, 3457)
shifts = (0, 1048573, 2097143, 3145727)
l2_weight = 1.0
BUDGET = 50 << 20
F32, BF16, I32 = jnp.float32, jnp.bfloat16, jnp.int32
MESH = pl.DeviceIdType.MESH
VMEM = pl.BlockSpec(memory_space=pltpu.VMEM)
HBM = pl.BlockSpec(memory_space=pltpu.HBM)
SMEM = pl.BlockSpec(memory_space=pltpu.SMEM)


def iota(shape, axis):
    return lax.broadcasted_iota(I32, shape, axis)


def split(value):
    top = value.astype(BF16)
    return top, (value - top.astype(F32)).astype(BF16)


def hot(index, count):
    shape = (count, index.shape[1])
    return jnp.where(iota(shape, 0) == index, 1.0, 0.0).astype(BF16)


def greet(peers):
    barrier = pltpu.get_barrier_semaphore()
    for peer in peers:
        pl.semaphore_signal(barrier, inc=1, device_id=peer, device_id_type=MESH)
    pl.semaphore_wait(barrier, len(peers))


def others(axis):
    size, me = lax.axis_size(axis), lax.axis_index(axis)
    return [{axis: lax.rem(me + step, size)} for step in range(1, size)]


def send(source, target, peers, send_sems, recv_sems):
    copies = []
    for number, peer in enumerate(peers):
        copy = pltpu.make_async_remote_copy(
            src_ref=source,
            dst_ref=target,
            send_sem=send_sems.at[number],
            recv_sem=recv_sems.at[number],
            device_id=peer,
            device_id_type=MESH,
        )
        copy.start()
        copies.append(copy)
    return copies


def stage(axis, held, value, sems):
    me = lax.axis_index(axis)
    held[me] = value
    return send(held.at[me], held.at[me], others(axis), *sems)


def finish(copies, held):
    for copy in copies:
        copy.wait()
    total = held[0]
    for number in range(1, held.shape[0]):
        total = total + held[number]
    return total


def sum_scratch(shape):
    near, far = lax.axis_size("table"), lax.axis_size("dp")
    return [
        pltpu.VMEM((near, *shape), F32),
        pltpu.VMEM((far, *shape), F32),
        pltpu.SemaphoreType.DMA((near - 1,)),
        pltpu.SemaphoreType.DMA((near - 1,)),
        pltpu.SemaphoreType.DMA((far - 1,)),
        pltpu.SemaphoreType.DMA((far - 1,)),
    ]


def load(steps_hbm, diffs_hbm, steps, diffs, sems, first=0):
    parts, width = sems.shape[1], steps.shape[1]
    pairs = []
    for part in range(parts):
        size = width // parts
        pair = []
        for kind, (source, target) in enumerate(((steps_hbm, steps), (diffs_hbm, diffs))):
            copy = pltpu.make_async_copy(
                source.at[:, pl.ds(first + part * size, size)],
                target.at[:, pl.ds(part * size, size)],
                sems.at[kind, part],
            )
            copy.start()
            pair.append(copy)
        pairs.append(pair)
    return pairs


def gram_part(steps, diffs, pairs, part, carry):
    mem = steps.shape[0]
    each = steps.shape[1] // len(pairs) // LANES
    for copy in pairs[part]:
        copy.wait()

    def body(number, carry):
        at = pl.ds(pl.multiple_of(number * LANES, LANES), LANES)
        step, diff = steps[:, at], diffs[:, at]
        new = []
        for i in range(mem):
            row = jnp.broadcast_to(diffs[i : i + 1, at], diff.shape)
            new.append(carry[2 * i] + step * row)
            new.append(carry[2 * i + 1] + diff * row)
        return tuple(new)

    return lax.fori_loop(part * each, (part + 1) * each, body, carry, unroll=4)


def to_row(columns):
    mem = columns[0].shape[0]
    total = jnp.zeros((mem, LANES), F32)
    spot = iota((mem, LANES), 1) - iota((mem, LANES), 0)
    for number, column in enumerate(columns):
        total = jnp.where(spot == number * mem, jnp.sum(column, axis=1, keepdims=True), total)
    return jnp.sum(total, axis=0, keepdims=True)


def from_row(row, number, mem):
    spot = iota((mem, LANES), 1) - iota((mem, LANES), 0)
    wide = jnp.broadcast_to(row, (mem, LANES))
    column = jnp.sum(jnp.where(spot == number * mem, wide, 0.0), axis=1, keepdims=True)
    return jnp.broadcast_to(column, (mem, LANES))


def gram_row(carry, mem):
    return to_row([carry[2 * i] for i in range(mem)] + [carry[2 * i + 1] for i in range(mem)])


def share_kernel(mine_ref, steps_hbm, diffs_hbm, every_ref, gram_ref,
                 steps, diffs, send_sems, recv_sems, sems):
    mem = steps.shape[0]
    pairs = load(steps_hbm, diffs_hbm, steps, diffs, sems)
    me = lax.axis_index("dp")
    every_ref[me] = mine_ref[...]
    peers = others("dp")
    greet(peers)
    sent = send(mine_ref, every_ref.at[me], peers, send_sems, recv_sems)
    carry = (jnp.zeros((mem, LANES), F32),) * (2 * mem)
    for part in range(len(pairs)):
        carry = gram_part(steps, diffs, pairs, part, carry)
    gram_ref[...] = gram_row(carry, mem)
    for copy in sent:
        copy.wait()


def share(mine, steps, diffs):
    mem, width = steps.shape
    dp = lax.axis_size("dp")
    return pl.pallas_call(
        share_kernel,
        in_specs=[VMEM] + [HBM] * 2,
        out_specs=[VMEM] * 2,
        out_shape=[
            jax.ShapeDtypeStruct((dp, *mine.shape), I32),
            jax.ShapeDtypeStruct((1, LANES), F32),
        ],
        scratch_shapes=[
            pltpu.VMEM((mem, 3 * width // 4), F32),
            pltpu.VMEM((mem, 3 * width // 4), F32),
            pltpu.SemaphoreType.DMA((dp - 1,)),
            pltpu.SemaphoreType.DMA((dp - 1,)),
            pltpu.SemaphoreType.DMA((2, 3)),
        ],
        compiler_params=pltpu.CompilerParams(
            vmem_limit_bytes=BUDGET, collective_id=0, has_side_effects=True
        ),
        name="share",
    )(mine, steps, diffs)


def reduce_kernel(margin_ref, gram_ref, steps_hbm, diffs_hbm, out_ref, grams_ref,
                  steps, diffs, load_sems, near, far, *sems):
    mem, size = steps.shape
    pairs = load(steps_hbm, diffs_hbm, steps, diffs, load_sems, steps_hbm.shape[1] - size)
    greet(others("table") + others("dp"))
    carry = (jnp.zeros((mem, LANES), F32),) * (2 * mem)
    copies = stage("table", near, margin_ref[...], sems[:2])
    copies = stage("dp", far, finish(copies, near), sems[2:])
    carry = gram_part(steps, diffs, pairs, 0, carry)
    grams_ref[...] = gram_ref[...] + gram_row(carry, mem)
    out_ref[...] = finish(copies, far)


def reduced(margin, grams, steps, diffs):
    mem, width = steps.shape
    return pl.pallas_call(
        reduce_kernel,
        in_specs=[VMEM] * 2 + [HBM] * 2,
        out_specs=[VMEM] * 2,
        out_shape=[
            jax.ShapeDtypeStruct(margin.shape, F32),
            jax.ShapeDtypeStruct((1, LANES), F32),
        ],
        scratch_shapes=[
            pltpu.VMEM((mem, width // 4), F32),
            pltpu.VMEM((mem, width // 4), F32),
            pltpu.SemaphoreType.DMA((2, 1)),
        ]
        + sum_scratch(margin.shape),
        compiler_params=pltpu.CompilerParams(
            vmem_limit_bytes=BUDGET, collective_id=1, has_side_effects=True
        ),
        name="reduce",
    )(margin, grams, steps, diffs)


def margin_kernel(count, subs, bits, slot_total, every_ref, weights_ref, margin_ref, slots_ref, levels_ref, table, features):
    device = lax.axis_index("dp") * lax.axis_size("table") + lax.axis_index("table")
    width = 1 << bits
    for number in range(2 * slot_total):
        features[number] = every_ref[:, number, :]
    tops, rests = split(weights_ref[...].T)
    table[: LANES] = tops
    table[LANES :] = rests

    def one_pass(number, _):
        base = number * BLOCK

        def body(slot, carry):
            seen, outs = carry[0], list(carry[1:])
            for sub in range(subs):
                group, half = sub // 2, sub % 2
                at = (pl.ds(group * 8, 8), pl.ds(half * LANES, LANES))
                high, low = features[(slot, *at)], features[(slot + slot_total, *at)]
                for k in range(HASHES):
                    index = (high * high_mult[k] + low * low_mult[k] + (slot * slot_mult[k] + shifts[k])) & (count - 1)
                    owned = (index >> bits) == device
                    place = jnp.where(owned, seen, -1)
                    code = (index & (width - 1)) | (sub << bits)
                    for level in range(BLOCK):
                        outs[level] = jnp.where(place == level, code, outs[level])
                    seen = seen + owned.astype(I32)
            return (seen, *outs)

        empty = jnp.full((8, LANES), -1, I32)
        final = lax.fori_loop(0, slot_total, body, (jnp.zeros((8, LANES), I32) - base,) + (empty,) * BLOCK)
        for level in range(BLOCK):
            slots_ref[:, base + level, :] = final[1 + level]
        return final[0] + base

    seen = one_pass(0, None)
    most = jnp.max(seen)
    lax.fori_loop(1, (most + BLOCK - 1) // BLOCK, lambda n, c: (one_pass(n, None), c)[1], 0)
    for row in range(8):
        levels_ref[row] = (jnp.max(seen[row : row + 1]) + GROUP - 1) // GROUP

    def rows(row, _):
        def body(number, total):
            codes = slots_ref[row, pl.ds(number * GROUP, GROUP), :]
            code = jnp.concatenate([codes[i : i + 1] for i in range(GROUP)], axis=1)
            local = code & (width - 1)
            found = jnp.dot(table[...], hot(local >> 7, width // LANES), preferred_element_type=F32)
            found = found[:LANES] + found[LANES:]
            chosen = jnp.where(iota(found.shape, 0) == (local & (LANES - 1)), found, 0.0)
            value = jnp.sum(chosen, axis=0, keepdims=True)
            sub = code >> bits
            for i in range(GROUP):
                at = slice(i * LANES, (i + 1) * LANES)
                total = total + jnp.where(iota((subs, LANES), 0) == sub[:, at], value[:, at], 0.0)
            return total

        total = lax.fori_loop(0, levels_ref[row], body, jnp.zeros((subs, LANES), F32))
        for sub in range(subs):
            here = iota((8, LANES), 0) == row
            margin_ref[sub] = jnp.where(here, total[sub : sub + 1], margin_ref[sub])
        return 0

    margin_ref[...] = jnp.zeros_like(margin_ref)
    lax.fori_loop(0, 8, rows, 0)


def margins(every, weights, count, subs, bits, slots):
    levels = -(-subs * HASHES * slots // BLOCK) * BLOCK
    return pl.pallas_call(
        functools.partial(margin_kernel, count, subs, bits, slots),
        in_specs=[VMEM] * 2,
        out_specs=[VMEM, VMEM, SMEM],
        out_shape=[
            jax.ShapeDtypeStruct((subs, 8, LANES), F32),
            jax.ShapeDtypeStruct((8, levels, LANES), I32),
            jax.ShapeDtypeStruct((8,), I32),
        ],
        scratch_shapes=[
            pltpu.VMEM((2 * LANES, (1 << bits) // LANES), BF16),
            pltpu.VMEM((2 * slots, every.shape[0], every.shape[2]), I32),
        ],
        compiler_params=pltpu.CompilerParams(vmem_limit_bytes=BUDGET),
        name="margins",
    )(every, weights)


def gradient_kernel(subs, bits, label_row, total_ref, every_ref, slots_ref, levels_ref, weights_ref,
                    gradient_ref, residual, both):
    width = 1 << bits
    for sub in range(subs):
        label = every_ref[sub // 2 * 8 : sub // 2 * 8 + 8, label_row, sub % 2 * LANES : sub % 2 * LANES + LANES]
        residual[:, sub, :] = 1.0 / (1.0 + jnp.exp(-total_ref[sub])) - label.astype(F32)
    both[...] = jnp.zeros_like(both)

    def rows(row, _):
        value = residual[row]

        def body(number, _):
            codes = slots_ref[row, pl.ds(number * GROUP, GROUP), :]
            code = jnp.concatenate([codes[i : i + 1] for i in range(GROUP)], axis=1)
            local = code & (width - 1)
            sub = code >> bits
            wide = jnp.concatenate([value] * GROUP, axis=1)
            mine = jnp.sum(jnp.where(iota(wide.shape, 0) == sub, wide, 0.0), axis=0, keepdims=True)
            column = iota((LANES, GROUP * LANES), 0) == (local & (LANES - 1))
            top, rest = split(jnp.where(column, mine, 0.0))
            terms = jnp.concatenate([top, rest], axis=0)
            both[...] += lax.dot_general(
                hot(local >> 7, width // LANES), terms, (((1,), (1,)), ((), ())), preferred_element_type=F32
            )
            return 0

        lax.fori_loop(0, levels_ref[row], body, 0)
        return 0

    lax.fori_loop(0, 8, rows, 0)
    gradient_ref[...] = both[:, :LANES] + both[:, LANES:] + l2_weight * weights_ref[...]


def gradients(total, every, slots, levels, weights, subs, bits, label_row):
    return pl.pallas_call(
        functools.partial(gradient_kernel, subs, bits, label_row),
        in_specs=[VMEM, VMEM, VMEM, SMEM, VMEM],
        out_specs=VMEM,
        out_shape=jax.ShapeDtypeStruct(weights.shape, F32),
        scratch_shapes=[
            pltpu.VMEM((8, subs, LANES), F32),
            pltpu.VMEM((weights.shape[0], 2 * LANES), F32),
        ],
        compiler_params=pltpu.CompilerParams(vmem_limit_bytes=BUDGET),
        name="gradient",
    )(total, every, slots, levels, weights)


def coefficients(grams, products, mem):
    place = iota((mem, LANES), 0)

    def pick(array, number):
        return jnp.broadcast_to(array[number : number + 1], (mem, LANES))

    cross = [from_row(grams, i, mem) for i in range(mem)]
    square = [from_row(grams, mem + i, mem) for i in range(mem)]
    pairs = [pick(cross[i], i) for i in range(mem)]
    inverse = [1.0 / pair for pair in pairs]
    by_step, by_diff = from_row(products, 0, mem), from_row(products, 1, mem)
    alphas = [None] * mem
    for i in reversed(range(mem)):
        alphas[i] = inverse[i] * pick(by_step, i)
        by_step = by_step - alphas[i] * cross[i]
        by_diff = by_diff - alphas[i] * square[i]
    scale = pairs[mem - 1] / pick(square[mem - 1], mem - 1)
    by_diff = scale * by_diff
    on_steps = jnp.zeros((mem, LANES), F32)
    on_diffs = jnp.zeros((mem, LANES), F32)
    for i in range(mem):
        extra = jnp.sum(on_steps * cross[i], axis=0, keepdims=True)
        beta = inverse[i] * (pick(by_diff, i) + extra)
        on_steps = jnp.where(place == i, alphas[i] - beta, on_steps)
        on_diffs = jnp.where(place == i, -scale * alphas[i], on_diffs)
    return scale, on_diffs, on_steps


def row_sums(tiles):
    place = iota((8, LANES), 0)
    gap = 1
    while len(tiles) > 1:
        low = (place & gap) == 0
        tiles = [
            jnp.where(low, a, b) + pltpu.roll(jnp.where(low, b, a), 8 - gap, 0)
            for a, b in zip(tiles[::2], tiles[1::2])
        ]
        gap *= 2
    return tiles[0]


def direction_kernel(grams_ref, gradient_ref, steps_hbm, diffs_hbm, out_ref,
                     steps, diffs, load_sems, held, send_sems, recv_sems):
    mem, width = steps.shape
    pairs = load(steps_hbm, diffs_hbm, steps, diffs, load_sems)
    near, far = lax.axis_size("table"), lax.axis_size("dp")
    column, row = lax.axis_index("table"), lax.axis_index("dp")
    peers = [
        {"dp": lax.rem(row + down, far), "table": lax.rem(column + across, near)}
        for down in range(far)
        for across in range(near)
        if down or across
    ]
    barrier = pltpu.get_barrier_semaphore()
    for peer in peers:
        pl.semaphore_signal(barrier, inc=1, device_id=peer, device_id_type=MESH)

    def product(number, carry):
        by_step, by_diff = carry
        for i in range(8):
            at = pl.ds(pl.multiple_of(number * 8 * LANES, LANES) + i * LANES, LANES)
            line = jnp.broadcast_to(gradient_ref[pl.ds(number * 8 + i, 1), :], (mem, LANES))
            by_step = by_step + steps[:, at] * line
            by_diff = by_diff + diffs[:, at] * line
        return by_step, by_diff

    carry = (jnp.zeros((mem, LANES), F32),) * 2
    each = width // len(pairs) // (8 * LANES)
    for part, pair in enumerate(pairs):
        for copy in pair:
            copy.wait()
        carry = lax.fori_loop(part * each, (part + 1) * each, product, carry)
    me = row * near + column
    held[me, 0:1] = grams_ref[...]
    held[me, 1:2] = to_row(carry)
    pl.semaphore_wait(barrier, len(peers))
    total = finish(send(held.at[me], held.at[me], peers, send_sems, recv_sems), held)
    scale, on_diffs, on_steps = coefficients(total[0:1], total[1:2], mem)
    scale, on_diffs, on_steps = -scale, -on_diffs, -on_steps

    def body(number, _):
        rows = []
        for i in range(8):
            at = pl.ds(pl.multiple_of(number * 8 * LANES, LANES) + i * LANES, LANES)
            rows.append(on_diffs * diffs[:, at] + on_steps * steps[:, at])
        at = pl.ds(pl.multiple_of(number * 8, 8), 8)
        out_ref[at, :] = scale * gradient_ref[at, :] + row_sums(rows)
        return 0

    lax.fori_loop(0, out_ref.shape[0] // 8, body, 0, unroll=2)


def directions(grams, gradient, steps, diffs):
    mem, width = steps.shape
    devices = lax.axis_size("dp") * lax.axis_size("table")
    return pl.pallas_call(
        direction_kernel,
        in_specs=[VMEM] * 2 + [HBM] * 2,
        out_specs=VMEM,
        out_shape=jax.ShapeDtypeStruct(gradient.shape, F32),
        scratch_shapes=[
            pltpu.VMEM((mem, width), F32),
            pltpu.VMEM((mem, width), F32),
            pltpu.SemaphoreType.DMA((2, 4)),
            pltpu.VMEM((devices, 2, LANES), F32),
            pltpu.SemaphoreType.DMA((devices - 1,)),
            pltpu.SemaphoreType.DMA((devices - 1,)),
        ],
        compiler_params=pltpu.CompilerParams(
            vmem_limit_bytes=BUDGET, collective_id=2, has_side_effects=True
        ),
        name="direction",
    )(grams, gradient, steps, diffs)


def local(feature_high, feature_low, labels, weights, history_steps, history_diffs):
    width = weights.shape[0]
    parts = lax.axis_size("dp")
    count = width * parts * lax.axis_size("table")
    bits = width.bit_length() - 1
    slots = feature_high.shape[0]
    subs = parts * feature_high.shape[1] // 1024
    table = weights.reshape(width // LANES, LANES)
    mine = jnp.concatenate([feature_high, feature_low, labels[None, :]], axis=0)
    every, partial_gram = share(mine, history_steps, history_diffs)
    margin, listed, levels = margins(every, table, count, subs, bits, slots)
    total, grams = reduced(margin, partial_gram, history_steps, history_diffs)
    gradient = gradients(total, every, listed, levels, table, subs, bits, 2 * slots)
    return directions(grams, gradient, history_steps, history_diffs).reshape(-1)


def wire(source, target, send_sem, recv_sem, peer):
    return pltpu.make_async_remote_copy(
        src_ref=source,
        dst_ref=target,
        send_sem=send_sem,
        recv_sem=recv_sem,
        device_id=peer,
        device_id_type=MESH,
    )


def merge_pairs(count):
    pairs = []
    size = 1
    while size < count:
        step = size
        while step >= 1:
            for base in range(step % size, count - step, 2 * step):
                for i in range(base, min(base + step, count - step)):
                    if i // (2 * size) == (i + step) // (2 * size):
                        pairs.append((i, i + step))
            step //= 2
        size *= 2
    return pairs


def settle(values):
    count = len(values)
    if count % 2:
        for i in range(count):
            for j in range(i + 1, count):
                low, high = values[i], values[j]
                values[i], values[j] = jnp.minimum(low, high), jnp.maximum(low, high)
        return values
    half = count // 2
    lows = [jnp.minimum(a, b) for a, b in zip(values[:half], values[half:])]
    highs = [jnp.maximum(a, b) for a, b in zip(values[:half], values[half:])]
    if half == 1:
        return lows + highs
    return settle(lows) + settle(highs)


def sort_lanes(values):
    spot = iota(values[0].shape, 0)
    bits = [(spot >> n) & 1 for n in range(3)]
    flips = -(bits[0] ^ bits[1] ^ bits[2])
    values = [value ^ flips for value in values]
    for i, j in merge_pairs(len(values)):
        low, high = values[i], values[j]
        values[i], values[j] = jnp.minimum(low, high), jnp.maximum(low, high)
    for level in range(3):
        flips = -bits[level]
        values = [value ^ flips for value in values]
        for inner in reversed(range(level + 1)):
            gap = 1 << inner
            upper = bits[inner] == 1
            values = [
                jnp.where(
                    upper,
                    jnp.maximum(value, pltpu.roll(value, gap, 0)),
                    jnp.minimum(value, pltpu.roll(value, 8 - gap, 0)),
                )
                for value in values
            ]
        values = settle(values)
    return values


def lift(tiles, offset, length):
    spot = iota(tiles[0].shape, 0)
    bit = 64
    while bit >= 8:
        keep = (bit - 1 + length + 7) // 8 + (1 if bit > 8 else 0)
        move = bit // 8
        taken = (offset & bit) != 0
        keep = min(keep, len(tiles) - move)
        tiles = [jnp.where(taken, tiles[n + move], tiles[n]) for n in range(keep)]
        bit //= 2
    while bit >= 1:
        taken = (offset & bit) != 0
        rolled = [pltpu.roll(tile, 8 - bit, 0) for tile in tiles]
        moved = [jnp.where(spot < 8 - bit, a, b) for a, b in zip(rolled, rolled[1:] + rolled[-1:])]
        tiles = [jnp.where(taken, a, b) for a, b in zip(moved, tiles)]
        bit //= 2
    return tiles[: length // 8]


def stripes(row, count):
    shape = (count, row.shape[1])
    value = jnp.broadcast_to(row.astype(F32), shape).astype(BF16)
    return iota(shape, 0).astype(BF16) == value


def one_hot(row, count):
    return jnp.where(stripes(row, count), jnp.array(1, BF16), jnp.array(0, BF16))


def choose(found, lane):
    size = found.shape[1]
    lane = jnp.broadcast_to(lane, (8, size))
    parts = [found[n : n + 8] for n in range(0, LANES, 8)]
    bit = 8
    while len(parts) > 1:
        taken = (lane & bit) != 0
        parts = [jnp.where(taken, b, a) for a, b in zip(parts[::2], parts[1::2])]
        bit *= 2
    chosen = jnp.where(iota((8, size), 0) == (lane & 7), parts[0], 0.0)
    return jnp.sum(chosen, axis=0, keepdims=True)


def whole_kernel(dims, high_hbm, low_hbm, labels_hbm, weights_hbm, steps_hbm, diffs_hbm,
                 out_ref, flag_ref,
                 steps, diffs, weights, table, features, ranked, codes, both, gradient,
                 near, far, held, parcels,
                 load_sems, weight_sem, local_sems, send_sems, recv_sems, pass_sems, take_sems,
                 near_send, near_recv, far_send, far_recv, held_send, held_recv):
    count, slots, parts_of_gram = dims
    mem, width = steps.shape
    bits = width.bit_length() - 1
    buckets, chunk = table.shape[0], table.shape[2]
    cap = codes.shape[1]
    dp, tables = lax.axis_size("dp"), lax.axis_size("table")
    me, column = lax.axis_index("dp"), lax.axis_index("table")
    ids = 2 * dp
    id_bits = ids.bit_length() - 1
    low_row = 24
    pairs_each = width // parts_of_gram

    def load_copies(part):
        at = pl.ds(pl.multiple_of(part * pairs_each, pairs_each), pairs_each)
        return [
            pltpu.make_async_copy(source.at[:, at], target.at[:, at], load_sems.at[kind, part])
            for kind, (source, target) in enumerate(((steps_hbm, steps), (diffs_hbm, diffs)))
        ]

    half = column % 2
    partner = {"table": column + 1 - 2 * half}
    lanes = pl.ds(pl.multiple_of(half * LANES, LANES), LANES)
    mine = features.at[half, me]
    features[half, me, slots + 1 : low_row] = jnp.zeros((low_row - slots - 1, LANES), I32)
    locals_ = [
        pltpu.make_async_copy(high_hbm.at[:, lanes], mine.at[pl.ds(0, slots)], local_sems.at[0]),
        pltpu.make_async_copy(low_hbm.at[:, lanes], mine.at[pl.ds(low_row, slots)], local_sems.at[1]),
        pltpu.make_async_copy(labels_hbm.at[:, lanes], mine.at[pl.ds(slots, 1)], local_sems.at[2]),
    ]
    for copy in locals_:
        copy.start()
    barrier = pltpu.get_barrier_semaphore()
    friends = others("dp") + others("table")
    for peer in friends:
        pl.semaphore_signal(barrier, inc=1, device_id=peer, device_id_type=MESH)

    def start_load(part, _):
        for copy in load_copies(part):
            copy.start()
        return 0

    lax.fori_loop(0, parts_of_gram, start_load, 0)
    weight_copy = pltpu.make_async_copy(weights_hbm, weights, weight_sem)
    weight_copy.start()

    def gram(part, carry):
        for copy in load_copies(part):
            copy.wait()

        def body(number, carry):
            at = pl.ds(pl.multiple_of(part * pairs_each + number * LANES, LANES), LANES)
            step, diff = steps[:, at], diffs[:, at]
            new = []
            for i in range(mem):
                row = jnp.broadcast_to(diffs[i : i + 1, at], diff.shape)
                new.append(carry[2 * i] + step * row)
                new.append(carry[2 * i + 1] + diff * row)
            return tuple(new)

        return lax.fori_loop(0, pairs_each // LANES, body, carry, unroll=4)

    ahead = ((dp - 1 - me) * parts_of_gram) // (dp + 2)
    carry = (jnp.zeros((mem, LANES), F32),) * (2 * mem)
    carry = lax.fori_loop(0, ahead, gram, carry)

    for copy in locals_:
        copy.wait()
    pl.semaphore_wait(barrier, len(friends))

    def across(step):
        return wire(mine, mine, send_sems.at[step - 1], recv_sems.at[step - 1], {"dp": me ^ step})

    def over(step):
        source = features.at[half, me ^ step]
        return wire(source, source, pass_sems.at[step], take_sems.at[step], partner)

    def start_across(step, _):
        across(dp - step).start()
        return 0

    lax.fori_loop(1, dp, start_across, 0)
    over(0).start()
    weight_copy.wait()
    for b in range(buckets):
        tops, rests = split(weights[b * chunk : (b + 1) * chunk].T)
        table[b, :LANES] = tops
        table[b, LANES:] = rests
    carry = lax.fori_loop(ahead, parts_of_gram, gram, carry)
    gram_here = gram_row(carry, mem)

    device = me * tables + column
    spot = iota((8, LANES), 0)
    invalid = 1 << 30
    depth = ranked.shape[0] // 8
    mask, limit = (count << id_bits) - 1, width << id_bits
    rests_of = slots % 8
    assert slots % 8 in (0, 4)
    tiles = [(8 * n + spot, True) for n in range(slots // 8)]
    if rests_of:
        tiles.append((slots - 4 + (spot & 3), False))
    starts = [
        [((slot * slot_mult[k] + shifts[k]) - device * width) << id_bits for k in range(HASHES)]
        for slot, _ in tiles
    ]

    def consume(source, stack):
        stack = list(stack)
        for number, (_, full) in enumerate(tiles):
            if full:
                group = [
                    (
                        features[h, source, 8 * number : 8 * number + 8],
                        features[h, source, low_row + 8 * number : low_row + 8 * number + 8],
                        2 * source + h,
                    )
                    for h in range(2)
                ]
            else:
                at = slots - 4
                pair = [
                    jnp.concatenate([features[h, source, at + base : at + base + 4] for h in range(2)], axis=0)
                    for base in (0, low_row)
                ]
                group = [(*pair, 2 * source + (spot >> 2))]
            for high, low, name in group:
                for k in range(HASHES):
                    key = (
                        high * (high_mult[k] << id_bits)
                        + low * (low_mult[k] << id_bits)
                        + (starts[number][k] + name)
                    ) & mask
                    owned = key < limit
                    for level in reversed(range(1, depth)):
                        stack[level] = jnp.where(owned, stack[level - 1], stack[level])
                    stack[0] = jnp.where(owned, key, stack[0])
        return tuple(stack)

    def receive(step, stack):
        across(step).wait_recv()
        over(step).start()
        over(step - 1).wait_recv()
        return consume(me ^ (step - 1), stack)

    stack = (jnp.full((8, LANES), invalid, I32),) * depth
    stack = lax.fori_loop(1, dp, receive, stack)
    over(dp - 1).wait_recv()
    stack = consume(me ^ (dp - 1), stack)

    spilled = jnp.where(stack[-1] < invalid, 1, 0)
    ends = []
    for b in range(buckets):
        below = jnp.zeros((8, LANES), I32)
        for value in stack:
            below = below + jnp.where(value < (((b + 1) * chunk * LANES) << id_bits), 1, 0)
        ends.append(jnp.broadcast_to(jnp.sum(below, axis=0, keepdims=True), (8, LANES)))
    begins = [jnp.zeros((8, LANES), I32)] + ends[:-1]
    for begin, end in zip(begins, ends):
        spilled = jnp.where(end - begin > cap, 1, spilled)
    spilled = jnp.where(begins[-1] > LANES - 1, 1, spilled)
    values = sort_lanes(list(stack))
    for level in range(depth):
        ranked[pl.ds(level, 8, stride=depth), :] = values[level]
    ordered = [ranked[8 * n : 8 * n + 8] for n in range(depth)]
    for b in range(buckets):
        lifted = lift(ordered, begins[b], cap) if b else ordered[: cap // 8]
        for n, tile in enumerate(lifted):
            codes[b, 8 * n : 8 * n + 8] = tile

    def fetch(b, number):
        rows = [codes[b, pl.ds(number * WIDE + n, 1), :] for n in range(WIDE)]
        code = jnp.concatenate(rows, axis=1)
        return (code >> (7 + id_bits)) - b * chunk, (code >> id_bits) & (LANES - 1), code & (ids - 1)

    def gather(number, total):
        for b in range(buckets):
            row, lane, name = fetch(b, number)
            found = jnp.dot(table[b], one_hot(row, chunk), preferred_element_type=F32)
            value = choose(found[:LANES] + found[LANES:], lane)
            for n in range(WIDE):
                at = slice(n * LANES, (n + 1) * LANES)
                total = total + jnp.where(iota((ids, LANES), 0) == name[:, at], value[:, at], 0.0)
        return total

    margin = lax.fori_loop(0, cap // WIDE, gather, jnp.zeros((ids, LANES), F32), unroll=UNROLL)
    near[column] = margin
    copies = send(near.at[column], near.at[column], others("table"), near_send, near_recv)
    both[...] = jnp.zeros_like(both)
    margin = finish(copies, near)
    far[me] = margin
    copies = send(far.at[me], far.at[me], others("dp"), far_send, far_recv)
    labels = jnp.concatenate(
        [features[n % 2, n // 2, slots : slots + 1] for n in range(ids)], axis=0
    ).astype(F32)

    def retire(step, _):
        across(step).wait_send()
        over(step).wait_send()
        return 0

    over(0).wait_send()
    lax.fori_loop(1, dp, retire, 0)
    margin = finish(copies, far)
    residual = 1.0 / (1.0 + jnp.exp(-margin)) - labels

    def scatter(number, _):
        for b in range(buckets):
            row, lane, name = fetch(b, number)
            spread = jnp.concatenate([residual] * WIDE, axis=1)
            value = jnp.sum(jnp.where(iota(spread.shape, 0) == name, spread, 0.0), axis=0, keepdims=True)
            top = value.astype(BF16).astype(F32)
            here = stripes(lane, LANES)
            terms = [
                jnp.where(here, jnp.broadcast_to(piece, here.shape).astype(BF16), jnp.array(0, BF16))
                for piece in (top, value - top)
            ]
            both[b] += lax.dot_general(
                one_hot(row, chunk), jnp.concatenate(terms, axis=0), (((1,), (1,)), ((), ())),
                preferred_element_type=F32,
            )
        return 0

    lax.fori_loop(0, cap // WIDE, scatter, 0, unroll=UNROLL)
    for b in range(buckets):
        at = slice(b * chunk, (b + 1) * chunk)
        gradient[at] = both[b, :, :LANES] + both[b, :, LANES:] + l2_weight * weights[at]

    def product(number, carry):
        by_step, by_diff = carry
        for i in range(8):
            at = pl.ds(pl.multiple_of(number * 8 * LANES, LANES) + i * LANES, LANES)
            line = jnp.broadcast_to(gradient[pl.ds(number * 8 + i, 1), :], (mem, LANES))
            by_step = by_step + steps[:, at] * line
            by_diff = by_diff + diffs[:, at] * line
        return by_step, by_diff

    carry = (jnp.zeros((mem, LANES), F32),) * 2
    carry = lax.fori_loop(0, width // (8 * LANES), product, carry)
    held[device, 0:1] = gram_here
    held[device, 1:2] = to_row(carry)
    held[device, 2:3] = jnp.max(spilled, axis=0, keepdims=True).astype(F32)
    peers = [
        {"dp": lax.rem(me + down, dp), "table": lax.rem(column + sideways, tables)}
        for down in range(dp)
        for sideways in range(tables)
        if down or sideways
    ]
    total = finish(send(held.at[device], held.at[device], peers, held_send, held_recv), held)
    scale, on_diffs, on_steps = coefficients(total[0:1], total[1:2], mem)
    scale, on_diffs, on_steps = -scale, -on_diffs, -on_steps

    def body(number, _):
        rows = []
        for i in range(8):
            at = pl.ds(pl.multiple_of(number * 8 * LANES, LANES) + i * LANES, LANES)
            rows.append(on_diffs * diffs[:, at] + on_steps * steps[:, at])
        at = pl.ds(pl.multiple_of(number * 8, 8), 8)
        out_ref[at, :] = scale * gradient[at, :] + row_sums(rows)
        return 0

    lax.fori_loop(0, out_ref.shape[0] // 8, body, 0, unroll=2)
    flag_ref[0] = jnp.max(jnp.where(total[2:3] > 0.0, 1, 0))


def whole(high, low, labels, weights, steps, diffs):
    mem, width = steps.shape
    slots = high.shape[0]
    dp, tables = lax.axis_size("dp"), lax.axis_size("table")
    devices = dp * tables
    rows = width // LANES
    chunk = min(2 * LANES, rows)
    buckets = rows // chunk
    cap = CAP if buckets > 1 else 3 * CAP
    DMA = pltpu.SemaphoreType.DMA
    parts = 8
    return pl.pallas_call(
        functools.partial(whole_kernel, (width * devices, slots, parts)),
        in_specs=[HBM] * 6,
        out_specs=[VMEM, SMEM],
        out_shape=[jax.ShapeDtypeStruct((rows, LANES), F32), jax.ShapeDtypeStruct((1,), I32)],
        scratch_shapes=[
            pltpu.VMEM((mem, width), F32),
            pltpu.VMEM((mem, width), F32),
            pltpu.VMEM((rows, LANES), F32),
            pltpu.VMEM((buckets, 2 * LANES, chunk), BF16),
            pltpu.VMEM((2, dp, 24 + slots, LANES), I32),
            pltpu.VMEM((8 * DEPTH, LANES), I32),
            pltpu.VMEM((buckets, cap, LANES), I32),
            pltpu.VMEM((buckets, chunk, 2 * LANES), F32),
            pltpu.VMEM((rows, LANES), F32),
            pltpu.VMEM((tables, 2 * dp, LANES), F32),
            pltpu.VMEM((dp, 2 * dp, LANES), F32),
            pltpu.VMEM((devices, 3, LANES), F32),
            pltpu.VMEM((8, LANES), F32),
            DMA((2, parts)),
            DMA,
            DMA((3,)),
            DMA((dp - 1,)),
            DMA((dp - 1,)),
            DMA((dp,)),
            DMA((dp,)),
            DMA((tables - 1,)),
            DMA((tables - 1,)),
            DMA((dp - 1,)),
            DMA((dp - 1,)),
            DMA((devices - 1,)),
            DMA((devices - 1,)),
        ],
        compiler_params=pltpu.CompilerParams(
            vmem_limit_bytes=BUDGET, collective_id=3, has_side_effects=True
        ),
        name="whole",
    )(high, low, labels, weights, steps, diffs)


def quick(feature_high, feature_low, labels, weights, history_steps, history_diffs):
    width = weights.shape[0]
    direction, flag = whole(
        feature_high, feature_low, labels[None, :], weights.reshape(width // LANES, LANES),
        history_steps, history_diffs,
    )
    return lax.cond(
        flag[0] > 0,
        lambda: local(feature_high, feature_low, labels, weights, history_steps, history_diffs),
        lambda: direction.reshape(-1),
    )


def solution(mesh):
    placed = (
        P(None, "dp"),
        P(None, "dp"),
        P("dp"),
        P(("dp", "table")),
        P(None, ("dp", "table")),
        P(None, ("dp", "table")),
    )
    return jax.shard_map(
        quick, mesh=mesh, in_specs=placed, out_specs=P(("dp", "table")), check_vma=False
    )
```

```python
import functools

import jax
import jax.numpy as jnp
from jax import lax
from jax.experimental import pallas as pl
from jax.experimental.pallas import tpu as pltpu
from jax.sharding import PartitionSpec as P

HASHES = 4
LANES = 128
BLOCK = 16
GROUP = 4
DEPTH = 24
CAP = 40
WIDE = 8
UNROLL = 5

high_mult = (40503, 96469, 255361, 362443)
low_mult = (2053, 6151, 12289, 98317)
slot_mult = (1543, 3079, 769, 3457)
shifts = (0, 1048573, 2097143, 3145727)
l2_weight = 1.0
BUDGET = 50 << 20
F32, BF16, I32 = jnp.float32, jnp.bfloat16, jnp.int32
MESH = pl.DeviceIdType.MESH
VMEM = pl.BlockSpec(memory_space=pltpu.VMEM)
HBM = pl.BlockSpec(memory_space=pltpu.HBM)
SMEM = pl.BlockSpec(memory_space=pltpu.SMEM)


def iota(shape, axis):
    return lax.broadcasted_iota(I32, shape, axis)


def split(value):
    top = value.astype(BF16)
    return top, (value - top.astype(F32)).astype(BF16)


def hot(index, count):
    shape = (count, index.shape[1])
    return jnp.where(iota(shape, 0) == index, 1.0, 0.0).astype(BF16)


def greet(peers):
    barrier = pltpu.get_barrier_semaphore()
    for peer in peers:
        pl.semaphore_signal(barrier, inc=1, device_id=peer, device_id_type=MESH)
    pl.semaphore_wait(barrier, len(peers))


def others(axis):
    size, me = lax.axis_size(axis), lax.axis_index(axis)
    return [{axis: lax.rem(me + step, size)} for step in range(1, size)]


def send(source, target, peers, send_sems, recv_sems):
    copies = []
    for number, peer in enumerate(peers):
        copy = pltpu.make_async_remote_copy(
            src_ref=source,
            dst_ref=target,
            send_sem=send_sems.at[number],
            recv_sem=recv_sems.at[number],
            device_id=peer,
            device_id_type=MESH,
        )
        copy.start()
        copies.append(copy)
    return copies


def stage(axis, held, value, sems):
    me = lax.axis_index(axis)
    held[me] = value
    return send(held.at[me], held.at[me], others(axis), *sems)


def finish(copies, held):
    for copy in copies:
        copy.wait()
    total = held[0]
    for number in range(1, held.shape[0]):
        total = total + held[number]
    return total


def sum_scratch(shape):
    near, far = lax.axis_size("table"), lax.axis_size("dp")
    return [
        pltpu.VMEM((near, *shape), F32),
        pltpu.VMEM((far, *shape), F32),
        pltpu.SemaphoreType.DMA((near - 1,)),
        pltpu.SemaphoreType.DMA((near - 1,)),
        pltpu.SemaphoreType.DMA((far - 1,)),
        pltpu.SemaphoreType.DMA((far - 1,)),
    ]


def load(steps_hbm, diffs_hbm, steps, diffs, sems, first=0):
    parts, width = sems.shape[1], steps.shape[1]
    pairs = []
    for part in range(parts):
        size = width // parts
        pair = []
        for kind, (source, target) in enumerate(((steps_hbm, steps), (diffs_hbm, diffs))):
            copy = pltpu.make_async_copy(
                source.at[:, pl.ds(first + part * size, size)],
                target.at[:, pl.ds(part * size, size)],
                sems.at[kind, part],
            )
            copy.start()
            pair.append(copy)
        pairs.append(pair)
    return pairs


def gram_part(steps, diffs, pairs, part, carry):
    mem = steps.shape[0]
    each = steps.shape[1] // len(pairs) // LANES
    for copy in pairs[part]:
        copy.wait()

    def body(number, carry):
        at = pl.ds(pl.multiple_of(number * LANES, LANES), LANES)
        step, diff = steps[:, at], diffs[:, at]
        new = []
        for i in range(mem):
            row = jnp.broadcast_to(diffs[i : i + 1, at], diff.shape)
            new.append(carry[2 * i] + step * row)
            new.append(carry[2 * i + 1] + diff * row)
        return tuple(new)

    return lax.fori_loop(part * each, (part + 1) * each, body, carry, unroll=4)


def to_row(columns):
    mem = columns[0].shape[0]
    total = jnp.zeros((mem, LANES), F32)
    spot = iota((mem, LANES), 1) - iota((mem, LANES), 0)
    for number, column in enumerate(columns):
        total = jnp.where(spot == number * mem, jnp.sum(column, axis=1, keepdims=True), total)
    return jnp.sum(total, axis=0, keepdims=True)


def from_row(row, number, mem):
    spot = iota((mem, LANES), 1) - iota((mem, LANES), 0)
    wide = jnp.broadcast_to(row, (mem, LANES))
    column = jnp.sum(jnp.where(spot == number * mem, wide, 0.0), axis=1, keepdims=True)
    return jnp.broadcast_to(column, (mem, LANES))


def gram_row(carry, mem):
    return to_row([carry[2 * i] for i in range(mem)] + [carry[2 * i + 1] for i in range(mem)])


def share_kernel(mine_ref, steps_hbm, diffs_hbm, every_ref, gram_ref,
                 steps, diffs, send_sems, recv_sems, sems):
    mem = steps.shape[0]
    pairs = load(steps_hbm, diffs_hbm, steps, diffs, sems)
    me = lax.axis_index("dp")
    every_ref[me] = mine_ref[...]
    peers = others("dp")
    greet(peers)
    sent = send(mine_ref, every_ref.at[me], peers, send_sems, recv_sems)
    carry = (jnp.zeros((mem, LANES), F32),) * (2 * mem)
    for part in range(len(pairs)):
        carry = gram_part(steps, diffs, pairs, part, carry)
    gram_ref[...] = gram_row(carry, mem)
    for copy in sent:
        copy.wait()


def share(mine, steps, diffs):
    mem, width = steps.shape
    dp = lax.axis_size("dp")
    return pl.pallas_call(
        share_kernel,
        in_specs=[VMEM] + [HBM] * 2,
        out_specs=[VMEM] * 2,
        out_shape=[
            jax.ShapeDtypeStruct((dp, *mine.shape), I32),
            jax.ShapeDtypeStruct((1, LANES), F32),
        ],
        scratch_shapes=[
            pltpu.VMEM((mem, 3 * width // 4), F32),
            pltpu.VMEM((mem, 3 * width // 4), F32),
            pltpu.SemaphoreType.DMA((dp - 1,)),
            pltpu.SemaphoreType.DMA((dp - 1,)),
            pltpu.SemaphoreType.DMA((2, 3)),
        ],
        compiler_params=pltpu.CompilerParams(
            vmem_limit_bytes=BUDGET, collective_id=0, has_side_effects=True
        ),
        name="share",
    )(mine, steps, diffs)


def reduce_kernel(margin_ref, gram_ref, steps_hbm, diffs_hbm, out_ref, grams_ref,
                  steps, diffs, load_sems, near, far, *sems):
    mem, size = steps.shape
    pairs = load(steps_hbm, diffs_hbm, steps, diffs, load_sems, steps_hbm.shape[1] - size)
    greet(others("table") + others("dp"))
    carry = (jnp.zeros((mem, LANES), F32),) * (2 * mem)
    copies = stage("table", near, margin_ref[...], sems[:2])
    copies = stage("dp", far, finish(copies, near), sems[2:])
    carry = gram_part(steps, diffs, pairs, 0, carry)
    grams_ref[...] = gram_ref[...] + gram_row(carry, mem)
    out_ref[...] = finish(copies, far)


def reduced(margin, grams, steps, diffs):
    mem, width = steps.shape
    return pl.pallas_call(
        reduce_kernel,
        in_specs=[VMEM] * 2 + [HBM] * 2,
        out_specs=[VMEM] * 2,
        out_shape=[
            jax.ShapeDtypeStruct(margin.shape, F32),
            jax.ShapeDtypeStruct((1, LANES), F32),
        ],
        scratch_shapes=[
            pltpu.VMEM((mem, width // 4), F32),
            pltpu.VMEM((mem, width // 4), F32),
            pltpu.SemaphoreType.DMA((2, 1)),
        ]
        + sum_scratch(margin.shape),
        compiler_params=pltpu.CompilerParams(
            vmem_limit_bytes=BUDGET, collective_id=1, has_side_effects=True
        ),
        name="reduce",
    )(margin, grams, steps, diffs)


def margin_kernel(count, subs, bits, slot_total, every_ref, weights_ref, margin_ref, slots_ref, levels_ref, table, features):
    device = lax.axis_index("dp") * lax.axis_size("table") + lax.axis_index("table")
    width = 1 << bits
    for number in range(2 * slot_total):
        features[number] = every_ref[:, number, :]
    tops, rests = split(weights_ref[...].T)
    table[: LANES] = tops
    table[LANES :] = rests

    def one_pass(number, _):
        base = number * BLOCK

        def body(slot, carry):
            seen, outs = carry[0], list(carry[1:])
            for sub in range(subs):
                group, half = sub // 2, sub % 2
                at = (pl.ds(group * 8, 8), pl.ds(half * LANES, LANES))
                high, low = features[(slot, *at)], features[(slot + slot_total, *at)]
                for k in range(HASHES):
                    index = (high * high_mult[k] + low * low_mult[k] + (slot * slot_mult[k] + shifts[k])) & (count - 1)
                    owned = (index >> bits) == device
                    place = jnp.where(owned, seen, -1)
                    code = (index & (width - 1)) | (sub << bits)
                    for level in range(BLOCK):
                        outs[level] = jnp.where(place == level, code, outs[level])
                    seen = seen + owned.astype(I32)
            return (seen, *outs)

        empty = jnp.full((8, LANES), -1, I32)
        final = lax.fori_loop(0, slot_total, body, (jnp.zeros((8, LANES), I32) - base,) + (empty,) * BLOCK)
        for level in range(BLOCK):
            slots_ref[:, base + level, :] = final[1 + level]
        return final[0] + base

    seen = one_pass(0, None)
    most = jnp.max(seen)
    lax.fori_loop(1, (most + BLOCK - 1) // BLOCK, lambda n, c: (one_pass(n, None), c)[1], 0)
    for row in range(8):
        levels_ref[row] = (jnp.max(seen[row : row + 1]) + GROUP - 1) // GROUP

    def rows(row, _):
        def body(number, total):
            codes = slots_ref[row, pl.ds(number * GROUP, GROUP), :]
            code = jnp.concatenate([codes[i : i + 1] for i in range(GROUP)], axis=1)
            local = code & (width - 1)
            found = jnp.dot(table[...], hot(local >> 7, width // LANES), preferred_element_type=F32)
            found = found[:LANES] + found[LANES:]
            chosen = jnp.where(iota(found.shape, 0) == (local & (LANES - 1)), found, 0.0)
            value = jnp.sum(chosen, axis=0, keepdims=True)
            sub = code >> bits
            for i in range(GROUP):
                at = slice(i * LANES, (i + 1) * LANES)
                total = total + jnp.where(iota((subs, LANES), 0) == sub[:, at], value[:, at], 0.0)
            return total

        total = lax.fori_loop(0, levels_ref[row], body, jnp.zeros((subs, LANES), F32))
        for sub in range(subs):
            here = iota((8, LANES), 0) == row
            margin_ref[sub] = jnp.where(here, total[sub : sub + 1], margin_ref[sub])
        return 0

    margin_ref[...] = jnp.zeros_like(margin_ref)
    lax.fori_loop(0, 8, rows, 0)


def margins(every, weights, count, subs, bits, slots):
    levels = -(-subs * HASHES * slots // BLOCK) * BLOCK
    return pl.pallas_call(
        functools.partial(margin_kernel, count, subs, bits, slots),
        in_specs=[VMEM] * 2,
        out_specs=[VMEM, VMEM, SMEM],
        out_shape=[
            jax.ShapeDtypeStruct((subs, 8, LANES), F32),
            jax.ShapeDtypeStruct((8, levels, LANES), I32),
            jax.ShapeDtypeStruct((8,), I32),
        ],
        scratch_shapes=[
            pltpu.VMEM((2 * LANES, (1 << bits) // LANES), BF16),
            pltpu.VMEM((2 * slots, every.shape[0], every.shape[2]), I32),
        ],
        compiler_params=pltpu.CompilerParams(vmem_limit_bytes=BUDGET),
        name="margins",
    )(every, weights)


def gradient_kernel(subs, bits, label_row, total_ref, every_ref, slots_ref, levels_ref, weights_ref,
                    gradient_ref, residual, both):
    width = 1 << bits
    for sub in range(subs):
        label = every_ref[sub // 2 * 8 : sub // 2 * 8 + 8, label_row, sub % 2 * LANES : sub % 2 * LANES + LANES]
        residual[:, sub, :] = 1.0 / (1.0 + jnp.exp(-total_ref[sub])) - label.astype(F32)
    both[...] = jnp.zeros_like(both)

    def rows(row, _):
        value = residual[row]

        def body(number, _):
            codes = slots_ref[row, pl.ds(number * GROUP, GROUP), :]
            code = jnp.concatenate([codes[i : i + 1] for i in range(GROUP)], axis=1)
            local = code & (width - 1)
            sub = code >> bits
            wide = jnp.concatenate([value] * GROUP, axis=1)
            mine = jnp.sum(jnp.where(iota(wide.shape, 0) == sub, wide, 0.0), axis=0, keepdims=True)
            column = iota((LANES, GROUP * LANES), 0) == (local & (LANES - 1))
            top, rest = split(jnp.where(column, mine, 0.0))
            terms = jnp.concatenate([top, rest], axis=0)
            both[...] += lax.dot_general(
                hot(local >> 7, width // LANES), terms, (((1,), (1,)), ((), ())), preferred_element_type=F32
            )
            return 0

        lax.fori_loop(0, levels_ref[row], body, 0)
        return 0

    lax.fori_loop(0, 8, rows, 0)
    gradient_ref[...] = both[:, :LANES] + both[:, LANES:] + l2_weight * weights_ref[...]


def gradients(total, every, slots, levels, weights, subs, bits, label_row):
    return pl.pallas_call(
        functools.partial(gradient_kernel, subs, bits, label_row),
        in_specs=[VMEM, VMEM, VMEM, SMEM, VMEM],
        out_specs=VMEM,
        out_shape=jax.ShapeDtypeStruct(weights.shape, F32),
        scratch_shapes=[
            pltpu.VMEM((8, subs, LANES), F32),
            pltpu.VMEM((weights.shape[0], 2 * LANES), F32),
        ],
        compiler_params=pltpu.CompilerParams(vmem_limit_bytes=BUDGET),
        name="gradient",
    )(total, every, slots, levels, weights)


def coefficients(grams, products, mem):
    place = iota((mem, LANES), 0)

    def pick(array, number):
        return jnp.broadcast_to(array[number : number + 1], (mem, LANES))

    cross = [from_row(grams, i, mem) for i in range(mem)]
    square = [from_row(grams, mem + i, mem) for i in range(mem)]
    pairs = [pick(cross[i], i) for i in range(mem)]
    inverse = [1.0 / pair for pair in pairs]
    by_step, by_diff = from_row(products, 0, mem), from_row(products, 1, mem)
    alphas = [None] * mem
    for i in reversed(range(mem)):
        alphas[i] = inverse[i] * pick(by_step, i)
        by_step = by_step - alphas[i] * cross[i]
        by_diff = by_diff - alphas[i] * square[i]
    scale = pairs[mem - 1] / pick(square[mem - 1], mem - 1)
    by_diff = scale * by_diff
    on_steps = jnp.zeros((mem, LANES), F32)
    on_diffs = jnp.zeros((mem, LANES), F32)
    for i in range(mem):
        extra = jnp.sum(on_steps * cross[i], axis=0, keepdims=True)
        beta = inverse[i] * (pick(by_diff, i) + extra)
        on_steps = jnp.where(place == i, alphas[i] - beta, on_steps)
        on_diffs = jnp.where(place == i, -scale * alphas[i], on_diffs)
    return scale, on_diffs, on_steps


def row_sums(tiles):
    place = iota((8, LANES), 0)
    gap = 1
    while len(tiles) > 1:
        low = (place & gap) == 0
        tiles = [
            jnp.where(low, a, b) + pltpu.roll(jnp.where(low, b, a), 8 - gap, 0)
            for a, b in zip(tiles[::2], tiles[1::2])
        ]
        gap *= 2
    return tiles[0]


def direction_kernel(grams_ref, gradient_ref, steps_hbm, diffs_hbm, out_ref,
                     steps, diffs, load_sems, held, send_sems, recv_sems):
    mem, width = steps.shape
    pairs = load(steps_hbm, diffs_hbm, steps, diffs, load_sems)
    near, far = lax.axis_size("table"), lax.axis_size("dp")
    column, row = lax.axis_index("table"), lax.axis_index("dp")
    peers = [
        {"dp": lax.rem(row + down, far), "table": lax.rem(column + across, near)}
        for down in range(far)
        for across in range(near)
        if down or across
    ]
    barrier = pltpu.get_barrier_semaphore()
    for peer in peers:
        pl.semaphore_signal(barrier, inc=1, device_id=peer, device_id_type=MESH)

    def product(number, carry):
        by_step, by_diff = carry
        for i in range(8):
            at = pl.ds(pl.multiple_of(number * 8 * LANES, LANES) + i * LANES, LANES)
            line = jnp.broadcast_to(gradient_ref[pl.ds(number * 8 + i, 1), :], (mem, LANES))
            by_step = by_step + steps[:, at] * line
            by_diff = by_diff + diffs[:, at] * line
        return by_step, by_diff

    carry = (jnp.zeros((mem, LANES), F32),) * 2
    each = width // len(pairs) // (8 * LANES)
    for part, pair in enumerate(pairs):
        for copy in pair:
            copy.wait()
        carry = lax.fori_loop(part * each, (part + 1) * each, product, carry)
    me = row * near + column
    held[me, 0:1] = grams_ref[...]
    held[me, 1:2] = to_row(carry)
    pl.semaphore_wait(barrier, len(peers))
    total = finish(send(held.at[me], held.at[me], peers, send_sems, recv_sems), held)
    scale, on_diffs, on_steps = coefficients(total[0:1], total[1:2], mem)
    scale, on_diffs, on_steps = -scale, -on_diffs, -on_steps

    def body(number, _):
        rows = []
        for i in range(8):
            at = pl.ds(pl.multiple_of(number * 8 * LANES, LANES) + i * LANES, LANES)
            rows.append(on_diffs * diffs[:, at] + on_steps * steps[:, at])
        at = pl.ds(pl.multiple_of(number * 8, 8), 8)
        out_ref[at, :] = scale * gradient_ref[at, :] + row_sums(rows)
        return 0

    lax.fori_loop(0, out_ref.shape[0] // 8, body, 0, unroll=2)


def directions(grams, gradient, steps, diffs):
    mem, width = steps.shape
    devices = lax.axis_size("dp") * lax.axis_size("table")
    return pl.pallas_call(
        direction_kernel,
        in_specs=[VMEM] * 2 + [HBM] * 2,
        out_specs=VMEM,
        out_shape=jax.ShapeDtypeStruct(gradient.shape, F32),
        scratch_shapes=[
            pltpu.VMEM((mem, width), F32),
            pltpu.VMEM((mem, width), F32),
            pltpu.SemaphoreType.DMA((2, 4)),
            pltpu.VMEM((devices, 2, LANES), F32),
            pltpu.SemaphoreType.DMA((devices - 1,)),
            pltpu.SemaphoreType.DMA((devices - 1,)),
        ],
        compiler_params=pltpu.CompilerParams(
            vmem_limit_bytes=BUDGET, collective_id=2, has_side_effects=True
        ),
        name="direction",
    )(grams, gradient, steps, diffs)


def local(feature_high, feature_low, labels, weights, history_steps, history_diffs):
    width = weights.shape[0]
    parts = lax.axis_size("dp")
    count = width * parts * lax.axis_size("table")
    bits = width.bit_length() - 1
    slots = feature_high.shape[0]
    subs = parts * feature_high.shape[1] // 1024
    table = weights.reshape(width // LANES, LANES)
    mine = jnp.concatenate([feature_high, feature_low, labels[None, :]], axis=0)
    every, partial_gram = share(mine, history_steps, history_diffs)
    margin, listed, levels = margins(every, table, count, subs, bits, slots)
    total, grams = reduced(margin, partial_gram, history_steps, history_diffs)
    gradient = gradients(total, every, listed, levels, table, subs, bits, 2 * slots)
    return directions(grams, gradient, history_steps, history_diffs).reshape(-1)


def wire(source, target, send_sem, recv_sem, peer):
    return pltpu.make_async_remote_copy(
        src_ref=source,
        dst_ref=target,
        send_sem=send_sem,
        recv_sem=recv_sem,
        device_id=peer,
        device_id_type=MESH,
    )


def merge_pairs(count):
    pairs = []
    size = 1
    while size < count:
        step = size
        while step >= 1:
            for base in range(step % size, count - step, 2 * step):
                for i in range(base, min(base + step, count - step)):
                    if i // (2 * size) == (i + step) // (2 * size):
                        pairs.append((i, i + step))
            step //= 2
        size *= 2
    return pairs


def settle(values):
    count = len(values)
    if count % 2:
        for i in range(count):
            for j in range(i + 1, count):
                low, high = values[i], values[j]
                values[i], values[j] = jnp.minimum(low, high), jnp.maximum(low, high)
        return values
    half = count // 2
    lows = [jnp.minimum(a, b) for a, b in zip(values[:half], values[half:])]
    highs = [jnp.maximum(a, b) for a, b in zip(values[:half], values[half:])]
    if half == 1:
        return lows + highs
    return settle(lows) + settle(highs)


def sort_lanes(values):
    spot = iota(values[0].shape, 0)
    bits = [(spot >> n) & 1 for n in range(3)]
    flips = -(bits[0] ^ bits[1] ^ bits[2])
    values = [value ^ flips for value in values]
    for i, j in merge_pairs(len(values)):
        low, high = values[i], values[j]
        values[i], values[j] = jnp.minimum(low, high), jnp.maximum(low, high)
    for level in range(3):
        flips = -bits[level]
        values = [value ^ flips for value in values]
        for inner in reversed(range(level + 1)):
            gap = 1 << inner
            upper = bits[inner] == 1
            values = [
                jnp.where(
                    upper,
                    jnp.maximum(value, pltpu.roll(value, gap, 0)),
                    jnp.minimum(value, pltpu.roll(value, 8 - gap, 0)),
                )
                for value in values
            ]
        values = settle(values)
    return values


def lift(tiles, offset, length):
    spot = iota(tiles[0].shape, 0)
    bit = 64
    while bit >= 8:
        keep = (bit - 1 + length + 7) // 8 + (1 if bit > 8 else 0)
        move = bit // 8
        taken = (offset & bit) != 0
        keep = min(keep, len(tiles) - move)
        tiles = [jnp.where(taken, tiles[n + move], tiles[n]) for n in range(keep)]
        bit //= 2
    while bit >= 1:
        taken = (offset & bit) != 0
        rolled = [pltpu.roll(tile, 8 - bit, 0) for tile in tiles]
        moved = [jnp.where(spot < 8 - bit, a, b) for a, b in zip(rolled, rolled[1:] + rolled[-1:])]
        tiles = [jnp.where(taken, a, b) for a, b in zip(moved, tiles)]
        bit //= 2
    return tiles[: length // 8]


def stripes(row, count):
    shape = (count, row.shape[1])
    value = jnp.broadcast_to(row.astype(F32), shape).astype(BF16)
    return iota(shape, 0).astype(BF16) == value


def one_hot(row, count):
    return jnp.where(stripes(row, count), jnp.array(1, BF16), jnp.array(0, BF16))


def choose(found, lane):
    size = found.shape[1]
    lane = jnp.broadcast_to(lane, (8, size))
    parts = [found[n : n + 8] for n in range(0, LANES, 8)]
    bit = 8
    while len(parts) > 1:
        taken = (lane & bit) != 0
        parts = [jnp.where(taken, b, a) for a, b in zip(parts[::2], parts[1::2])]
        bit *= 2
    chosen = jnp.where(iota((8, size), 0) == (lane & 7), parts[0], 0.0)
    return jnp.sum(chosen, axis=0, keepdims=True)


def whole_kernel(dims, high_hbm, low_hbm, labels_hbm, weights_hbm, steps_hbm, diffs_hbm,
                 out_ref, flag_ref,
                 steps, diffs, weights, table, features, ranked, codes, both, gradient,
                 near, far, held, parcels,
                 load_sems, weight_sem, local_sems, send_sems, recv_sems, pass_sems, take_sems,
                 near_send, near_recv, far_send, far_recv, held_send, held_recv):
    count, slots, parts_of_gram = dims
    mem, width = steps.shape
    bits = width.bit_length() - 1
    buckets, chunk = table.shape[0], table.shape[2]
    cap = codes.shape[1]
    dp, tables = lax.axis_size("dp"), lax.axis_size("table")
    me, column = lax.axis_index("dp"), lax.axis_index("table")
    ids = 2 * dp
    id_bits = ids.bit_length() - 1
    low_row = 24
    pairs_each = width // parts_of_gram

    def load_copies(part):
        at = pl.ds(pl.multiple_of(part * pairs_each, pairs_each), pairs_each)
        return [
            pltpu.make_async_copy(source.at[:, at], target.at[:, at], load_sems.at[kind, part])
            for kind, (source, target) in enumerate(((steps_hbm, steps), (diffs_hbm, diffs)))
        ]

    half = column % 2
    partner = {"table": column + 1 - 2 * half}
    lanes = pl.ds(pl.multiple_of(half * LANES, LANES), LANES)
    mine = features.at[half, me]
    features[half, me, slots + 1 : low_row] = jnp.zeros((low_row - slots - 1, LANES), I32)
    locals_ = [
        pltpu.make_async_copy(high_hbm.at[:, lanes], mine.at[pl.ds(0, slots)], local_sems.at[0]),
        pltpu.make_async_copy(low_hbm.at[:, lanes], mine.at[pl.ds(low_row, slots)], local_sems.at[1]),
        pltpu.make_async_copy(labels_hbm.at[:, lanes], mine.at[pl.ds(slots, 1)], local_sems.at[2]),
    ]
    for copy in locals_:
        copy.start()
    barrier = pltpu.get_barrier_semaphore()
    friends = others("dp") + others("table")
    for peer in friends:
        pl.semaphore_signal(barrier, inc=1, device_id=peer, device_id_type=MESH)

    def start_load(part, _):
        for copy in load_copies(part):
            copy.start()
        return 0

    lax.fori_loop(0, parts_of_gram, start_load, 0)
    weight_copy = pltpu.make_async_copy(weights_hbm, weights, weight_sem)
    weight_copy.start()

    def gram(part, carry):
        for copy in load_copies(part):
            copy.wait()

        def body(number, carry):
            at = pl.ds(pl.multiple_of(part * pairs_each + number * LANES, LANES), LANES)
            step, diff = steps[:, at], diffs[:, at]
            new = []
            for i in range(mem):
                row = jnp.broadcast_to(diffs[i : i + 1, at], diff.shape)
                new.append(carry[2 * i] + step * row)
                new.append(carry[2 * i + 1] + diff * row)
            return tuple(new)

        return lax.fori_loop(0, pairs_each // LANES, body, carry, unroll=4)

    ahead = ((dp - 1 - me) * parts_of_gram) // (dp + 2)
    carry = (jnp.zeros((mem, LANES), F32),) * (2 * mem)
    carry = lax.fori_loop(0, ahead, gram, carry)

    for copy in locals_:
        copy.wait()
    pl.semaphore_wait(barrier, len(friends))

    def across(step):
        return wire(mine, mine, send_sems.at[step - 1], recv_sems.at[step - 1], {"dp": me ^ step})

    def over(step):
        source = features.at[half, me ^ step]
        return wire(source, source, pass_sems.at[step], take_sems.at[step], partner)

    def start_across(step, _):
        across(dp - step).start()
        return 0

    lax.fori_loop(1, dp, start_across, 0)
    over(0).start()
    weight_copy.wait()
    for b in range(buckets):
        tops, rests = split(weights[b * chunk : (b + 1) * chunk].T)
        table[b, :LANES] = tops
        table[b, LANES:] = rests
    later = ahead + 3
    last = later + (parts_of_gram - later + 1) // 3
    carry = lax.fori_loop(ahead, later, gram, carry)

    device = me * tables + column
    spot = iota((8, LANES), 0)
    invalid = 1 << 30
    depth = ranked.shape[0] // 8
    mask, limit = (count << id_bits) - 1, width << id_bits
    rests_of = slots % 8
    assert slots % 8 in (0, 4)
    tiles = [(8 * n + spot, True) for n in range(slots // 8)]
    if rests_of:
        tiles.append((slots - 4 + (spot & 3), False))
    starts = [
        [((slot * slot_mult[k] + shifts[k]) - device * width) << id_bits for k in range(HASHES)]
        for slot, _ in tiles
    ]

    def consume(source, stack):
        stack = list(stack)
        for number, (_, full) in enumerate(tiles):
            if full:
                group = [
                    (
                        features[h, source, 8 * number : 8 * number + 8],
                        features[h, source, low_row + 8 * number : low_row + 8 * number + 8],
                        2 * source + h,
                    )
                    for h in range(2)
                ]
            else:
                at = slots - 4
                pair = [
                    jnp.concatenate([features[h, source, at + base : at + base + 4] for h in range(2)], axis=0)
                    for base in (0, low_row)
                ]
                group = [(*pair, 2 * source + (spot >> 2))]
            for high, low, name in group:
                for k in range(HASHES):
                    key = (
                        high * (high_mult[k] << id_bits)
                        + low * (low_mult[k] << id_bits)
                        + (starts[number][k] + name)
                    ) & mask
                    owned = key < limit
                    for level in reversed(range(1, depth)):
                        stack[level] = jnp.where(owned, stack[level - 1], stack[level])
                    stack[0] = jnp.where(owned, key, stack[0])
        return tuple(stack)

    def receive(step, stack):
        across(step).wait_recv()
        over(step).start()
        over(step - 1).wait_recv()
        return consume(me ^ (step - 1), stack)

    stack = (jnp.full((8, LANES), invalid, I32),) * depth
    stack = lax.fori_loop(1, dp, receive, stack)
    over(dp - 1).wait_recv()
    stack = consume(me ^ (dp - 1), stack)

    spilled = jnp.where(stack[-1] < invalid, 1, 0)
    ends = []
    for b in range(buckets):
        below = jnp.zeros((8, LANES), I32)
        for value in stack:
            below = below + jnp.where(value < (((b + 1) * chunk * LANES) << id_bits), 1, 0)
        ends.append(jnp.broadcast_to(jnp.sum(below, axis=0, keepdims=True), (8, LANES)))
    begins = [jnp.zeros((8, LANES), I32)] + ends[:-1]
    for begin, end in zip(begins, ends):
        spilled = jnp.where(end - begin > cap, 1, spilled)
    spilled = jnp.where(begins[-1] > LANES - 1, 1, spilled)
    values = sort_lanes(list(stack))
    for level in range(depth):
        ranked[pl.ds(level, 8, stride=depth), :] = values[level]
    ordered = [ranked[8 * n : 8 * n + 8] for n in range(depth)]
    for b in range(buckets):
        lifted = lift(ordered, begins[b], cap) if b else ordered[: cap // 8]
        for n, tile in enumerate(lifted):
            codes[b, 8 * n : 8 * n + 8] = tile

    def fetch(b, number):
        rows = [codes[b, pl.ds(number * WIDE + n, 1), :] for n in range(WIDE)]
        code = jnp.concatenate(rows, axis=1)
        return (code >> (7 + id_bits)) - b * chunk, (code >> id_bits) & (LANES - 1), code & (ids - 1)

    def gather(number, total):
        for b in range(buckets):
            row, lane, name = fetch(b, number)
            found = jnp.dot(table[b], one_hot(row, chunk), preferred_element_type=F32)
            value = choose(found[:LANES] + found[LANES:], lane)
            for n in range(WIDE):
                at = slice(n * LANES, (n + 1) * LANES)
                total = total + jnp.where(iota((ids, LANES), 0) == name[:, at], value[:, at], 0.0)
        return total

    margin = lax.fori_loop(0, cap // WIDE, gather, jnp.zeros((ids, LANES), F32), unroll=UNROLL)
    near[column] = margin
    copies = send(near.at[column], near.at[column], others("table"), near_send, near_recv)
    both[...] = jnp.zeros_like(both)
    carry = lax.fori_loop(later, last, gram, carry)
    margin = finish(copies, near)
    far[me] = margin
    copies = send(far.at[me], far.at[me], others("dp"), far_send, far_recv)
    labels = jnp.concatenate(
        [features[n % 2, n // 2, slots : slots + 1] for n in range(ids)], axis=0
    ).astype(F32)

    def retire(step, _):
        across(step).wait_send()
        over(step).wait_send()
        return 0

    over(0).wait_send()
    lax.fori_loop(1, dp, retire, 0)
    carry = lax.fori_loop(last, parts_of_gram, gram, carry)
    gram_here = gram_row(carry, mem)
    margin = finish(copies, far)
    residual = 1.0 / (1.0 + jnp.exp(-margin)) - labels

    def scatter(number, _):
        for b in range(buckets):
            row, lane, name = fetch(b, number)
            spread = jnp.concatenate([residual] * WIDE, axis=1)
            value = jnp.sum(jnp.where(iota(spread.shape, 0) == name, spread, 0.0), axis=0, keepdims=True)
            top = value.astype(BF16).astype(F32)
            here = stripes(lane, LANES)
            terms = [
                jnp.where(here, jnp.broadcast_to(piece, here.shape).astype(BF16), jnp.array(0, BF16))
                for piece in (top, value - top)
            ]
            both[b] += lax.dot_general(
                one_hot(row, chunk), jnp.concatenate(terms, axis=0), (((1,), (1,)), ((), ())),
                preferred_element_type=F32,
            )
        return 0

    lax.fori_loop(0, cap // WIDE, scatter, 0, unroll=UNROLL)
    for b in range(buckets):
        at = slice(b * chunk, (b + 1) * chunk)
        gradient[at] = both[b, :, :LANES] + both[b, :, LANES:] + l2_weight * weights[at]

    def product(number, sums):
        sums = list(sums)
        for i in range(8):
            at = pl.ds(pl.multiple_of(number * 8 * LANES, LANES) + i * LANES, LANES)
            line = jnp.broadcast_to(gradient[pl.ds(number * 8 + i, 1), :], (mem, LANES))
            sums[2 * i] = sums[2 * i] + steps[:, at] * line
            sums[2 * i + 1] = sums[2 * i + 1] + diffs[:, at] * line
        return tuple(sums)

    sums = (jnp.zeros((mem, LANES), F32),) * 16
    sums = list(lax.fori_loop(0, width // (8 * LANES), product, sums, unroll=2))
    while len(sums) > 2:
        sums = [a + b for a, b in zip(sums[: len(sums) // 2], sums[len(sums) // 2 :])]
    held[device, 0:1] = gram_here
    held[device, 1:2] = to_row(sums)
    held[device, 2:3] = jnp.max(spilled, axis=0, keepdims=True).astype(F32)
    peers = [
        {"dp": lax.rem(me + down, dp), "table": lax.rem(column + sideways, tables)}
        for down in range(dp)
        for sideways in range(tables)
        if down or sideways
    ]
    total = finish(send(held.at[device], held.at[device], peers, held_send, held_recv), held)
    scale, on_diffs, on_steps = coefficients(total[0:1], total[1:2], mem)
    scale, on_diffs, on_steps = -scale, -on_diffs, -on_steps

    def body(number, _):
        rows = []
        for i in range(8):
            at = pl.ds(pl.multiple_of(number * 8 * LANES, LANES) + i * LANES, LANES)
            rows.append(on_diffs * diffs[:, at] + on_steps * steps[:, at])
        at = pl.ds(pl.multiple_of(number * 8, 8), 8)
        out_ref[at, :] = scale * gradient[at, :] + row_sums(rows)
        return 0

    lax.fori_loop(0, out_ref.shape[0] // 8, body, 0, unroll=8)
    flag_ref[0] = jnp.max(jnp.where(total[2:3] > 0.0, 1, 0))


def whole(high, low, labels, weights, steps, diffs):
    mem, width = steps.shape
    slots = high.shape[0]
    dp, tables = lax.axis_size("dp"), lax.axis_size("table")
    devices = dp * tables
    rows = width // LANES
    chunk = min(2 * LANES, rows)
    buckets = rows // chunk
    cap = CAP if buckets > 1 else 3 * CAP
    DMA = pltpu.SemaphoreType.DMA
    parts = 8
    return pl.pallas_call(
        functools.partial(whole_kernel, (width * devices, slots, parts)),
        in_specs=[HBM] * 6,
        out_specs=[VMEM, SMEM],
        out_shape=[jax.ShapeDtypeStruct((rows, LANES), F32), jax.ShapeDtypeStruct((1,), I32)],
        scratch_shapes=[
            pltpu.VMEM((mem, width), F32),
            pltpu.VMEM((mem, width), F32),
            pltpu.VMEM((rows, LANES), F32),
            pltpu.VMEM((buckets, 2 * LANES, chunk), BF16),
            pltpu.VMEM((2, dp, 24 + slots, LANES), I32),
            pltpu.VMEM((8 * DEPTH, LANES), I32),
            pltpu.VMEM((buckets, cap, LANES), I32),
            pltpu.VMEM((buckets, chunk, 2 * LANES), F32),
            pltpu.VMEM((rows, LANES), F32),
            pltpu.VMEM((tables, 2 * dp, LANES), F32),
            pltpu.VMEM((dp, 2 * dp, LANES), F32),
            pltpu.VMEM((devices, 3, LANES), F32),
            pltpu.VMEM((8, LANES), F32),
            DMA((2, parts)),
            DMA,
            DMA((3,)),
            DMA((dp - 1,)),
            DMA((dp - 1,)),
            DMA((dp,)),
            DMA((dp,)),
            DMA((tables - 1,)),
            DMA((tables - 1,)),
            DMA((dp - 1,)),
            DMA((dp - 1,)),
            DMA((devices - 1,)),
            DMA((devices - 1,)),
        ],
        compiler_params=pltpu.CompilerParams(
            vmem_limit_bytes=BUDGET, collective_id=3, has_side_effects=True
        ),
        name="whole",
    )(high, low, labels, weights, steps, diffs)


def quick(feature_high, feature_low, labels, weights, history_steps, history_diffs):
    width = weights.shape[0]
    direction, flag = whole(
        feature_high, feature_low, labels[None, :], weights.reshape(width // LANES, LANES),
        history_steps, history_diffs,
    )
    return lax.cond(
        flag[0] > 0,
        lambda: local(feature_high, feature_low, labels, weights, history_steps, history_diffs),
        lambda: direction.reshape(-1),
    )


def solution(mesh):
    placed = (
        P(None, "dp"),
        P(None, "dp"),
        P("dp"),
        P(("dp", "table")),
        P(None, ("dp", "table")),
        P(None, ("dp", "table")),
    )
    return jax.shard_map(
        quick, mesh=mesh, in_specs=placed, out_specs=P(("dp", "table")), check_vma=False
    )
```

```python
import functools

import jax
import jax.numpy as jnp
from jax import lax
from jax.experimental import pallas as pl
from jax.experimental.pallas import tpu as pltpu
from jax.sharding import PartitionSpec as P

HASHES = 4
LANES = 128
BLOCK = 16
GROUP = 4
DEPTH = 24
CAP = 40
WIDE = 8
UNROLL = 5

high_mult = (40503, 96469, 255361, 362443)
low_mult = (2053, 6151, 12289, 98317)
slot_mult = (1543, 3079, 769, 3457)
shifts = (0, 1048573, 2097143, 3145727)
l2_weight = 1.0
BUDGET = 50 << 20
ROOM = 60 << 20
F32, BF16, I32 = jnp.float32, jnp.bfloat16, jnp.int32
MESH = pl.DeviceIdType.MESH
VMEM = pl.BlockSpec(memory_space=pltpu.VMEM)
HBM = pl.BlockSpec(memory_space=pltpu.HBM)
SMEM = pl.BlockSpec(memory_space=pltpu.SMEM)


def iota(shape, axis):
    return lax.broadcasted_iota(I32, shape, axis)


def split(value):
    top = value.astype(BF16)
    return top, (value - top.astype(F32)).astype(BF16)


def hot(index, count):
    shape = (count, index.shape[1])
    return jnp.where(iota(shape, 0) == index, 1.0, 0.0).astype(BF16)


def greet(peers):
    barrier = pltpu.get_barrier_semaphore()
    for peer in peers:
        pl.semaphore_signal(barrier, inc=1, device_id=peer, device_id_type=MESH)
    pl.semaphore_wait(barrier, len(peers))


def others(axis):
    size, me = lax.axis_size(axis), lax.axis_index(axis)
    return [{axis: lax.rem(me + step, size)} for step in range(1, size)]


def send(source, target, peers, send_sems, recv_sems):
    copies = []
    for number, peer in enumerate(peers):
        copy = pltpu.make_async_remote_copy(
            src_ref=source,
            dst_ref=target,
            send_sem=send_sems.at[number],
            recv_sem=recv_sems.at[number],
            device_id=peer,
            device_id_type=MESH,
        )
        copy.start()
        copies.append(copy)
    return copies


def stage(axis, held, value, sems):
    me = lax.axis_index(axis)
    held[me] = value
    return send(held.at[me], held.at[me], others(axis), *sems)


def finish(copies, held):
    for copy in copies:
        copy.wait()
    total = held[0]
    for number in range(1, held.shape[0]):
        total = total + held[number]
    return total


def sum_scratch(shape):
    near, far = lax.axis_size("table"), lax.axis_size("dp")
    return [
        pltpu.VMEM((near, *shape), F32),
        pltpu.VMEM((far, *shape), F32),
        pltpu.SemaphoreType.DMA((near - 1,)),
        pltpu.SemaphoreType.DMA((near - 1,)),
        pltpu.SemaphoreType.DMA((far - 1,)),
        pltpu.SemaphoreType.DMA((far - 1,)),
    ]


def load(steps_hbm, diffs_hbm, steps, diffs, sems, first=0):
    parts, width = sems.shape[1], steps.shape[1]
    pairs = []
    for part in range(parts):
        size = width // parts
        pair = []
        for kind, (source, target) in enumerate(((steps_hbm, steps), (diffs_hbm, diffs))):
            copy = pltpu.make_async_copy(
                source.at[:, pl.ds(first + part * size, size)],
                target.at[:, pl.ds(part * size, size)],
                sems.at[kind, part],
            )
            copy.start()
            pair.append(copy)
        pairs.append(pair)
    return pairs


def gram_part(steps, diffs, pairs, part, carry):
    mem = steps.shape[0]
    each = steps.shape[1] // len(pairs) // LANES
    for copy in pairs[part]:
        copy.wait()

    def body(number, carry):
        at = pl.ds(pl.multiple_of(number * LANES, LANES), LANES)
        step, diff = steps[:, at], diffs[:, at]
        new = []
        for i in range(mem):
            row = jnp.broadcast_to(diffs[i : i + 1, at], diff.shape)
            new.append(carry[2 * i] + step * row)
            new.append(carry[2 * i + 1] + diff * row)
        return tuple(new)

    return lax.fori_loop(part * each, (part + 1) * each, body, carry, unroll=4)


def to_row(columns):
    mem = columns[0].shape[0]
    total = jnp.zeros((mem, LANES), F32)
    spot = iota((mem, LANES), 1) - iota((mem, LANES), 0)
    for number, column in enumerate(columns):
        total = jnp.where(spot == number * mem, jnp.sum(column, axis=1, keepdims=True), total)
    return jnp.sum(total, axis=0, keepdims=True)


def from_row(row, number, mem):
    spot = iota((mem, LANES), 1) - iota((mem, LANES), 0)
    wide = jnp.broadcast_to(row, (mem, LANES))
    column = jnp.sum(jnp.where(spot == number * mem, wide, 0.0), axis=1, keepdims=True)
    return jnp.broadcast_to(column, (mem, LANES))


def gram_row(carry, mem):
    return to_row([carry[2 * i] for i in range(mem)] + [carry[2 * i + 1] for i in range(mem)])


def share_kernel(mine_ref, steps_hbm, diffs_hbm, every_ref, gram_ref,
                 steps, diffs, send_sems, recv_sems, sems):
    mem = steps.shape[0]
    pairs = load(steps_hbm, diffs_hbm, steps, diffs, sems)
    me = lax.axis_index("dp")
    every_ref[me] = mine_ref[...]
    peers = others("dp")
    greet(peers)
    sent = send(mine_ref, every_ref.at[me], peers, send_sems, recv_sems)
    carry = (jnp.zeros((mem, LANES), F32),) * (2 * mem)
    for part in range(len(pairs)):
        carry = gram_part(steps, diffs, pairs, part, carry)
    gram_ref[...] = gram_row(carry, mem)
    for copy in sent:
        copy.wait()


def share(mine, steps, diffs):
    mem, width = steps.shape
    dp = lax.axis_size("dp")
    return pl.pallas_call(
        share_kernel,
        in_specs=[VMEM] + [HBM] * 2,
        out_specs=[VMEM] * 2,
        out_shape=[
            jax.ShapeDtypeStruct((dp, *mine.shape), I32),
            jax.ShapeDtypeStruct((1, LANES), F32),
        ],
        scratch_shapes=[
            pltpu.VMEM((mem, 3 * width // 4), F32),
            pltpu.VMEM((mem, 3 * width // 4), F32),
            pltpu.SemaphoreType.DMA((dp - 1,)),
            pltpu.SemaphoreType.DMA((dp - 1,)),
            pltpu.SemaphoreType.DMA((2, 3)),
        ],
        compiler_params=pltpu.CompilerParams(
            vmem_limit_bytes=BUDGET, collective_id=0, has_side_effects=True
        ),
        name="share",
    )(mine, steps, diffs)


def reduce_kernel(margin_ref, gram_ref, steps_hbm, diffs_hbm, out_ref, grams_ref,
                  steps, diffs, load_sems, near, far, *sems):
    mem, size = steps.shape
    pairs = load(steps_hbm, diffs_hbm, steps, diffs, load_sems, steps_hbm.shape[1] - size)
    greet(others("table") + others("dp"))
    carry = (jnp.zeros((mem, LANES), F32),) * (2 * mem)
    copies = stage("table", near, margin_ref[...], sems[:2])
    copies = stage("dp", far, finish(copies, near), sems[2:])
    carry = gram_part(steps, diffs, pairs, 0, carry)
    grams_ref[...] = gram_ref[...] + gram_row(carry, mem)
    out_ref[...] = finish(copies, far)


def reduced(margin, grams, steps, diffs):
    mem, width = steps.shape
    return pl.pallas_call(
        reduce_kernel,
        in_specs=[VMEM] * 2 + [HBM] * 2,
        out_specs=[VMEM] * 2,
        out_shape=[
            jax.ShapeDtypeStruct(margin.shape, F32),
            jax.ShapeDtypeStruct((1, LANES), F32),
        ],
        scratch_shapes=[
            pltpu.VMEM((mem, width // 4), F32),
            pltpu.VMEM((mem, width // 4), F32),
            pltpu.SemaphoreType.DMA((2, 1)),
        ]
        + sum_scratch(margin.shape),
        compiler_params=pltpu.CompilerParams(
            vmem_limit_bytes=BUDGET, collective_id=1, has_side_effects=True
        ),
        name="reduce",
    )(margin, grams, steps, diffs)


def margin_kernel(count, subs, bits, slot_total, every_ref, weights_ref, margin_ref, slots_ref, levels_ref, table, features):
    device = lax.axis_index("dp") * lax.axis_size("table") + lax.axis_index("table")
    width = 1 << bits
    for number in range(2 * slot_total):
        features[number] = every_ref[:, number, :]
    tops, rests = split(weights_ref[...].T)
    table[: LANES] = tops
    table[LANES :] = rests

    def one_pass(number, _):
        base = number * BLOCK

        def body(slot, carry):
            seen, outs = carry[0], list(carry[1:])
            for sub in range(subs):
                group, half = sub // 2, sub % 2
                at = (pl.ds(group * 8, 8), pl.ds(half * LANES, LANES))
                high, low = features[(slot, *at)], features[(slot + slot_total, *at)]
                for k in range(HASHES):
                    index = (high * high_mult[k] + low * low_mult[k] + (slot * slot_mult[k] + shifts[k])) & (count - 1)
                    owned = (index >> bits) == device
                    place = jnp.where(owned, seen, -1)
                    code = (index & (width - 1)) | (sub << bits)
                    for level in range(BLOCK):
                        outs[level] = jnp.where(place == level, code, outs[level])
                    seen = seen + owned.astype(I32)
            return (seen, *outs)

        empty = jnp.full((8, LANES), -1, I32)
        final = lax.fori_loop(0, slot_total, body, (jnp.zeros((8, LANES), I32) - base,) + (empty,) * BLOCK)
        for level in range(BLOCK):
            slots_ref[:, base + level, :] = final[1 + level]
        return final[0] + base

    seen = one_pass(0, None)
    most = jnp.max(seen)
    lax.fori_loop(1, (most + BLOCK - 1) // BLOCK, lambda n, c: (one_pass(n, None), c)[1], 0)
    for row in range(8):
        levels_ref[row] = (jnp.max(seen[row : row + 1]) + GROUP - 1) // GROUP

    def rows(row, _):
        def body(number, total):
            codes = slots_ref[row, pl.ds(number * GROUP, GROUP), :]
            code = jnp.concatenate([codes[i : i + 1] for i in range(GROUP)], axis=1)
            local = code & (width - 1)
            found = jnp.dot(table[...], hot(local >> 7, width // LANES), preferred_element_type=F32)
            found = found[:LANES] + found[LANES:]
            chosen = jnp.where(iota(found.shape, 0) == (local & (LANES - 1)), found, 0.0)
            value = jnp.sum(chosen, axis=0, keepdims=True)
            sub = code >> bits
            for i in range(GROUP):
                at = slice(i * LANES, (i + 1) * LANES)
                total = total + jnp.where(iota((subs, LANES), 0) == sub[:, at], value[:, at], 0.0)
            return total

        total = lax.fori_loop(0, levels_ref[row], body, jnp.zeros((subs, LANES), F32))
        for sub in range(subs):
            here = iota((8, LANES), 0) == row
            margin_ref[sub] = jnp.where(here, total[sub : sub + 1], margin_ref[sub])
        return 0

    margin_ref[...] = jnp.zeros_like(margin_ref)
    lax.fori_loop(0, 8, rows, 0)


def margins(every, weights, count, subs, bits, slots):
    levels = -(-subs * HASHES * slots // BLOCK) * BLOCK
    return pl.pallas_call(
        functools.partial(margin_kernel, count, subs, bits, slots),
        in_specs=[VMEM] * 2,
        out_specs=[VMEM, VMEM, SMEM],
        out_shape=[
            jax.ShapeDtypeStruct((subs, 8, LANES), F32),
            jax.ShapeDtypeStruct((8, levels, LANES), I32),
            jax.ShapeDtypeStruct((8,), I32),
        ],
        scratch_shapes=[
            pltpu.VMEM((2 * LANES, (1 << bits) // LANES), BF16),
            pltpu.VMEM((2 * slots, every.shape[0], every.shape[2]), I32),
        ],
        compiler_params=pltpu.CompilerParams(vmem_limit_bytes=BUDGET),
        name="margins",
    )(every, weights)


def gradient_kernel(subs, bits, label_row, total_ref, every_ref, slots_ref, levels_ref, weights_ref,
                    gradient_ref, residual, both):
    width = 1 << bits
    for sub in range(subs):
        label = every_ref[sub // 2 * 8 : sub // 2 * 8 + 8, label_row, sub % 2 * LANES : sub % 2 * LANES + LANES]
        residual[:, sub, :] = 1.0 / (1.0 + jnp.exp(-total_ref[sub])) - label.astype(F32)
    both[...] = jnp.zeros_like(both)

    def rows(row, _):
        value = residual[row]

        def body(number, _):
            codes = slots_ref[row, pl.ds(number * GROUP, GROUP), :]
            code = jnp.concatenate([codes[i : i + 1] for i in range(GROUP)], axis=1)
            local = code & (width - 1)
            sub = code >> bits
            wide = jnp.concatenate([value] * GROUP, axis=1)
            mine = jnp.sum(jnp.where(iota(wide.shape, 0) == sub, wide, 0.0), axis=0, keepdims=True)
            column = iota((LANES, GROUP * LANES), 0) == (local & (LANES - 1))
            top, rest = split(jnp.where(column, mine, 0.0))
            terms = jnp.concatenate([top, rest], axis=0)
            both[...] += lax.dot_general(
                hot(local >> 7, width // LANES), terms, (((1,), (1,)), ((), ())), preferred_element_type=F32
            )
            return 0

        lax.fori_loop(0, levels_ref[row], body, 0)
        return 0

    lax.fori_loop(0, 8, rows, 0)
    gradient_ref[...] = both[:, :LANES] + both[:, LANES:] + l2_weight * weights_ref[...]


def gradients(total, every, slots, levels, weights, subs, bits, label_row):
    return pl.pallas_call(
        functools.partial(gradient_kernel, subs, bits, label_row),
        in_specs=[VMEM, VMEM, VMEM, SMEM, VMEM],
        out_specs=VMEM,
        out_shape=jax.ShapeDtypeStruct(weights.shape, F32),
        scratch_shapes=[
            pltpu.VMEM((8, subs, LANES), F32),
            pltpu.VMEM((weights.shape[0], 2 * LANES), F32),
        ],
        compiler_params=pltpu.CompilerParams(vmem_limit_bytes=BUDGET),
        name="gradient",
    )(total, every, slots, levels, weights)


def coefficients(grams, products, mem):
    place = iota((mem, LANES), 0)

    def pick(array, number):
        return jnp.broadcast_to(array[number : number + 1], (mem, LANES))

    cross = [from_row(grams, i, mem) for i in range(mem)]
    square = [from_row(grams, mem + i, mem) for i in range(mem)]
    pairs = [pick(cross[i], i) for i in range(mem)]
    inverse = [1.0 / pair for pair in pairs]
    by_step, by_diff = from_row(products, 0, mem), from_row(products, 1, mem)
    alphas = [None] * mem
    for i in reversed(range(mem)):
        alphas[i] = inverse[i] * pick(by_step, i)
        by_step = by_step - alphas[i] * cross[i]
        by_diff = by_diff - alphas[i] * square[i]
    scale = pairs[mem - 1] / pick(square[mem - 1], mem - 1)
    by_diff = scale * by_diff
    on_steps = jnp.zeros((mem, LANES), F32)
    on_diffs = jnp.zeros((mem, LANES), F32)
    for i in range(mem):
        extra = jnp.sum(on_steps * cross[i], axis=0, keepdims=True)
        beta = inverse[i] * (pick(by_diff, i) + extra)
        on_steps = jnp.where(place == i, alphas[i] - beta, on_steps)
        on_diffs = jnp.where(place == i, -scale * alphas[i], on_diffs)
    return scale, on_diffs, on_steps


def row_sums(tiles):
    place = iota((8, LANES), 0)
    gap = 1
    while len(tiles) > 1:
        low = (place & gap) == 0
        tiles = [
            jnp.where(low, a, b) + pltpu.roll(jnp.where(low, b, a), 8 - gap, 0)
            for a, b in zip(tiles[::2], tiles[1::2])
        ]
        gap *= 2
    return tiles[0]


def direction_kernel(grams_ref, gradient_ref, steps_hbm, diffs_hbm, out_ref,
                     steps, diffs, load_sems, held, send_sems, recv_sems):
    mem, width = steps.shape
    pairs = load(steps_hbm, diffs_hbm, steps, diffs, load_sems)
    near, far = lax.axis_size("table"), lax.axis_size("dp")
    column, row = lax.axis_index("table"), lax.axis_index("dp")
    peers = [
        {"dp": lax.rem(row + down, far), "table": lax.rem(column + across, near)}
        for down in range(far)
        for across in range(near)
        if down or across
    ]
    barrier = pltpu.get_barrier_semaphore()
    for peer in peers:
        pl.semaphore_signal(barrier, inc=1, device_id=peer, device_id_type=MESH)

    def product(number, carry):
        by_step, by_diff = carry
        for i in range(8):
            at = pl.ds(pl.multiple_of(number * 8 * LANES, LANES) + i * LANES, LANES)
            line = jnp.broadcast_to(gradient_ref[pl.ds(number * 8 + i, 1), :], (mem, LANES))
            by_step = by_step + steps[:, at] * line
            by_diff = by_diff + diffs[:, at] * line
        return by_step, by_diff

    carry = (jnp.zeros((mem, LANES), F32),) * 2
    each = width // len(pairs) // (8 * LANES)
    for part, pair in enumerate(pairs):
        for copy in pair:
            copy.wait()
        carry = lax.fori_loop(part * each, (part + 1) * each, product, carry)
    me = row * near + column
    held[me, 0:1] = grams_ref[...]
    held[me, 1:2] = to_row(carry)
    pl.semaphore_wait(barrier, len(peers))
    total = finish(send(held.at[me], held.at[me], peers, send_sems, recv_sems), held)
    scale, on_diffs, on_steps = coefficients(total[0:1], total[1:2], mem)
    scale, on_diffs, on_steps = -scale, -on_diffs, -on_steps

    def body(number, _):
        rows = []
        for i in range(8):
            at = pl.ds(pl.multiple_of(number * 8 * LANES, LANES) + i * LANES, LANES)
            rows.append(on_diffs * diffs[:, at] + on_steps * steps[:, at])
        at = pl.ds(pl.multiple_of(number * 8, 8), 8)
        out_ref[at, :] = scale * gradient_ref[at, :] + row_sums(rows)
        return 0

    lax.fori_loop(0, out_ref.shape[0] // 8, body, 0, unroll=2)


def directions(grams, gradient, steps, diffs):
    mem, width = steps.shape
    devices = lax.axis_size("dp") * lax.axis_size("table")
    return pl.pallas_call(
        direction_kernel,
        in_specs=[VMEM] * 2 + [HBM] * 2,
        out_specs=VMEM,
        out_shape=jax.ShapeDtypeStruct(gradient.shape, F32),
        scratch_shapes=[
            pltpu.VMEM((mem, width), F32),
            pltpu.VMEM((mem, width), F32),
            pltpu.SemaphoreType.DMA((2, 4)),
            pltpu.VMEM((devices, 2, LANES), F32),
            pltpu.SemaphoreType.DMA((devices - 1,)),
            pltpu.SemaphoreType.DMA((devices - 1,)),
        ],
        compiler_params=pltpu.CompilerParams(
            vmem_limit_bytes=BUDGET, collective_id=2, has_side_effects=True
        ),
        name="direction",
    )(grams, gradient, steps, diffs)


def local(feature_high, feature_low, labels, weights, history_steps, history_diffs):
    width = weights.shape[0]
    parts = lax.axis_size("dp")
    count = width * parts * lax.axis_size("table")
    bits = width.bit_length() - 1
    slots = feature_high.shape[0]
    subs = parts * feature_high.shape[1] // 1024
    table = weights.reshape(width // LANES, LANES)
    mine = jnp.concatenate([feature_high, feature_low, labels[None, :]], axis=0)
    every, partial_gram = share(mine, history_steps, history_diffs)
    margin, listed, levels = margins(every, table, count, subs, bits, slots)
    total, grams = reduced(margin, partial_gram, history_steps, history_diffs)
    gradient = gradients(total, every, listed, levels, table, subs, bits, 2 * slots)
    return directions(grams, gradient, history_steps, history_diffs).reshape(-1)


def wire(source, target, send_sem, recv_sem, peer):
    return pltpu.make_async_remote_copy(
        src_ref=source,
        dst_ref=target,
        send_sem=send_sem,
        recv_sem=recv_sem,
        device_id=peer,
        device_id_type=MESH,
    )


def share_out(array, place, peers, send_sem, recv_sem):
    for peer in peers:
        wire(array.at[place], array.at[place], send_sem, recv_sem, peer).start()


def collect(array, send_sem, recv_sem):
    rest = array.at[pl.ds(0, array.shape[0] - 1)]
    wire(rest, rest, send_sem, recv_sem, others("table")[0]).wait()
    total = array[0]
    for number in range(1, array.shape[0]):
        total = total + array[number]
    return total


def merge_pairs(count):
    pairs = []
    size = 1
    while size < count:
        step = size
        while step >= 1:
            for base in range(step % size, count - step, 2 * step):
                for i in range(base, min(base + step, count - step)):
                    if i // (2 * size) == (i + step) // (2 * size):
                        pairs.append((i, i + step))
            step //= 2
        size *= 2
    return pairs


def settle(values):
    count = len(values)
    if count % 2:
        for i in range(count):
            for j in range(i + 1, count):
                low, high = values[i], values[j]
                values[i], values[j] = jnp.minimum(low, high), jnp.maximum(low, high)
        return values
    half = count // 2
    lows = [jnp.minimum(a, b) for a, b in zip(values[:half], values[half:])]
    highs = [jnp.maximum(a, b) for a, b in zip(values[:half], values[half:])]
    if half == 1:
        return lows + highs
    return settle(lows) + settle(highs)


def sort_lanes(values):
    spot = iota(values[0].shape, 0)
    bits = [(spot >> n) & 1 for n in range(3)]
    flips = -(bits[0] ^ bits[1] ^ bits[2])
    values = [value ^ flips for value in values]
    for i, j in merge_pairs(len(values)):
        low, high = values[i], values[j]
        values[i], values[j] = jnp.minimum(low, high), jnp.maximum(low, high)
    for level in range(3):
        flips = -bits[level]
        values = [value ^ flips for value in values]
        for inner in reversed(range(level + 1)):
            gap = 1 << inner
            upper = bits[inner] == 1
            values = [
                jnp.where(
                    upper,
                    jnp.maximum(value, pltpu.roll(value, gap, 0)),
                    jnp.minimum(value, pltpu.roll(value, 8 - gap, 0)),
                )
                for value in values
            ]
        values = settle(values)
    return values


def lift(tiles, offset, length):
    spot = iota(tiles[0].shape, 0)
    bit = 64
    while bit >= 8:
        keep = (bit - 1 + length + 7) // 8 + (1 if bit > 8 else 0)
        move = bit // 8
        taken = (offset & bit) != 0
        keep = min(keep, len(tiles) - move)
        tiles = [jnp.where(taken, tiles[n + move], tiles[n]) for n in range(keep)]
        bit //= 2
    while bit >= 1:
        taken = (offset & bit) != 0
        rolled = [pltpu.roll(tile, 8 - bit, 0) for tile in tiles]
        moved = [jnp.where(spot < 8 - bit, a, b) for a, b in zip(rolled, rolled[1:] + rolled[-1:])]
        tiles = [jnp.where(taken, a, b) for a, b in zip(moved, tiles)]
        bit //= 2
    return tiles[: length // 8]


def stripes(row, count):
    shape = (count, row.shape[1])
    value = jnp.broadcast_to(row.astype(F32), shape).astype(BF16)
    return iota(shape, 0).astype(BF16) == value


def one_hot(row, count):
    return jnp.where(stripes(row, count), jnp.array(1, BF16), jnp.array(0, BF16))


def choose(found, lane):
    size = found.shape[1]
    lane = jnp.broadcast_to(lane, (8, size))
    parts = [found[n : n + 8] for n in range(0, LANES, 8)]
    bit = 8
    while len(parts) > 1:
        taken = (lane & bit) != 0
        parts = [jnp.where(taken, b, a) for a, b in zip(parts[::2], parts[1::2])]
        bit *= 2
    chosen = jnp.where(iota((8, size), 0) == (lane & 7), parts[0], 0.0)
    return jnp.sum(chosen, axis=0, keepdims=True)


def whole_kernel(dims, high_hbm, low_hbm, labels_hbm, weights_hbm, steps_hbm, diffs_hbm,
                 out_ref, flag_ref,
                 steps, diffs, weights, table, features, ranked, codes, both, gradient,
                 near, far, held, grams,
                 load_sems, weight_sem, local_sems, send_sem, recv_sems, take_sems,
                 near_send, near_recv, far_send, far_recv, held_send, held_recv):
    count, slots, parts_of_gram = dims
    mem, lines = steps.shape[:2]
    width = lines * LANES
    bits = width.bit_length() - 1
    buckets, chunk = table.shape[0], table.shape[2]
    cap = codes.shape[1]
    dp, tables = lax.axis_size("dp"), lax.axis_size("table")
    me, column = lax.axis_index("dp"), lax.axis_index("table")
    ids = 2 * dp
    id_bits = ids.bit_length() - 1
    low_row = 24
    part_lines = lines // parts_of_gram

    loads = [
        pltpu.make_async_copy(source.at[:, i], target.at[i], load_sems.at[kind])
        for i in range(mem)
        for kind, (source, target) in enumerate(((steps_hbm, steps), (diffs_hbm, diffs)))
    ]

    def await_loads():
        pltpu.make_async_copy(steps, steps, load_sems.at[0]).wait()
        pltpu.make_async_copy(diffs, diffs, load_sems.at[1]).wait()

    half = column % 2
    partner = {"table": column + 1 - 2 * half}
    lanes = pl.ds(pl.multiple_of(half * LANES, LANES), LANES)
    mine = features.at[half, me]
    features[half, me, slots + 1 : low_row] = jnp.zeros((low_row - slots - 1, LANES), I32)
    locals_ = [
        pltpu.make_async_copy(high_hbm.at[:, lanes], mine.at[pl.ds(0, slots)], local_sems.at[0]),
        pltpu.make_async_copy(low_hbm.at[:, lanes], mine.at[pl.ds(low_row, slots)], local_sems.at[1]),
        pltpu.make_async_copy(labels_hbm.at[:, lanes], mine.at[pl.ds(slots, 1)], local_sems.at[2]),
    ]
    for copy in locals_:
        copy.start()
    barrier = pltpu.get_barrier_semaphore()
    opposite = {"dp": me ^ (dp - 1), "table": column + 1 - 2 * half}
    friends = others("dp") + others("table") + [opposite]
    for peer in friends:
        pl.semaphore_signal(barrier, inc=1, device_id=peer, device_id_type=MESH)

    for copy in loads:
        copy.start()
    weight_copy = pltpu.make_async_copy(weights_hbm, weights, weight_sem)
    weight_copy.start()

    half_mem = mem // 2
    passes = [
        [(steps, i, j) for i in range(0, half_mem) for j in range(mem)],
        [(steps, i, j) for i in range(half_mem, mem) for j in range(mem)],
        [(diffs, i, j) for i in range(mem) for j in range(i, mem)],
    ]

    def gram(part, _):
        first = 0
        for chosen in passes:
            size = len(chosen)

            def body(number, sums):
                at = pl.ds(pl.multiple_of(part * part_lines + number * 8, 8), 8)
                left = {i: chosen[0][0][i, at] for i in {i for _, i, _ in chosen}}
                right = left if chosen[0][0] is diffs else {j: diffs[j, at] for j in range(mem)}
                return tuple(total + left[i] * right[j] for total, (_, i, j) in zip(sums, chosen))

            sums = tuple(grams[first + n] for n in range(size))
            sums = lax.fori_loop(0, part_lines // 8, body, sums, unroll=2)
            for n in range(size):
                grams[first + n] = sums[n]
            first += size
        return 0

    def gram_line():
        where = {}
        for chosen in passes:
            for source, i, j in chosen:
                where[source is diffs, i, j] = len(where)
        columns = [row_sums([grams[where[False, j, i]] for j in range(mem)]) for i in range(mem)]
        columns += [
            row_sums([grams[where[True, min(i, j), max(i, j)]] for j in range(mem)]) for i in range(mem)
        ]
        return to_row(columns)

    later = ((dp - 1 - me) * parts_of_gram) // (2 * dp)
    last = later + (parts_of_gram - later + 2) // 3
    grams[...] = jnp.zeros_like(grams)
    for copy in locals_:
        copy.wait()

    pl.semaphore_wait(barrier, len(friends))

    def across(step):
        return wire(mine, mine, send_sem, recv_sems.at[step - 1], {"dp": me ^ step})

    def over(step):
        source = features.at[half, me ^ step]
        return wire(source, source, send_sem, take_sems.at[step], partner)

    def start_across(step, _):
        across(dp - step).start()
        return 0

    lax.fori_loop(1, dp, start_across, 0)
    direct = wire(mine, mine, send_sem, take_sems.at[dp - 1], opposite)
    direct.start()
    over(0).start()
    weight_copy.wait()
    for b in range(buckets):
        tops, rests = split(weights[b * chunk : (b + 1) * chunk].T)
        table[b, :LANES] = tops
        table[b, LANES:] = rests

    @pl.when(later > 0)
    def _():
        await_loads()
        lax.fori_loop(0, later, gram, 0)

    device = me * tables + column
    spot = iota((8, LANES), 0)
    invalid = 1 << 30
    depth = ranked.shape[0] // 8
    mask, limit = (count << id_bits) - 1, width << id_bits
    rests_of = slots % 8
    assert slots % 8 in (0, 4)
    tiles = [(8 * n + spot, True) for n in range(slots // 8)]
    if rests_of:
        tiles.append((slots - 4 + (spot & 3), False))
    starts = [
        [((slot * slot_mult[k] + shifts[k]) - device * width) << id_bits for k in range(HASHES)]
        for slot, _ in tiles
    ]

    def consume(source, stack):
        stack = list(stack)
        for number, (_, full) in enumerate(tiles):
            if full:
                group = [
                    (
                        features[h, source, 8 * number : 8 * number + 8],
                        features[h, source, low_row + 8 * number : low_row + 8 * number + 8],
                        2 * source + h,
                    )
                    for h in range(2)
                ]
            else:
                at = slots - 4
                pair = [
                    jnp.concatenate([features[h, source, at + base : at + base + 4] for h in range(2)], axis=0)
                    for base in (0, low_row)
                ]
                group = [(*pair, 2 * source + (spot >> 2))]
            for high, low, name in group:
                for k in range(HASHES):
                    key = (
                        high * (high_mult[k] << id_bits)
                        + low * (low_mult[k] << id_bits)
                        + (starts[number][k] + name)
                    ) & mask
                    owned = key < limit
                    for level in reversed(range(1, depth)):
                        stack[level] = jnp.where(owned, stack[level - 1], stack[level])
                    stack[0] = jnp.where(owned, key, stack[0])
        return tuple(stack)

    def receive(step, stack):
        across(step).wait_recv()
        over(step).start()
        over(step - 1).wait_recv()
        return consume(me ^ (step - 1), stack)

    stack = (jnp.full((8, LANES), invalid, I32),) * depth
    stack = lax.fori_loop(1, dp - 1, receive, stack)
    over(dp - 2).wait_recv()
    stack = consume(me ^ (dp - 2), stack)
    across(dp - 1).wait_recv()
    direct.wait_recv()
    stack = consume(me ^ (dp - 1), stack)

    spilled = jnp.where(stack[-1] < invalid, 1, 0)
    ends = []
    for b in range(buckets):
        below = jnp.zeros((8, LANES), I32)
        for value in stack:
            below = below + jnp.where(value < (((b + 1) * chunk * LANES) << id_bits), 1, 0)
        ends.append(jnp.broadcast_to(jnp.sum(below, axis=0, keepdims=True), (8, LANES)))
    begins = [jnp.zeros((8, LANES), I32)] + ends[:-1]
    for begin, end in zip(begins, ends):
        spilled = jnp.where(end - begin > cap, 1, spilled)
    spilled = jnp.where(begins[-1] > LANES - 1, 1, spilled)
    values = sort_lanes(list(stack))
    for level in range(depth):
        ranked[pl.ds(level, 8, stride=depth), :] = values[level]
    ordered = [ranked[8 * n : 8 * n + 8] for n in range(depth)]
    for b in range(buckets):
        lifted = lift(ordered, begins[b], cap) if b else ordered[: cap // 8]
        for n, tile in enumerate(lifted):
            codes[b, 8 * n : 8 * n + 8] = tile

    def fetch(b, number):
        rows = [codes[b, pl.ds(number * WIDE + n, 1), :] for n in range(WIDE)]
        code = jnp.concatenate(rows, axis=1)
        return (code >> (7 + id_bits)) - b * chunk, (code >> id_bits) & (LANES - 1), code & (ids - 1)

    def gather(number, total):
        for b in range(buckets):
            row, lane, name = fetch(b, number)
            found = jnp.dot(table[b], one_hot(row, chunk), preferred_element_type=F32)
            value = choose(found[:LANES] + found[LANES:], lane)
            for n in range(WIDE):
                at = slice(n * LANES, (n + 1) * LANES)
                total = total + jnp.where(iota((ids, LANES), 0) == name[:, at], value[:, at], 0.0)
        return total

    margin = lax.fori_loop(0, cap // WIDE, gather, jnp.zeros((ids, LANES), F32), unroll=UNROLL)
    near[column] = margin
    share_out(near, column, others("table"), near_send, near_recv)
    both[...] = jnp.zeros_like(both)

    @pl.when(later == 0)
    def _():
        await_loads()

    lax.fori_loop(later, last, gram, 0)
    margin = collect(near, near_send, near_recv)
    far[me] = margin
    share_out(far, me, others("dp"), far_send, far_recv)
    labels = jnp.concatenate(
        [features[n % 2, n // 2, slots : slots + 1] for n in range(ids)], axis=0
    ).astype(F32)

    for copies in (dp, dp - 1):
        done = features.at[half, pl.ds(0, copies)]
        wire(done, done, send_sem, send_sem, partner).wait_send()
    lax.fori_loop(last, parts_of_gram, gram, 0)
    held[device, 0:1] = gram_line()
    margin = collect(far, far_send, far_recv)
    residual = 1.0 / (1.0 + jnp.exp(-margin)) - labels

    def scatter(number, _):
        for b in range(buckets):
            row, lane, name = fetch(b, number)
            spread = jnp.concatenate([residual] * WIDE, axis=1)
            value = jnp.sum(jnp.where(iota(spread.shape, 0) == name, spread, 0.0), axis=0, keepdims=True)
            top = value.astype(BF16).astype(F32)
            here = stripes(lane, LANES)
            terms = [
                jnp.where(here, jnp.broadcast_to(piece, here.shape).astype(BF16), jnp.array(0, BF16))
                for piece in (top, value - top)
            ]
            both[b * chunk : (b + 1) * chunk] += lax.dot_general(
                one_hot(row, chunk), jnp.concatenate(terms, axis=0), (((1,), (1,)), ((), ())),
                preferred_element_type=F32,
            )
        return 0

    lax.fori_loop(0, cap // WIDE, scatter, 0, unroll=UNROLL)

    def product(number, sums):
        at = pl.ds(pl.multiple_of(number * 8, 8), 8)
        line = both[at, :LANES] + both[at, LANES:] + l2_weight * weights[at]
        gradient[at] = line
        return tuple(
            total + (steps, diffs)[n // mem][n % mem, at] * line for n, total in enumerate(sums)
        )

    sums = (jnp.zeros((8, LANES), F32),) * (2 * mem)
    sums = lax.fori_loop(0, lines // 8, product, sums, unroll=4)
    held[device, 1:2] = to_row([row_sums(list(sums[:mem])), row_sums(list(sums[mem:]))])
    held[device, 2:3] = jnp.max(spilled, axis=0, keepdims=True).astype(F32)
    peers = [
        {"dp": lax.rem(me + down, dp), "table": lax.rem(column + sideways, tables)}
        for down in range(dp)
        for sideways in range(tables)
        if down or sideways
    ]
    share_out(held, device, peers, held_send, held_recv)
    total = collect(held, held_send, held_recv)
    scale, on_diffs, on_steps = coefficients(total[0:1], total[1:2], mem)
    factors = [
        jnp.broadcast_to(-group[i : i + 1], (8, LANES)) for group in (on_steps, on_diffs) for i in range(mem)
    ]
    scale = jnp.broadcast_to(-scale[0:1], (8, LANES))

    def body(number, _):
        at = pl.ds(pl.multiple_of(number * 8, 8), 8)
        by_steps = scale * gradient[at]
        by_diffs = factors[mem] * diffs[0, at]
        for i in range(mem):
            by_steps = by_steps + factors[i] * steps[i, at]
            if i:
                by_diffs = by_diffs + factors[mem + i] * diffs[i, at]
        out_ref[at] = by_steps + by_diffs
        return 0

    lax.fori_loop(0, lines // 8, body, 0, unroll=4)
    flag_ref[0] = jnp.max(jnp.where(total[2:3] > 0.0, 1, 0))


def whole(high, low, labels, weights, steps, diffs):
    mem, width = steps.shape
    slots = high.shape[0]
    steps, diffs = (
        array.reshape(mem, width // LANES, LANES).transpose(1, 0, 2) for array in (steps, diffs)
    )
    dp, tables = lax.axis_size("dp"), lax.axis_size("table")
    devices = dp * tables
    rows = width // LANES
    chunk = min(2 * LANES, rows)
    buckets = rows // chunk
    cap = CAP if buckets > 1 else 3 * CAP
    DMA = pltpu.SemaphoreType.DMA
    parts = 8
    return pl.pallas_call(
        functools.partial(whole_kernel, (width * devices, slots, parts)),
        in_specs=[HBM] * 6,
        out_specs=[VMEM, SMEM],
        out_shape=[jax.ShapeDtypeStruct((rows, LANES), F32), jax.ShapeDtypeStruct((1,), I32)],
        scratch_shapes=[
            pltpu.VMEM((mem, rows, LANES), F32),
            pltpu.VMEM((mem, rows, LANES), F32),
            pltpu.VMEM((rows, LANES), F32),
            pltpu.VMEM((buckets, 2 * LANES, chunk), BF16),
            pltpu.VMEM((2, dp, 24 + slots, LANES), I32),
            pltpu.VMEM((8 * DEPTH, LANES), I32),
            pltpu.VMEM((buckets, cap, LANES), I32),
            pltpu.VMEM((rows, 2 * LANES), F32),
            pltpu.VMEM((rows, LANES), F32),
            pltpu.VMEM((tables, 2 * dp, LANES), F32),
            pltpu.VMEM((dp, 2 * dp, LANES), F32),
            pltpu.VMEM((devices, 3, LANES), F32),
            pltpu.VMEM((mem * mem + mem * (mem + 1) // 2, 8, LANES), F32),
            DMA((2,)),
            DMA,
            DMA((3,)),
            DMA,
            DMA((dp - 1,)),
            DMA((dp,)),
            DMA,
            DMA,
            DMA,
            DMA,
            DMA,
            DMA,
        ],
        compiler_params=pltpu.CompilerParams(
            vmem_limit_bytes=ROOM, collective_id=3, has_side_effects=True
        ),
        name="whole",
    )(high, low, labels, weights, steps, diffs)


def quick(feature_high, feature_low, labels, weights, history_steps, history_diffs):
    width = weights.shape[0]
    direction, flag = whole(
        feature_high, feature_low, labels[None, :], weights.reshape(width // LANES, LANES),
        history_steps, history_diffs,
    )
    return lax.cond(
        flag[0] > 0,
        lambda: local(feature_high, feature_low, labels, weights, history_steps, history_diffs),
        lambda: direction.reshape(-1),
    )


def solution(mesh):
    placed = (
        P(None, "dp"),
        P(None, "dp"),
        P("dp"),
        P(("dp", "table")),
        P(None, ("dp", "table")),
        P(None, ("dp", "table")),
    )
    return jax.shard_map(
        quick, mesh=mesh, in_specs=placed, out_specs=P(("dp", "table")), check_vma=False
    )
```

```python
import functools

import jax
import jax.numpy as jnp
from jax import lax
from jax.experimental import pallas as pl
from jax.experimental.pallas import tpu as pltpu
from jax.sharding import PartitionSpec as P

HASHES = 4
LANES = 128
BLOCK = 16
GROUP = 4
DEPTH = 24
CAP = 40
WIDE = 8
UNROLL = 5

high_mult = (40503, 96469, 255361, 362443)
low_mult = (2053, 6151, 12289, 98317)
slot_mult = (1543, 3079, 769, 3457)
shifts = (0, 1048573, 2097143, 3145727)
l2_weight = 1.0
BUDGET = 50 << 20
ROOM = 60 << 20
F32, BF16, I32 = jnp.float32, jnp.bfloat16, jnp.int32
MESH = pl.DeviceIdType.MESH
VMEM = pl.BlockSpec(memory_space=pltpu.VMEM)
HBM = pl.BlockSpec(memory_space=pltpu.HBM)
SMEM = pl.BlockSpec(memory_space=pltpu.SMEM)


def iota(shape, axis):
    return lax.broadcasted_iota(I32, shape, axis)


def split(value):
    top = value.astype(BF16)
    return top, (value - top.astype(F32)).astype(BF16)


def hot(index, count):
    shape = (count, index.shape[1])
    return jnp.where(iota(shape, 0) == index, 1.0, 0.0).astype(BF16)


def greet(peers):
    barrier = pltpu.get_barrier_semaphore()
    for peer in peers:
        pl.semaphore_signal(barrier, inc=1, device_id=peer, device_id_type=MESH)
    pl.semaphore_wait(barrier, len(peers))


def others(axis):
    size, me = lax.axis_size(axis), lax.axis_index(axis)
    return [{axis: lax.rem(me + step, size)} for step in range(1, size)]


def send(source, target, peers, send_sems, recv_sems):
    copies = []
    for number, peer in enumerate(peers):
        copy = pltpu.make_async_remote_copy(
            src_ref=source,
            dst_ref=target,
            send_sem=send_sems.at[number],
            recv_sem=recv_sems.at[number],
            device_id=peer,
            device_id_type=MESH,
        )
        copy.start()
        copies.append(copy)
    return copies


def stage(axis, held, value, sems):
    me = lax.axis_index(axis)
    held[me] = value
    return send(held.at[me], held.at[me], others(axis), *sems)


def finish(copies, held):
    for copy in copies:
        copy.wait()
    total = held[0]
    for number in range(1, held.shape[0]):
        total = total + held[number]
    return total


def sum_scratch(shape):
    near, far = lax.axis_size("table"), lax.axis_size("dp")
    return [
        pltpu.VMEM((near, *shape), F32),
        pltpu.VMEM((far, *shape), F32),
        pltpu.SemaphoreType.DMA((near - 1,)),
        pltpu.SemaphoreType.DMA((near - 1,)),
        pltpu.SemaphoreType.DMA((far - 1,)),
        pltpu.SemaphoreType.DMA((far - 1,)),
    ]


def load(steps_hbm, diffs_hbm, steps, diffs, sems, first=0):
    parts, width = sems.shape[1], steps.shape[1]
    pairs = []
    for part in range(parts):
        size = width // parts
        pair = []
        for kind, (source, target) in enumerate(((steps_hbm, steps), (diffs_hbm, diffs))):
            copy = pltpu.make_async_copy(
                source.at[:, pl.ds(first + part * size, size)],
                target.at[:, pl.ds(part * size, size)],
                sems.at[kind, part],
            )
            copy.start()
            pair.append(copy)
        pairs.append(pair)
    return pairs


def gram_part(steps, diffs, pairs, part, carry):
    mem = steps.shape[0]
    each = steps.shape[1] // len(pairs) // LANES
    for copy in pairs[part]:
        copy.wait()

    def body(number, carry):
        at = pl.ds(pl.multiple_of(number * LANES, LANES), LANES)
        step, diff = steps[:, at], diffs[:, at]
        new = []
        for i in range(mem):
            row = jnp.broadcast_to(diffs[i : i + 1, at], diff.shape)
            new.append(carry[2 * i] + step * row)
            new.append(carry[2 * i + 1] + diff * row)
        return tuple(new)

    return lax.fori_loop(part * each, (part + 1) * each, body, carry, unroll=4)


def to_row(columns):
    mem = columns[0].shape[0]
    total = jnp.zeros((mem, LANES), F32)
    spot = iota((mem, LANES), 1) - iota((mem, LANES), 0)
    for number, column in enumerate(columns):
        total = jnp.where(spot == number * mem, jnp.sum(column, axis=1, keepdims=True), total)
    return jnp.sum(total, axis=0, keepdims=True)


def from_row(row, number, mem):
    spot = iota((mem, LANES), 1) - iota((mem, LANES), 0)
    wide = jnp.broadcast_to(row, (mem, LANES))
    column = jnp.sum(jnp.where(spot == number * mem, wide, 0.0), axis=1, keepdims=True)
    return jnp.broadcast_to(column, (mem, LANES))


def gram_row(carry, mem):
    return to_row([carry[2 * i] for i in range(mem)] + [carry[2 * i + 1] for i in range(mem)])


def share_kernel(mine_ref, steps_hbm, diffs_hbm, every_ref, gram_ref,
                 steps, diffs, send_sems, recv_sems, sems):
    mem = steps.shape[0]
    pairs = load(steps_hbm, diffs_hbm, steps, diffs, sems)
    me = lax.axis_index("dp")
    every_ref[me] = mine_ref[...]
    peers = others("dp")
    greet(peers)
    sent = send(mine_ref, every_ref.at[me], peers, send_sems, recv_sems)
    carry = (jnp.zeros((mem, LANES), F32),) * (2 * mem)
    for part in range(len(pairs)):
        carry = gram_part(steps, diffs, pairs, part, carry)
    gram_ref[...] = gram_row(carry, mem)
    for copy in sent:
        copy.wait()


def share(mine, steps, diffs):
    mem, width = steps.shape
    dp = lax.axis_size("dp")
    return pl.pallas_call(
        share_kernel,
        in_specs=[VMEM] + [HBM] * 2,
        out_specs=[VMEM] * 2,
        out_shape=[
            jax.ShapeDtypeStruct((dp, *mine.shape), I32),
            jax.ShapeDtypeStruct((1, LANES), F32),
        ],
        scratch_shapes=[
            pltpu.VMEM((mem, 3 * width // 4), F32),
            pltpu.VMEM((mem, 3 * width // 4), F32),
            pltpu.SemaphoreType.DMA((dp - 1,)),
            pltpu.SemaphoreType.DMA((dp - 1,)),
            pltpu.SemaphoreType.DMA((2, 3)),
        ],
        compiler_params=pltpu.CompilerParams(
            vmem_limit_bytes=BUDGET, collective_id=0, has_side_effects=True
        ),
        name="share",
    )(mine, steps, diffs)


def reduce_kernel(margin_ref, gram_ref, steps_hbm, diffs_hbm, out_ref, grams_ref,
                  steps, diffs, load_sems, near, far, *sems):
    mem, size = steps.shape
    pairs = load(steps_hbm, diffs_hbm, steps, diffs, load_sems, steps_hbm.shape[1] - size)
    greet(others("table") + others("dp"))
    carry = (jnp.zeros((mem, LANES), F32),) * (2 * mem)
    copies = stage("table", near, margin_ref[...], sems[:2])
    copies = stage("dp", far, finish(copies, near), sems[2:])
    carry = gram_part(steps, diffs, pairs, 0, carry)
    grams_ref[...] = gram_ref[...] + gram_row(carry, mem)
    out_ref[...] = finish(copies, far)


def reduced(margin, grams, steps, diffs):
    mem, width = steps.shape
    return pl.pallas_call(
        reduce_kernel,
        in_specs=[VMEM] * 2 + [HBM] * 2,
        out_specs=[VMEM] * 2,
        out_shape=[
            jax.ShapeDtypeStruct(margin.shape, F32),
            jax.ShapeDtypeStruct((1, LANES), F32),
        ],
        scratch_shapes=[
            pltpu.VMEM((mem, width // 4), F32),
            pltpu.VMEM((mem, width // 4), F32),
            pltpu.SemaphoreType.DMA((2, 1)),
        ]
        + sum_scratch(margin.shape),
        compiler_params=pltpu.CompilerParams(
            vmem_limit_bytes=BUDGET, collective_id=1, has_side_effects=True
        ),
        name="reduce",
    )(margin, grams, steps, diffs)


def margin_kernel(count, subs, bits, slot_total, every_ref, weights_ref, margin_ref, slots_ref, levels_ref, table, features):
    device = lax.axis_index("dp") * lax.axis_size("table") + lax.axis_index("table")
    width = 1 << bits
    for number in range(2 * slot_total):
        features[number] = every_ref[:, number, :]
    tops, rests = split(weights_ref[...].T)
    table[: LANES] = tops
    table[LANES :] = rests

    def one_pass(number, _):
        base = number * BLOCK

        def body(slot, carry):
            seen, outs = carry[0], list(carry[1:])
            for sub in range(subs):
                group, half = sub // 2, sub % 2
                at = (pl.ds(group * 8, 8), pl.ds(half * LANES, LANES))
                high, low = features[(slot, *at)], features[(slot + slot_total, *at)]
                for k in range(HASHES):
                    index = (high * high_mult[k] + low * low_mult[k] + (slot * slot_mult[k] + shifts[k])) & (count - 1)
                    owned = (index >> bits) == device
                    place = jnp.where(owned, seen, -1)
                    code = (index & (width - 1)) | (sub << bits)
                    for level in range(BLOCK):
                        outs[level] = jnp.where(place == level, code, outs[level])
                    seen = seen + owned.astype(I32)
            return (seen, *outs)

        empty = jnp.full((8, LANES), -1, I32)
        final = lax.fori_loop(0, slot_total, body, (jnp.zeros((8, LANES), I32) - base,) + (empty,) * BLOCK)
        for level in range(BLOCK):
            slots_ref[:, base + level, :] = final[1 + level]
        return final[0] + base

    seen = one_pass(0, None)
    most = jnp.max(seen)
    lax.fori_loop(1, (most + BLOCK - 1) // BLOCK, lambda n, c: (one_pass(n, None), c)[1], 0)
    for row in range(8):
        levels_ref[row] = (jnp.max(seen[row : row + 1]) + GROUP - 1) // GROUP

    def rows(row, _):
        def body(number, total):
            codes = slots_ref[row, pl.ds(number * GROUP, GROUP), :]
            code = jnp.concatenate([codes[i : i + 1] for i in range(GROUP)], axis=1)
            local = code & (width - 1)
            found = jnp.dot(table[...], hot(local >> 7, width // LANES), preferred_element_type=F32)
            found = found[:LANES] + found[LANES:]
            chosen = jnp.where(iota(found.shape, 0) == (local & (LANES - 1)), found, 0.0)
            value = jnp.sum(chosen, axis=0, keepdims=True)
            sub = code >> bits
            for i in range(GROUP):
                at = slice(i * LANES, (i + 1) * LANES)
                total = total + jnp.where(iota((subs, LANES), 0) == sub[:, at], value[:, at], 0.0)
            return total

        total = lax.fori_loop(0, levels_ref[row], body, jnp.zeros((subs, LANES), F32))
        for sub in range(subs):
            here = iota((8, LANES), 0) == row
            margin_ref[sub] = jnp.where(here, total[sub : sub + 1], margin_ref[sub])
        return 0

    margin_ref[...] = jnp.zeros_like(margin_ref)
    lax.fori_loop(0, 8, rows, 0)


def margins(every, weights, count, subs, bits, slots):
    levels = -(-subs * HASHES * slots // BLOCK) * BLOCK
    return pl.pallas_call(
        functools.partial(margin_kernel, count, subs, bits, slots),
        in_specs=[VMEM] * 2,
        out_specs=[VMEM, VMEM, SMEM],
        out_shape=[
            jax.ShapeDtypeStruct((subs, 8, LANES), F32),
            jax.ShapeDtypeStruct((8, levels, LANES), I32),
            jax.ShapeDtypeStruct((8,), I32),
        ],
        scratch_shapes=[
            pltpu.VMEM((2 * LANES, (1 << bits) // LANES), BF16),
            pltpu.VMEM((2 * slots, every.shape[0], every.shape[2]), I32),
        ],
        compiler_params=pltpu.CompilerParams(vmem_limit_bytes=BUDGET),
        name="margins",
    )(every, weights)


def gradient_kernel(subs, bits, label_row, total_ref, every_ref, slots_ref, levels_ref, weights_ref,
                    gradient_ref, residual, both):
    width = 1 << bits
    for sub in range(subs):
        label = every_ref[sub // 2 * 8 : sub // 2 * 8 + 8, label_row, sub % 2 * LANES : sub % 2 * LANES + LANES]
        residual[:, sub, :] = 1.0 / (1.0 + jnp.exp(-total_ref[sub])) - label.astype(F32)
    both[...] = jnp.zeros_like(both)

    def rows(row, _):
        value = residual[row]

        def body(number, _):
            codes = slots_ref[row, pl.ds(number * GROUP, GROUP), :]
            code = jnp.concatenate([codes[i : i + 1] for i in range(GROUP)], axis=1)
            local = code & (width - 1)
            sub = code >> bits
            wide = jnp.concatenate([value] * GROUP, axis=1)
            mine = jnp.sum(jnp.where(iota(wide.shape, 0) == sub, wide, 0.0), axis=0, keepdims=True)
            column = iota((LANES, GROUP * LANES), 0) == (local & (LANES - 1))
            top, rest = split(jnp.where(column, mine, 0.0))
            terms = jnp.concatenate([top, rest], axis=0)
            both[...] += lax.dot_general(
                hot(local >> 7, width // LANES), terms, (((1,), (1,)), ((), ())), preferred_element_type=F32
            )
            return 0

        lax.fori_loop(0, levels_ref[row], body, 0)
        return 0

    lax.fori_loop(0, 8, rows, 0)
    gradient_ref[...] = both[:, :LANES] + both[:, LANES:] + l2_weight * weights_ref[...]


def gradients(total, every, slots, levels, weights, subs, bits, label_row):
    return pl.pallas_call(
        functools.partial(gradient_kernel, subs, bits, label_row),
        in_specs=[VMEM, VMEM, VMEM, SMEM, VMEM],
        out_specs=VMEM,
        out_shape=jax.ShapeDtypeStruct(weights.shape, F32),
        scratch_shapes=[
            pltpu.VMEM((8, subs, LANES), F32),
            pltpu.VMEM((weights.shape[0], 2 * LANES), F32),
        ],
        compiler_params=pltpu.CompilerParams(vmem_limit_bytes=BUDGET),
        name="gradient",
    )(total, every, slots, levels, weights)


def coefficients(grams, products, mem):
    place = iota((mem, LANES), 0)

    def pick(array, number):
        return jnp.broadcast_to(array[number : number + 1], (mem, LANES))

    cross = [from_row(grams, i, mem) for i in range(mem)]
    square = [from_row(grams, mem + i, mem) for i in range(mem)]
    pairs = [pick(cross[i], i) for i in range(mem)]
    inverse = [1.0 / pair for pair in pairs]
    by_step, by_diff = from_row(products, 0, mem), from_row(products, 1, mem)
    alphas = [None] * mem
    for i in reversed(range(mem)):
        alphas[i] = inverse[i] * pick(by_step, i)
        by_step = by_step - alphas[i] * cross[i]
        by_diff = by_diff - alphas[i] * square[i]
    scale = pairs[mem - 1] / pick(square[mem - 1], mem - 1)
    by_diff = scale * by_diff
    on_steps = jnp.zeros((mem, LANES), F32)
    on_diffs = jnp.zeros((mem, LANES), F32)
    for i in range(mem):
        extra = jnp.sum(on_steps * cross[i], axis=0, keepdims=True)
        beta = inverse[i] * (pick(by_diff, i) + extra)
        on_steps = jnp.where(place == i, alphas[i] - beta, on_steps)
        on_diffs = jnp.where(place == i, -scale * alphas[i], on_diffs)
    return scale, on_diffs, on_steps


def row_sums(tiles):
    place = iota((8, LANES), 0)
    gap = 1
    while len(tiles) > 1:
        low = (place & gap) == 0
        tiles = [
            jnp.where(low, a, b) + pltpu.roll(jnp.where(low, b, a), 8 - gap, 0)
            for a, b in zip(tiles[::2], tiles[1::2])
        ]
        gap *= 2
    return tiles[0]


def direction_kernel(grams_ref, gradient_ref, steps_hbm, diffs_hbm, out_ref,
                     steps, diffs, load_sems, held, send_sems, recv_sems):
    mem, width = steps.shape
    pairs = load(steps_hbm, diffs_hbm, steps, diffs, load_sems)
    near, far = lax.axis_size("table"), lax.axis_size("dp")
    column, row = lax.axis_index("table"), lax.axis_index("dp")
    peers = [
        {"dp": lax.rem(row + down, far), "table": lax.rem(column + across, near)}
        for down in range(far)
        for across in range(near)
        if down or across
    ]
    barrier = pltpu.get_barrier_semaphore()
    for peer in peers:
        pl.semaphore_signal(barrier, inc=1, device_id=peer, device_id_type=MESH)

    def product(number, carry):
        by_step, by_diff = carry
        for i in range(8):
            at = pl.ds(pl.multiple_of(number * 8 * LANES, LANES) + i * LANES, LANES)
            line = jnp.broadcast_to(gradient_ref[pl.ds(number * 8 + i, 1), :], (mem, LANES))
            by_step = by_step + steps[:, at] * line
            by_diff = by_diff + diffs[:, at] * line
        return by_step, by_diff

    carry = (jnp.zeros((mem, LANES), F32),) * 2
    each = width // len(pairs) // (8 * LANES)
    for part, pair in enumerate(pairs):
        for copy in pair:
            copy.wait()
        carry = lax.fori_loop(part * each, (part + 1) * each, product, carry)
    me = row * near + column
    held[me, 0:1] = grams_ref[...]
    held[me, 1:2] = to_row(carry)
    pl.semaphore_wait(barrier, len(peers))
    total = finish(send(held.at[me], held.at[me], peers, send_sems, recv_sems), held)
    scale, on_diffs, on_steps = coefficients(total[0:1], total[1:2], mem)
    scale, on_diffs, on_steps = -scale, -on_diffs, -on_steps

    def body(number, _):
        rows = []
        for i in range(8):
            at = pl.ds(pl.multiple_of(number * 8 * LANES, LANES) + i * LANES, LANES)
            rows.append(on_diffs * diffs[:, at] + on_steps * steps[:, at])
        at = pl.ds(pl.multiple_of(number * 8, 8), 8)
        out_ref[at, :] = scale * gradient_ref[at, :] + row_sums(rows)
        return 0

    lax.fori_loop(0, out_ref.shape[0] // 8, body, 0, unroll=2)


def directions(grams, gradient, steps, diffs):
    mem, width = steps.shape
    devices = lax.axis_size("dp") * lax.axis_size("table")
    return pl.pallas_call(
        direction_kernel,
        in_specs=[VMEM] * 2 + [HBM] * 2,
        out_specs=VMEM,
        out_shape=jax.ShapeDtypeStruct(gradient.shape, F32),
        scratch_shapes=[
            pltpu.VMEM((mem, width), F32),
            pltpu.VMEM((mem, width), F32),
            pltpu.SemaphoreType.DMA((2, 4)),
            pltpu.VMEM((devices, 2, LANES), F32),
            pltpu.SemaphoreType.DMA((devices - 1,)),
            pltpu.SemaphoreType.DMA((devices - 1,)),
        ],
        compiler_params=pltpu.CompilerParams(
            vmem_limit_bytes=BUDGET, collective_id=2, has_side_effects=True
        ),
        name="direction",
    )(grams, gradient, steps, diffs)


def local(feature_high, feature_low, labels, weights, history_steps, history_diffs):
    width = weights.shape[0]
    parts = lax.axis_size("dp")
    count = width * parts * lax.axis_size("table")
    bits = width.bit_length() - 1
    slots = feature_high.shape[0]
    subs = parts * feature_high.shape[1] // 1024
    table = weights.reshape(width // LANES, LANES)
    mine = jnp.concatenate([feature_high, feature_low, labels[None, :]], axis=0)
    every, partial_gram = share(mine, history_steps, history_diffs)
    margin, listed, levels = margins(every, table, count, subs, bits, slots)
    total, grams = reduced(margin, partial_gram, history_steps, history_diffs)
    gradient = gradients(total, every, listed, levels, table, subs, bits, 2 * slots)
    return directions(grams, gradient, history_steps, history_diffs).reshape(-1)


def wire(source, target, send_sem, recv_sem, peer):
    return pltpu.make_async_remote_copy(
        src_ref=source,
        dst_ref=target,
        send_sem=send_sem,
        recv_sem=recv_sem,
        device_id=peer,
        device_id_type=MESH,
    )


def share_out(array, place, peers, send_sem, recv_sem):
    for peer in peers:
        wire(array.at[place], array.at[place], send_sem, recv_sem, peer).start()


def collect(array, send_sem, recv_sem):
    rest = array.at[pl.ds(0, array.shape[0] - 1)]
    wire(rest, rest, send_sem, recv_sem, others("table")[0]).wait()
    total = array[0]
    for number in range(1, array.shape[0]):
        total = total + array[number]
    return total


def merge_pairs(count):
    pairs = []
    size = 1
    while size < count:
        step = size
        while step >= 1:
            for base in range(step % size, count - step, 2 * step):
                for i in range(base, min(base + step, count - step)):
                    if i // (2 * size) == (i + step) // (2 * size):
                        pairs.append((i, i + step))
            step //= 2
        size *= 2
    return pairs


def settle(values):
    count = len(values)
    if count % 2:
        for i in range(count):
            for j in range(i + 1, count):
                low, high = values[i], values[j]
                values[i], values[j] = jnp.minimum(low, high), jnp.maximum(low, high)
        return values
    half = count // 2
    lows = [jnp.minimum(a, b) for a, b in zip(values[:half], values[half:])]
    highs = [jnp.maximum(a, b) for a, b in zip(values[:half], values[half:])]
    if half == 1:
        return lows + highs
    return settle(lows) + settle(highs)


def sort_lanes(values):
    spot = iota(values[0].shape, 0)
    bits = [(spot >> n) & 1 for n in range(3)]
    flips = -(bits[0] ^ bits[1] ^ bits[2])
    values = [value ^ flips for value in values]
    for i, j in merge_pairs(len(values)):
        low, high = values[i], values[j]
        values[i], values[j] = jnp.minimum(low, high), jnp.maximum(low, high)
    for level in range(3):
        flips = -bits[level]
        values = [value ^ flips for value in values]
        for inner in reversed(range(level + 1)):
            gap = 1 << inner
            upper = bits[inner] == 1
            values = [
                jnp.where(
                    upper,
                    jnp.maximum(value, pltpu.roll(value, gap, 0)),
                    jnp.minimum(value, pltpu.roll(value, 8 - gap, 0)),
                )
                for value in values
            ]
        values = settle(values)
    return values


def lift(tiles, offset, length):
    spot = iota(tiles[0].shape, 0)
    bit = 64
    while bit >= 8:
        keep = (bit - 1 + length + 7) // 8 + (1 if bit > 8 else 0)
        move = bit // 8
        taken = (offset & bit) != 0
        keep = min(keep, len(tiles) - move)
        tiles = [jnp.where(taken, tiles[n + move], tiles[n]) for n in range(keep)]
        bit //= 2
    while bit >= 1:
        taken = (offset & bit) != 0
        rolled = [pltpu.roll(tile, 8 - bit, 0) for tile in tiles]
        moved = [jnp.where(spot < 8 - bit, a, b) for a, b in zip(rolled, rolled[1:] + rolled[-1:])]
        tiles = [jnp.where(taken, a, b) for a, b in zip(moved, tiles)]
        bit //= 2
    return tiles[: length // 8]


def stripes(row, count):
    shape = (count, row.shape[1])
    value = jnp.broadcast_to(row.astype(F32), shape).astype(BF16)
    return iota(shape, 0).astype(BF16) == value


def one_hot(row, count):
    return jnp.where(stripes(row, count), jnp.array(1, BF16), jnp.array(0, BF16))


def choose(found, lane):
    size = found.shape[1]
    lane = jnp.broadcast_to(lane, (8, size))
    parts = [found[n : n + 8] for n in range(0, LANES, 8)]
    bit = 8
    while len(parts) > 1:
        taken = (lane & bit) != 0
        parts = [jnp.where(taken, b, a) for a, b in zip(parts[::2], parts[1::2])]
        bit *= 2
    chosen = jnp.where(iota((8, size), 0) == (lane & 7), parts[0], 0.0)
    return jnp.sum(chosen, axis=0, keepdims=True)


def whole_kernel(dims, high_hbm, low_hbm, labels_hbm, weights_hbm, steps_hbm, diffs_hbm,
                 out_ref, flag_ref,
                 steps, diffs, weights, table, features, ranked, codes, both, gradient,
                 near, far, held, grams,
                 load_sems, weight_sem, local_sems, send_sem, recv_sems, take_sems,
                 near_send, near_recv, far_send, far_recv, held_send, held_recv):
    count, slots, parts_of_gram = dims
    mem, lines = steps.shape[:2]
    width = lines * LANES
    bits = width.bit_length() - 1
    buckets, chunk = table.shape[0], table.shape[2]
    cap = codes.shape[1]
    dp, tables = lax.axis_size("dp"), lax.axis_size("table")
    me, column = lax.axis_index("dp"), lax.axis_index("table")
    ids = 2 * dp
    id_bits = ids.bit_length() - 1
    low_row = 24
    part_lines = lines // parts_of_gram

    loads = [
        pltpu.make_async_copy(source.at[:, i], target.at[i], load_sems.at[kind])
        for i in range(mem)
        for kind, (source, target) in enumerate(((steps_hbm, steps), (diffs_hbm, diffs)))
    ]

    def await_loads():
        pltpu.make_async_copy(steps, steps, load_sems.at[0]).wait()
        pltpu.make_async_copy(diffs, diffs, load_sems.at[1]).wait()

    half = column % 2
    partner = {"table": column + 1 - 2 * half}
    lanes = pl.ds(pl.multiple_of(half * LANES, LANES), LANES)
    mine = features.at[half, me]
    features[half, me, slots + 1 : low_row] = jnp.zeros((low_row - slots - 1, LANES), I32)
    locals_ = [
        pltpu.make_async_copy(high_hbm.at[:, lanes], mine.at[pl.ds(0, slots)], local_sems.at[0]),
        pltpu.make_async_copy(low_hbm.at[:, lanes], mine.at[pl.ds(low_row, slots)], local_sems.at[1]),
        pltpu.make_async_copy(labels_hbm.at[:, lanes], mine.at[pl.ds(slots, 1)], local_sems.at[2]),
    ]
    for copy in locals_:
        copy.start()
    barrier = pltpu.get_barrier_semaphore()
    opposite = {"dp": me ^ (dp - 1), "table": column + 1 - 2 * half}
    friends = [opposite] + [{"dp": me ^ n} for n in reversed(range(1, dp))] + [{"table": column ^ n} for n in range(1, tables)]
    for peer in friends:
        pl.semaphore_signal(barrier, inc=1, device_id=peer, device_id_type=MESH)

    for copy in loads:
        copy.start()
    weight_copy = pltpu.make_async_copy(weights_hbm, weights, weight_sem)
    weight_copy.start()

    half_mem = mem // 2
    passes = [
        [(steps, i, j) for i in range(0, half_mem) for j in range(mem)],
        [(steps, i, j) for i in range(half_mem, mem) for j in range(mem)],
        [(diffs, i, j) for i in range(mem) for j in range(i, mem)],
    ]

    def gram(part, _):
        first = 0
        for chosen in passes:
            size = len(chosen)

            def body(number, sums):
                at = pl.ds(pl.multiple_of(part * part_lines + number * 8, 8), 8)
                left = {i: chosen[0][0][i, at] for i in {i for _, i, _ in chosen}}
                right = left if chosen[0][0] is diffs else {j: diffs[j, at] for j in range(mem)}
                return tuple(total + left[i] * right[j] for total, (_, i, j) in zip(sums, chosen))

            sums = tuple(grams[first + n] for n in range(size))
            sums = lax.fori_loop(0, part_lines // 8, body, sums, unroll=2)
            for n in range(size):
                grams[first + n] = sums[n]
            first += size
        return 0

    def gram_line():
        where = {}
        for chosen in passes:
            for source, i, j in chosen:
                where[source is diffs, i, j] = len(where)
        columns = [row_sums([grams[where[False, j, i]] for j in range(mem)]) for i in range(mem)]
        columns += [
            row_sums([grams[where[True, min(i, j), max(i, j)]] for j in range(mem)]) for i in range(mem)
        ]
        return to_row(columns)

    later = ((dp - 1 - me) * parts_of_gram) // (2 * dp)
    last = later + (parts_of_gram - later + 2) // 3
    grams[...] = jnp.zeros_like(grams)
    for copy in locals_:
        copy.wait()

    pl.semaphore_wait(barrier, len(friends))

    def across(step):
        return wire(mine, mine, send_sem, recv_sems.at[step - 1], {"dp": me ^ step})

    def over(step):
        source = features.at[half, me ^ step]
        return wire(source, source, send_sem, take_sems.at[step], partner)

    def start_across(step, _):
        across(dp - step).start()
        return 0

    lax.fori_loop(1, dp, start_across, 0)
    direct = wire(mine, mine, send_sem, take_sems.at[dp - 1], opposite)
    direct.start()
    over(0).start()
    weight_copy.wait()
    for b in range(buckets):
        tops, rests = split(weights[b * chunk : (b + 1) * chunk].T)
        table[b, :LANES] = tops
        table[b, LANES:] = rests

    @pl.when(later > 0)
    def _():
        await_loads()
        lax.fori_loop(0, later, gram, 0)

    device = me * tables + column
    spot = iota((8, LANES), 0)
    invalid = 1 << 30
    depth = ranked.shape[0] // 8
    mask, limit = (count << id_bits) - 1, width << id_bits
    rests_of = slots % 8
    assert slots % 8 in (0, 4)
    tiles = [(8 * n + spot, True) for n in range(slots // 8)]
    if rests_of:
        tiles.append((slots - 4 + (spot & 3), False))
    starts = [
        [((slot * slot_mult[k] + shifts[k]) - device * width) << id_bits for k in range(HASHES)]
        for slot, _ in tiles
    ]

    def consume(source, stack):
        stack = list(stack)
        for number, (_, full) in enumerate(tiles):
            if full:
                group = [
                    (
                        features[h, source, 8 * number : 8 * number + 8],
                        features[h, source, low_row + 8 * number : low_row + 8 * number + 8],
                        2 * source + h,
                    )
                    for h in range(2)
                ]
            else:
                at = slots - 4
                pair = [
                    jnp.concatenate([features[h, source, at + base : at + base + 4] for h in range(2)], axis=0)
                    for base in (0, low_row)
                ]
                group = [(*pair, 2 * source + (spot >> 2))]
            for high, low, name in group:
                for k in range(HASHES):
                    key = (
                        high * (high_mult[k] << id_bits)
                        + low * (low_mult[k] << id_bits)
                        + (starts[number][k] + name)
                    ) & mask
                    owned = key < limit
                    for level in reversed(range(1, depth)):
                        stack[level] = jnp.where(owned, stack[level - 1], stack[level])
                    stack[0] = jnp.where(owned, key, stack[0])
        return tuple(stack)

    def receive(step, stack):
        across(step).wait_recv()
        over(step).start()
        over(step - 1).wait_recv()
        return consume(me ^ (step - 1), stack)

    stack = (jnp.full((8, LANES), invalid, I32),) * depth
    stack = lax.fori_loop(1, dp - 1, receive, stack)
    over(dp - 2).wait_recv()
    stack = consume(me ^ (dp - 2), stack)
    across(dp - 1).wait_recv()
    direct.wait_recv()
    stack = consume(me ^ (dp - 1), stack)

    spilled = jnp.where(stack[-1] < invalid, 1, 0)
    ends = []
    for b in range(buckets):
        below = jnp.zeros((8, LANES), I32)
        for value in stack:
            below = below + jnp.where(value < (((b + 1) * chunk * LANES) << id_bits), 1, 0)
        ends.append(jnp.broadcast_to(jnp.sum(below, axis=0, keepdims=True), (8, LANES)))
    begins = [jnp.zeros((8, LANES), I32)] + ends[:-1]
    for begin, end in zip(begins, ends):
        spilled = jnp.where(end - begin > cap, 1, spilled)
    spilled = jnp.where(begins[-1] > LANES - 1, 1, spilled)
    values = sort_lanes(list(stack))
    for level in range(depth):
        ranked[pl.ds(level, 8, stride=depth), :] = values[level]
    ordered = [ranked[8 * n : 8 * n + 8] for n in range(depth)]
    for b in range(buckets):
        lifted = lift(ordered, begins[b], cap) if b else ordered[: cap // 8]
        for n, tile in enumerate(lifted):
            codes[b, 8 * n : 8 * n + 8] = tile

    def fetch(b, number):
        rows = [codes[b, pl.ds(number * WIDE + n, 1), :] for n in range(WIDE)]
        code = jnp.concatenate(rows, axis=1)
        return (code >> (7 + id_bits)) - b * chunk, (code >> id_bits) & (LANES - 1), code & (ids - 1)

    def gather(number, total):
        for b in range(buckets):
            row, lane, name = fetch(b, number)
            found = jnp.dot(table[b], one_hot(row, chunk), preferred_element_type=F32)
            value = choose(found[:LANES] + found[LANES:], lane)
            for n in range(WIDE):
                at = slice(n * LANES, (n + 1) * LANES)
                total = total + jnp.where(iota((ids, LANES), 0) == name[:, at], value[:, at], 0.0)
        return total

    margin = lax.fori_loop(0, cap // WIDE, gather, jnp.zeros((ids, LANES), F32), unroll=UNROLL)
    near[column] = margin
    share_out(near, column, [{"table": column ^ n} for n in reversed(range(1, tables))], near_send, near_recv)
    both[...] = jnp.zeros_like(both)

    @pl.when(later == 0)
    def _():
        await_loads()

    lax.fori_loop(later, last, gram, 0)
    margin = collect(near, near_send, near_recv)
    far[me] = margin
    share_out(far, me, [{"dp": me ^ n} for n in reversed(range(1, dp))], far_send, far_recv)
    labels = jnp.concatenate(
        [features[n % 2, n // 2, slots : slots + 1] for n in range(ids)], axis=0
    ).astype(F32)

    for copies in (dp, dp - 1):
        done = features.at[half, pl.ds(0, copies)]
        wire(done, done, send_sem, send_sem, partner).wait_send()
    lax.fori_loop(last, parts_of_gram, gram, 0)
    held[device, 0:1] = gram_line()
    margin = collect(far, far_send, far_recv)
    residual = 1.0 / (1.0 + jnp.exp(-margin)) - labels

    def scatter(number, _):
        for b in range(buckets):
            row, lane, name = fetch(b, number)
            spread = jnp.concatenate([residual] * WIDE, axis=1)
            value = jnp.sum(jnp.where(iota(spread.shape, 0) == name, spread, 0.0), axis=0, keepdims=True)
            top = value.astype(BF16).astype(F32)
            here = stripes(lane, LANES)
            terms = [
                jnp.where(here, jnp.broadcast_to(piece, here.shape).astype(BF16), jnp.array(0, BF16))
                for piece in (top, value - top)
            ]
            both[b * chunk : (b + 1) * chunk] += lax.dot_general(
                one_hot(row, chunk), jnp.concatenate(terms, axis=0), (((1,), (1,)), ((), ())),
                preferred_element_type=F32,
            )
        return 0

    lax.fori_loop(0, cap // WIDE, scatter, 0, unroll=UNROLL)

    def product(number, sums):
        at = pl.ds(pl.multiple_of(number * 8, 8), 8)
        line = both[at, :LANES] + both[at, LANES:] + l2_weight * weights[at]
        gradient[at] = line
        return tuple(
            total + (steps, diffs)[n // mem][n % mem, at] * line for n, total in enumerate(sums)
        )

    sums = (jnp.zeros((8, LANES), F32),) * (2 * mem)
    sums = lax.fori_loop(0, lines // 8, product, sums, unroll=8)
    held[device, 1:2] = to_row([row_sums(list(sums[:mem])), row_sums(list(sums[mem:]))])
    held[device, 2:3] = jnp.max(spilled, axis=0, keepdims=True).astype(F32)
    peers = [
        {"dp": me ^ down, "table": column ^ sideways}
        for down in reversed(range(dp))
        for sideways in reversed(range(tables))
        if down or sideways
    ]
    share_out(held, device, peers, held_send, held_recv)
    total = collect(held, held_send, held_recv)
    scale, on_diffs, on_steps = coefficients(total[0:1], total[1:2], mem)
    factors = [
        jnp.broadcast_to(-group[i : i + 1], (8, LANES)) for group in (on_steps, on_diffs) for i in range(mem)
    ]
    scale = jnp.broadcast_to(-scale[0:1], (8, LANES))

    def body(number, _):
        at = pl.ds(pl.multiple_of(number * 8, 8), 8)
        by_steps = scale * gradient[at]
        by_diffs = factors[mem] * diffs[0, at]
        for i in range(mem):
            by_steps = by_steps + factors[i] * steps[i, at]
            if i:
                by_diffs = by_diffs + factors[mem + i] * diffs[i, at]
        out_ref[at] = by_steps + by_diffs
        return 0

    lax.fori_loop(0, lines // 8, body, 0, unroll=8)
    flag_ref[0] = jnp.max(jnp.where(total[2:3] > 0.0, 1, 0))


def whole(high, low, labels, weights, steps, diffs):
    mem, width = steps.shape
    slots = high.shape[0]
    steps, diffs = (
        array.reshape(mem, width // LANES, LANES).transpose(1, 0, 2) for array in (steps, diffs)
    )
    dp, tables = lax.axis_size("dp"), lax.axis_size("table")
    devices = dp * tables
    rows = width // LANES
    chunk = min(2 * LANES, rows)
    buckets = rows // chunk
    cap = CAP if buckets > 1 else 3 * CAP
    DMA = pltpu.SemaphoreType.DMA
    parts = 8
    return pl.pallas_call(
        functools.partial(whole_kernel, (width * devices, slots, parts)),
        in_specs=[HBM] * 6,
        out_specs=[VMEM, SMEM],
        out_shape=[jax.ShapeDtypeStruct((rows, LANES), F32), jax.ShapeDtypeStruct((1,), I32)],
        scratch_shapes=[
            pltpu.VMEM((mem, rows, LANES), F32),
            pltpu.VMEM((mem, rows, LANES), F32),
            pltpu.VMEM((rows, LANES), F32),
            pltpu.VMEM((buckets, 2 * LANES, chunk), BF16),
            pltpu.VMEM((2, dp, 24 + slots, LANES), I32),
            pltpu.VMEM((8 * DEPTH, LANES), I32),
            pltpu.VMEM((buckets, cap, LANES), I32),
            pltpu.VMEM((rows, 2 * LANES), F32),
            pltpu.VMEM((rows, LANES), F32),
            pltpu.VMEM((tables, 2 * dp, LANES), F32),
            pltpu.VMEM((dp, 2 * dp, LANES), F32),
            pltpu.VMEM((devices, 3, LANES), F32),
            pltpu.VMEM((mem * mem + mem * (mem + 1) // 2, 8, LANES), F32),
            DMA((2,)),
            DMA,
            DMA((3,)),
            DMA,
            DMA((dp - 1,)),
            DMA((dp,)),
            DMA,
            DMA,
            DMA,
            DMA,
            DMA,
            DMA,
        ],
        compiler_params=pltpu.CompilerParams(
            vmem_limit_bytes=ROOM, collective_id=3, has_side_effects=True
        ),
        name="whole",
    )(high, low, labels, weights, steps, diffs)


def quick(feature_high, feature_low, labels, weights, history_steps, history_diffs):
    width = weights.shape[0]
    direction, flag = whole(
        feature_high, feature_low, labels[None, :], weights.reshape(width // LANES, LANES),
        history_steps, history_diffs,
    )
    return lax.cond(
        flag[0] > 0,
        lambda: local(feature_high, feature_low, labels, weights, history_steps, history_diffs),
        lambda: direction.reshape(-1),
    )


def solution(mesh):
    placed = (
        P(None, "dp"),
        P(None, "dp"),
        P("dp"),
        P(("dp", "table")),
        P(None, ("dp", "table")),
        P(None, ("dp", "table")),
    )
    return jax.shard_map(
        quick, mesh=mesh, in_specs=placed, out_specs=P(("dp", "table")), check_vma=False
    )
```

```python
import functools

import jax
import jax.numpy as jnp
from jax import lax
from jax.experimental import pallas as pl
from jax.experimental.pallas import tpu as pltpu
from jax.sharding import PartitionSpec as P

HASHES = 4
LANES = 128
BLOCK = 16
GROUP = 4
DEPTH = 24
CAP = 40
WIDE = 8
UNROLL = 5

high_mult = (40503, 96469, 255361, 362443)
low_mult = (2053, 6151, 12289, 98317)
slot_mult = (1543, 3079, 769, 3457)
shifts = (0, 1048573, 2097143, 3145727)
l2_weight = 1.0
BUDGET = 50 << 20
ROOM = 60 << 20
F32, BF16, I32 = jnp.float32, jnp.bfloat16, jnp.int32
MESH = pl.DeviceIdType.MESH
VMEM = pl.BlockSpec(memory_space=pltpu.VMEM)
HBM = pl.BlockSpec(memory_space=pltpu.HBM)
SMEM = pl.BlockSpec(memory_space=pltpu.SMEM)


def iota(shape, axis):
    return lax.broadcasted_iota(I32, shape, axis)


def split(value):
    top = value.astype(BF16)
    return top, (value - top.astype(F32)).astype(BF16)


def hot(index, count):
    shape = (count, index.shape[1])
    return jnp.where(iota(shape, 0) == index, 1.0, 0.0).astype(BF16)


def greet(peers):
    barrier = pltpu.get_barrier_semaphore()
    for peer in peers:
        pl.semaphore_signal(barrier, inc=1, device_id=peer, device_id_type=MESH)
    pl.semaphore_wait(barrier, len(peers))


def others(axis):
    size, me = lax.axis_size(axis), lax.axis_index(axis)
    return [{axis: lax.rem(me + step, size)} for step in range(1, size)]


def send(source, target, peers, send_sems, recv_sems):
    copies = []
    for number, peer in enumerate(peers):
        copy = pltpu.make_async_remote_copy(
            src_ref=source,
            dst_ref=target,
            send_sem=send_sems.at[number],
            recv_sem=recv_sems.at[number],
            device_id=peer,
            device_id_type=MESH,
        )
        copy.start()
        copies.append(copy)
    return copies


def stage(axis, held, value, sems):
    me = lax.axis_index(axis)
    held[me] = value
    return send(held.at[me], held.at[me], others(axis), *sems)


def finish(copies, held):
    for copy in copies:
        copy.wait()
    total = held[0]
    for number in range(1, held.shape[0]):
        total = total + held[number]
    return total


def sum_scratch(shape):
    near, far = lax.axis_size("table"), lax.axis_size("dp")
    return [
        pltpu.VMEM((near, *shape), F32),
        pltpu.VMEM((far, *shape), F32),
        pltpu.SemaphoreType.DMA((near - 1,)),
        pltpu.SemaphoreType.DMA((near - 1,)),
        pltpu.SemaphoreType.DMA((far - 1,)),
        pltpu.SemaphoreType.DMA((far - 1,)),
    ]


def load(steps_hbm, diffs_hbm, steps, diffs, sems, first=0):
    parts, width = sems.shape[1], steps.shape[1]
    pairs = []
    for part in range(parts):
        size = width // parts
        pair = []
        for kind, (source, target) in enumerate(((steps_hbm, steps), (diffs_hbm, diffs))):
            copy = pltpu.make_async_copy(
                source.at[:, pl.ds(first + part * size, size)],
                target.at[:, pl.ds(part * size, size)],
                sems.at[kind, part],
            )
            copy.start()
            pair.append(copy)
        pairs.append(pair)
    return pairs


def gram_part(steps, diffs, pairs, part, carry):
    mem = steps.shape[0]
    each = steps.shape[1] // len(pairs) // LANES
    for copy in pairs[part]:
        copy.wait()

    def body(number, carry):
        at = pl.ds(pl.multiple_of(number * LANES, LANES), LANES)
        step, diff = steps[:, at], diffs[:, at]
        new = []
        for i in range(mem):
            row = jnp.broadcast_to(diffs[i : i + 1, at], diff.shape)
            new.append(carry[2 * i] + step * row)
            new.append(carry[2 * i + 1] + diff * row)
        return tuple(new)

    return lax.fori_loop(part * each, (part + 1) * each, body, carry, unroll=4)


def to_row(columns):
    mem = columns[0].shape[0]
    total = jnp.zeros((mem, LANES), F32)
    spot = iota((mem, LANES), 1) - iota((mem, LANES), 0)
    for number, column in enumerate(columns):
        total = jnp.where(spot == number * mem, jnp.sum(column, axis=1, keepdims=True), total)
    return jnp.sum(total, axis=0, keepdims=True)


def from_row(row, number, mem):
    spot = iota((mem, LANES), 1) - iota((mem, LANES), 0)
    wide = jnp.broadcast_to(row, (mem, LANES))
    column = jnp.sum(jnp.where(spot == number * mem, wide, 0.0), axis=1, keepdims=True)
    return jnp.broadcast_to(column, (mem, LANES))


def gram_row(carry, mem):
    return to_row([carry[2 * i] for i in range(mem)] + [carry[2 * i + 1] for i in range(mem)])


def share_kernel(mine_ref, steps_hbm, diffs_hbm, every_ref, gram_ref,
                 steps, diffs, send_sems, recv_sems, sems):
    mem = steps.shape[0]
    pairs = load(steps_hbm, diffs_hbm, steps, diffs, sems)
    me = lax.axis_index("dp")
    every_ref[me] = mine_ref[...]
    peers = others("dp")
    greet(peers)
    sent = send(mine_ref, every_ref.at[me], peers, send_sems, recv_sems)
    carry = (jnp.zeros((mem, LANES), F32),) * (2 * mem)
    for part in range(len(pairs)):
        carry = gram_part(steps, diffs, pairs, part, carry)
    gram_ref[...] = gram_row(carry, mem)
    for copy in sent:
        copy.wait()


def share(mine, steps, diffs):
    mem, width = steps.shape
    dp = lax.axis_size("dp")
    return pl.pallas_call(
        share_kernel,
        in_specs=[VMEM] + [HBM] * 2,
        out_specs=[VMEM] * 2,
        out_shape=[
            jax.ShapeDtypeStruct((dp, *mine.shape), I32),
            jax.ShapeDtypeStruct((1, LANES), F32),
        ],
        scratch_shapes=[
            pltpu.VMEM((mem, 3 * width // 4), F32),
            pltpu.VMEM((mem, 3 * width // 4), F32),
            pltpu.SemaphoreType.DMA((dp - 1,)),
            pltpu.SemaphoreType.DMA((dp - 1,)),
            pltpu.SemaphoreType.DMA((2, 3)),
        ],
        compiler_params=pltpu.CompilerParams(
            vmem_limit_bytes=BUDGET, collective_id=0, has_side_effects=True
        ),
        name="share",
    )(mine, steps, diffs)


def reduce_kernel(margin_ref, gram_ref, steps_hbm, diffs_hbm, out_ref, grams_ref,
                  steps, diffs, load_sems, near, far, *sems):
    mem, size = steps.shape
    pairs = load(steps_hbm, diffs_hbm, steps, diffs, load_sems, steps_hbm.shape[1] - size)
    greet(others("table") + others("dp"))
    carry = (jnp.zeros((mem, LANES), F32),) * (2 * mem)
    copies = stage("table", near, margin_ref[...], sems[:2])
    copies = stage("dp", far, finish(copies, near), sems[2:])
    carry = gram_part(steps, diffs, pairs, 0, carry)
    grams_ref[...] = gram_ref[...] + gram_row(carry, mem)
    out_ref[...] = finish(copies, far)


def reduced(margin, grams, steps, diffs):
    mem, width = steps.shape
    return pl.pallas_call(
        reduce_kernel,
        in_specs=[VMEM] * 2 + [HBM] * 2,
        out_specs=[VMEM] * 2,
        out_shape=[
            jax.ShapeDtypeStruct(margin.shape, F32),
            jax.ShapeDtypeStruct((1, LANES), F32),
        ],
        scratch_shapes=[
            pltpu.VMEM((mem, width // 4), F32),
            pltpu.VMEM((mem, width // 4), F32),
            pltpu.SemaphoreType.DMA((2, 1)),
        ]
        + sum_scratch(margin.shape),
        compiler_params=pltpu.CompilerParams(
            vmem_limit_bytes=BUDGET, collective_id=1, has_side_effects=True
        ),
        name="reduce",
    )(margin, grams, steps, diffs)


def margin_kernel(count, subs, bits, slot_total, every_ref, weights_ref, margin_ref, slots_ref, levels_ref, table, features):
    device = lax.axis_index("dp") * lax.axis_size("table") + lax.axis_index("table")
    width = 1 << bits
    for number in range(2 * slot_total):
        features[number] = every_ref[:, number, :]
    tops, rests = split(weights_ref[...].T)
    table[: LANES] = tops
    table[LANES :] = rests

    def one_pass(number, _):
        base = number * BLOCK

        def body(slot, carry):
            seen, outs = carry[0], list(carry[1:])
            for sub in range(subs):
                group, half = sub // 2, sub % 2
                at = (pl.ds(group * 8, 8), pl.ds(half * LANES, LANES))
                high, low = features[(slot, *at)], features[(slot + slot_total, *at)]
                for k in range(HASHES):
                    index = (high * high_mult[k] + low * low_mult[k] + (slot * slot_mult[k] + shifts[k])) & (count - 1)
                    owned = (index >> bits) == device
                    place = jnp.where(owned, seen, -1)
                    code = (index & (width - 1)) | (sub << bits)
                    for level in range(BLOCK):
                        outs[level] = jnp.where(place == level, code, outs[level])
                    seen = seen + owned.astype(I32)
            return (seen, *outs)

        empty = jnp.full((8, LANES), -1, I32)
        final = lax.fori_loop(0, slot_total, body, (jnp.zeros((8, LANES), I32) - base,) + (empty,) * BLOCK)
        for level in range(BLOCK):
            slots_ref[:, base + level, :] = final[1 + level]
        return final[0] + base

    seen = one_pass(0, None)
    most = jnp.max(seen)
    lax.fori_loop(1, (most + BLOCK - 1) // BLOCK, lambda n, c: (one_pass(n, None), c)[1], 0)
    for row in range(8):
        levels_ref[row] = (jnp.max(seen[row : row + 1]) + GROUP - 1) // GROUP

    def rows(row, _):
        def body(number, total):
            codes = slots_ref[row, pl.ds(number * GROUP, GROUP), :]
            code = jnp.concatenate([codes[i : i + 1] for i in range(GROUP)], axis=1)
            local = code & (width - 1)
            found = jnp.dot(table[...], hot(local >> 7, width // LANES), preferred_element_type=F32)
            found = found[:LANES] + found[LANES:]
            chosen = jnp.where(iota(found.shape, 0) == (local & (LANES - 1)), found, 0.0)
            value = jnp.sum(chosen, axis=0, keepdims=True)
            sub = code >> bits
            for i in range(GROUP):
                at = slice(i * LANES, (i + 1) * LANES)
                total = total + jnp.where(iota((subs, LANES), 0) == sub[:, at], value[:, at], 0.0)
            return total

        total = lax.fori_loop(0, levels_ref[row], body, jnp.zeros((subs, LANES), F32))
        for sub in range(subs):
            here = iota((8, LANES), 0) == row
            margin_ref[sub] = jnp.where(here, total[sub : sub + 1], margin_ref[sub])
        return 0

    margin_ref[...] = jnp.zeros_like(margin_ref)
    lax.fori_loop(0, 8, rows, 0)


def margins(every, weights, count, subs, bits, slots):
    levels = -(-subs * HASHES * slots // BLOCK) * BLOCK
    return pl.pallas_call(
        functools.partial(margin_kernel, count, subs, bits, slots),
        in_specs=[VMEM] * 2,
        out_specs=[VMEM, VMEM, SMEM],
        out_shape=[
            jax.ShapeDtypeStruct((subs, 8, LANES), F32),
            jax.ShapeDtypeStruct((8, levels, LANES), I32),
            jax.ShapeDtypeStruct((8,), I32),
        ],
        scratch_shapes=[
            pltpu.VMEM((2 * LANES, (1 << bits) // LANES), BF16),
            pltpu.VMEM((2 * slots, every.shape[0], every.shape[2]), I32),
        ],
        compiler_params=pltpu.CompilerParams(vmem_limit_bytes=BUDGET),
        name="margins",
    )(every, weights)


def gradient_kernel(subs, bits, label_row, total_ref, every_ref, slots_ref, levels_ref, weights_ref,
                    gradient_ref, residual, both):
    width = 1 << bits
    for sub in range(subs):
        label = every_ref[sub // 2 * 8 : sub // 2 * 8 + 8, label_row, sub % 2 * LANES : sub % 2 * LANES + LANES]
        residual[:, sub, :] = 1.0 / (1.0 + jnp.exp(-total_ref[sub])) - label.astype(F32)
    both[...] = jnp.zeros_like(both)

    def rows(row, _):
        value = residual[row]

        def body(number, _):
            codes = slots_ref[row, pl.ds(number * GROUP, GROUP), :]
            code = jnp.concatenate([codes[i : i + 1] for i in range(GROUP)], axis=1)
            local = code & (width - 1)
            sub = code >> bits
            wide = jnp.concatenate([value] * GROUP, axis=1)
            mine = jnp.sum(jnp.where(iota(wide.shape, 0) == sub, wide, 0.0), axis=0, keepdims=True)
            column = iota((LANES, GROUP * LANES), 0) == (local & (LANES - 1))
            top, rest = split(jnp.where(column, mine, 0.0))
            terms = jnp.concatenate([top, rest], axis=0)
            both[...] += lax.dot_general(
                hot(local >> 7, width // LANES), terms, (((1,), (1,)), ((), ())), preferred_element_type=F32
            )
            return 0

        lax.fori_loop(0, levels_ref[row], body, 0)
        return 0

    lax.fori_loop(0, 8, rows, 0)
    gradient_ref[...] = both[:, :LANES] + both[:, LANES:] + l2_weight * weights_ref[...]


def gradients(total, every, slots, levels, weights, subs, bits, label_row):
    return pl.pallas_call(
        functools.partial(gradient_kernel, subs, bits, label_row),
        in_specs=[VMEM, VMEM, VMEM, SMEM, VMEM],
        out_specs=VMEM,
        out_shape=jax.ShapeDtypeStruct(weights.shape, F32),
        scratch_shapes=[
            pltpu.VMEM((8, subs, LANES), F32),
            pltpu.VMEM((weights.shape[0], 2 * LANES), F32),
        ],
        compiler_params=pltpu.CompilerParams(vmem_limit_bytes=BUDGET),
        name="gradient",
    )(total, every, slots, levels, weights)


def coefficients(grams, products, mem):
    place = iota((mem, LANES), 0)

    def pick(array, number):
        return jnp.broadcast_to(array[number : number + 1], (mem, LANES))

    cross = [from_row(grams, i, mem) for i in range(mem)]
    square = [from_row(grams, mem + i, mem) for i in range(mem)]
    pairs = [pick(cross[i], i) for i in range(mem)]
    inverse = [1.0 / pair for pair in pairs]
    by_step, by_diff = from_row(products, 0, mem), from_row(products, 1, mem)
    alphas = [None] * mem
    for i in reversed(range(mem)):
        alphas[i] = inverse[i] * pick(by_step, i)
        by_step = by_step - alphas[i] * cross[i]
        by_diff = by_diff - alphas[i] * square[i]
    scale = pairs[mem - 1] / pick(square[mem - 1], mem - 1)
    by_diff = scale * by_diff
    on_steps = jnp.zeros((mem, LANES), F32)
    on_diffs = jnp.zeros((mem, LANES), F32)
    for i in range(mem):
        extra = jnp.sum(on_steps * cross[i], axis=0, keepdims=True)
        beta = inverse[i] * (pick(by_diff, i) + extra)
        on_steps = jnp.where(place == i, alphas[i] - beta, on_steps)
        on_diffs = jnp.where(place == i, -scale * alphas[i], on_diffs)
    return scale, on_diffs, on_steps


def row_sums(tiles):
    place = iota((8, LANES), 0)
    gap = 1
    while len(tiles) > 1:
        low = (place & gap) == 0
        tiles = [
            jnp.where(low, a, b) + pltpu.roll(jnp.where(low, b, a), 8 - gap, 0)
            for a, b in zip(tiles[::2], tiles[1::2])
        ]
        gap *= 2
    return tiles[0]


def direction_kernel(grams_ref, gradient_ref, steps_hbm, diffs_hbm, out_ref,
                     steps, diffs, load_sems, held, send_sems, recv_sems):
    mem, width = steps.shape
    pairs = load(steps_hbm, diffs_hbm, steps, diffs, load_sems)
    near, far = lax.axis_size("table"), lax.axis_size("dp")
    column, row = lax.axis_index("table"), lax.axis_index("dp")
    peers = [
        {"dp": lax.rem(row + down, far), "table": lax.rem(column + across, near)}
        for down in range(far)
        for across in range(near)
        if down or across
    ]
    barrier = pltpu.get_barrier_semaphore()
    for peer in peers:
        pl.semaphore_signal(barrier, inc=1, device_id=peer, device_id_type=MESH)

    def product(number, carry):
        by_step, by_diff = carry
        for i in range(8):
            at = pl.ds(pl.multiple_of(number * 8 * LANES, LANES) + i * LANES, LANES)
            line = jnp.broadcast_to(gradient_ref[pl.ds(number * 8 + i, 1), :], (mem, LANES))
            by_step = by_step + steps[:, at] * line
            by_diff = by_diff + diffs[:, at] * line
        return by_step, by_diff

    carry = (jnp.zeros((mem, LANES), F32),) * 2
    each = width // len(pairs) // (8 * LANES)
    for part, pair in enumerate(pairs):
        for copy in pair:
            copy.wait()
        carry = lax.fori_loop(part * each, (part + 1) * each, product, carry)
    me = row * near + column
    held[me, 0:1] = grams_ref[...]
    held[me, 1:2] = to_row(carry)
    pl.semaphore_wait(barrier, len(peers))
    total = finish(send(held.at[me], held.at[me], peers, send_sems, recv_sems), held)
    scale, on_diffs, on_steps = coefficients(total[0:1], total[1:2], mem)
    scale, on_diffs, on_steps = -scale, -on_diffs, -on_steps

    def body(number, _):
        rows = []
        for i in range(8):
            at = pl.ds(pl.multiple_of(number * 8 * LANES, LANES) + i * LANES, LANES)
            rows.append(on_diffs * diffs[:, at] + on_steps * steps[:, at])
        at = pl.ds(pl.multiple_of(number * 8, 8), 8)
        out_ref[at, :] = scale * gradient_ref[at, :] + row_sums(rows)
        return 0

    lax.fori_loop(0, out_ref.shape[0] // 8, body, 0, unroll=2)


def directions(grams, gradient, steps, diffs):
    mem, width = steps.shape
    devices = lax.axis_size("dp") * lax.axis_size("table")
    return pl.pallas_call(
        direction_kernel,
        in_specs=[VMEM] * 2 + [HBM] * 2,
        out_specs=VMEM,
        out_shape=jax.ShapeDtypeStruct(gradient.shape, F32),
        scratch_shapes=[
            pltpu.VMEM((mem, width), F32),
            pltpu.VMEM((mem, width), F32),
            pltpu.SemaphoreType.DMA((2, 4)),
            pltpu.VMEM((devices, 2, LANES), F32),
            pltpu.SemaphoreType.DMA((devices - 1,)),
            pltpu.SemaphoreType.DMA((devices - 1,)),
        ],
        compiler_params=pltpu.CompilerParams(
            vmem_limit_bytes=BUDGET, collective_id=2, has_side_effects=True
        ),
        name="direction",
    )(grams, gradient, steps, diffs)


def local(feature_high, feature_low, labels, weights, history_steps, history_diffs):
    width = weights.shape[0]
    parts = lax.axis_size("dp")
    count = width * parts * lax.axis_size("table")
    bits = width.bit_length() - 1
    slots = feature_high.shape[0]
    subs = parts * feature_high.shape[1] // 1024
    table = weights.reshape(width // LANES, LANES)
    mine = jnp.concatenate([feature_high, feature_low, labels[None, :]], axis=0)
    every, partial_gram = share(mine, history_steps, history_diffs)
    margin, listed, levels = margins(every, table, count, subs, bits, slots)
    total, grams = reduced(margin, partial_gram, history_steps, history_diffs)
    gradient = gradients(total, every, listed, levels, table, subs, bits, 2 * slots)
    return directions(grams, gradient, history_steps, history_diffs).reshape(-1)


def wire(source, target, send_sem, recv_sem, peer):
    return pltpu.make_async_remote_copy(
        src_ref=source,
        dst_ref=target,
        send_sem=send_sem,
        recv_sem=recv_sem,
        device_id=peer,
        device_id_type=MESH,
    )


def share_out(array, place, peers, send_sem, recv_sem):
    for peer in peers:
        wire(array.at[place], array.at[place], send_sem, recv_sem, peer).start()


def collect(array, send_sem, recv_sem):
    rest = array.at[pl.ds(0, array.shape[0] - 1)]
    wire(rest, rest, send_sem, recv_sem, others("table")[0]).wait()
    total = array[0]
    for number in range(1, array.shape[0]):
        total = total + array[number]
    return total


def merge_pairs(count):
    pairs = []
    size = 1
    while size < count:
        step = size
        while step >= 1:
            for base in range(step % size, count - step, 2 * step):
                for i in range(base, min(base + step, count - step)):
                    if i // (2 * size) == (i + step) // (2 * size):
                        pairs.append((i, i + step))
            step //= 2
        size *= 2
    return pairs


def settle(values):
    count = len(values)
    if count % 2:
        for i in range(count):
            for j in range(i + 1, count):
                low, high = values[i], values[j]
                values[i], values[j] = jnp.minimum(low, high), jnp.maximum(low, high)
        return values
    half = count // 2
    lows = [jnp.minimum(a, b) for a, b in zip(values[:half], values[half:])]
    highs = [jnp.maximum(a, b) for a, b in zip(values[:half], values[half:])]
    if half == 1:
        return lows + highs
    return settle(lows) + settle(highs)


def sort_lanes(values):
    spot = iota(values[0].shape, 0)
    bits = [(spot >> n) & 1 for n in range(3)]
    flips = -(bits[0] ^ bits[1] ^ bits[2])
    values = [value ^ flips for value in values]
    for i, j in merge_pairs(len(values)):
        low, high = values[i], values[j]
        values[i], values[j] = jnp.minimum(low, high), jnp.maximum(low, high)
    for level in range(3):
        flips = -bits[level]
        values = [value ^ flips for value in values]
        for inner in reversed(range(level + 1)):
            gap = 1 << inner
            upper = bits[inner] == 1
            values = [
                jnp.where(
                    upper,
                    jnp.maximum(value, pltpu.roll(value, gap, 0)),
                    jnp.minimum(value, pltpu.roll(value, 8 - gap, 0)),
                )
                for value in values
            ]
        values = settle(values)
    return values


def lift(tiles, offset, length):
    spot = iota(tiles[0].shape, 0)
    bit = 64
    while bit >= 8:
        keep = (bit - 1 + length + 7) // 8 + (1 if bit > 8 else 0)
        move = bit // 8
        taken = (offset & bit) != 0
        keep = min(keep, len(tiles) - move)
        tiles = [jnp.where(taken, tiles[n + move], tiles[n]) for n in range(keep)]
        bit //= 2
    while bit >= 1:
        taken = (offset & bit) != 0
        rolled = [pltpu.roll(tile, 8 - bit, 0) for tile in tiles]
        moved = [jnp.where(spot < 8 - bit, a, b) for a, b in zip(rolled, rolled[1:] + rolled[-1:])]
        tiles = [jnp.where(taken, a, b) for a, b in zip(moved, tiles)]
        bit //= 2
    return tiles[: length // 8]


def stripes(row, count):
    shape = (count, row.shape[1])
    value = jnp.broadcast_to(row.astype(F32), shape).astype(BF16)
    return iota(shape, 0).astype(BF16) == value


def one_hot(row, count):
    return jnp.where(stripes(row, count), jnp.array(1, BF16), jnp.array(0, BF16))


def choose(found, lane):
    size = found.shape[1]
    lane = jnp.broadcast_to(lane, (8, size))
    parts = [found[n : n + 8] for n in range(0, LANES, 8)]
    bit = 8
    while len(parts) > 1:
        taken = (lane & bit) != 0
        parts = [jnp.where(taken, b, a) for a, b in zip(parts[::2], parts[1::2])]
        bit *= 2
    chosen = jnp.where(iota((8, size), 0) == (lane & 7), parts[0], 0.0)
    return jnp.sum(chosen, axis=0, keepdims=True)


def whole_kernel(dims, high_hbm, low_hbm, labels_hbm, weights_hbm, steps_hbm, diffs_hbm,
                 out_ref, flag_ref,
                 steps, diffs, weights, table, features, ranked, codes, both, gradient,
                 near, far, held, grams,
                 load_sems, weight_sem, local_sems, send_sem, recv_sems, take_sems,
                 near_send, near_recv, far_send, far_recv, held_send, held_recv):
    count, slots, parts_of_gram = dims
    mem, lines = steps.shape[:2]
    width = lines * LANES
    bits = width.bit_length() - 1
    buckets, chunk = table.shape[0], table.shape[2]
    cap = codes.shape[1]
    dp, tables = lax.axis_size("dp"), lax.axis_size("table")
    me, column = lax.axis_index("dp"), lax.axis_index("table")
    ids = 2 * dp
    id_bits = ids.bit_length() - 1
    low_row = 24
    part_lines = lines // parts_of_gram

    loads = [
        pltpu.make_async_copy(source.at[:, i], target.at[i], load_sems.at[kind])
        for i in range(mem)
        for kind, (source, target) in enumerate(((steps_hbm, steps), (diffs_hbm, diffs)))
    ]

    def await_loads():
        pltpu.make_async_copy(steps, steps, load_sems.at[0]).wait()
        pltpu.make_async_copy(diffs, diffs, load_sems.at[1]).wait()

    half = column % 2
    partner = {"table": column + 1 - 2 * half}
    lanes = pl.ds(pl.multiple_of(half * LANES, LANES), LANES)
    mine = features.at[half, me]
    features[half, me, slots + 1 : low_row] = jnp.zeros((low_row - slots - 1, LANES), I32)
    locals_ = [
        pltpu.make_async_copy(high_hbm.at[:, lanes], mine.at[pl.ds(0, slots)], local_sems.at[0]),
        pltpu.make_async_copy(low_hbm.at[:, lanes], mine.at[pl.ds(low_row, slots)], local_sems.at[1]),
        pltpu.make_async_copy(labels_hbm.at[:, lanes], mine.at[pl.ds(slots, 1)], local_sems.at[2]),
    ]
    for copy in locals_:
        copy.start()
    barrier = pltpu.get_barrier_semaphore()
    opposites = [{"dp": me ^ (dp - 1 - q), "table": column + 1 - 2 * half} for q in range(2)]
    friends = opposites + [{"dp": me ^ n} for n in reversed(range(1, dp))] + [{"table": column ^ n} for n in range(1, tables)]
    for peer in friends:
        pl.semaphore_signal(barrier, inc=1, device_id=peer, device_id_type=MESH)

    for copy in loads:
        copy.start()
    weight_copy = pltpu.make_async_copy(weights_hbm, weights, weight_sem)
    weight_copy.start()

    half_mem = mem // 2
    passes = [
        [(steps, i, j) for i in range(0, half_mem) for j in range(mem)],
        [(steps, i, j) for i in range(half_mem, mem) for j in range(mem)],
        [(diffs, i, j) for i in range(mem) for j in range(i, mem)],
    ]

    def gram(part, _):
        first = 0
        for chosen in passes:
            size = len(chosen)

            def body(number, sums):
                at = pl.ds(pl.multiple_of(part * part_lines + number * 8, 8), 8)
                left = {i: chosen[0][0][i, at] for i in {i for _, i, _ in chosen}}
                right = left if chosen[0][0] is diffs else {j: diffs[j, at] for j in range(mem)}
                return tuple(total + left[i] * right[j] for total, (_, i, j) in zip(sums, chosen))

            sums = tuple(grams[first + n] for n in range(size))
            sums = lax.fori_loop(0, part_lines // 8, body, sums, unroll=4)
            for n in range(size):
                grams[first + n] = sums[n]
            first += size
        return 0

    def gram_line():
        where = {}
        for chosen in passes:
            for source, i, j in chosen:
                where[source is diffs, i, j] = len(where)
        columns = [row_sums([grams[where[False, j, i]] for j in range(mem)]) for i in range(mem)]
        columns += [
            row_sums([grams[where[True, min(i, j), max(i, j)]] for j in range(mem)]) for i in range(mem)
        ]
        return to_row(columns)

    later = ((dp - 1 - me) * parts_of_gram) // (2 * dp)
    last = later + (parts_of_gram - later + 2) // 3
    grams[...] = jnp.zeros_like(grams)
    for copy in locals_:
        copy.wait()

    pl.semaphore_wait(barrier, len(friends))

    def across(step):
        return wire(mine, mine, send_sem, recv_sems.at[step - 1], {"dp": me ^ step})

    def over(step):
        source = features.at[half, me ^ step]
        return wire(source, source, send_sem, take_sems.at[step], partner)

    def start_across(step, _):
        across(dp - step).start()
        return 0

    lax.fori_loop(1, dp, start_across, 0)
    direct1 = wire(mine, mine, send_sem, take_sems.at[dp - 1], opposites[0])
    direct1.start()
    direct2 = wire(mine, mine, send_sem, take_sems.at[dp - 2], opposites[1])
    direct2.start()
    over(0).start()
    weight_copy.wait()
    for b in range(buckets):
        tops, rests = split(weights[b * chunk : (b + 1) * chunk].T)
        table[b, :LANES] = tops
        table[b, LANES:] = rests

    @pl.when(later > 0)
    def _():
        await_loads()
        lax.fori_loop(0, later, gram, 0)

    device = me * tables + column
    spot = iota((8, LANES), 0)
    invalid = 1 << 30
    depth = ranked.shape[0] // 8
    mask, limit = (count << id_bits) - 1, width << id_bits
    rests_of = slots % 8
    assert slots % 8 in (0, 4)
    tiles = [(8 * n + spot, True) for n in range(slots // 8)]
    if rests_of:
        tiles.append((slots - 4 + (spot & 3), False))
    starts = [
        [((slot * slot_mult[k] + shifts[k]) - device * width) << id_bits for k in range(HASHES)]
        for slot, _ in tiles
    ]

    def consume(source, stack):
        stack = list(stack)
        for number, (_, full) in enumerate(tiles):
            if full:
                group = [
                    (
                        features[h, source, 8 * number : 8 * number + 8],
                        features[h, source, low_row + 8 * number : low_row + 8 * number + 8],
                        2 * source + h,
                    )
                    for h in range(2)
                ]
            else:
                at = slots - 4
                pair = [
                    jnp.concatenate([features[h, source, at + base : at + base + 4] for h in range(2)], axis=0)
                    for base in (0, low_row)
                ]
                group = [(*pair, 2 * source + (spot >> 2))]
            for high, low, name in group:
                for k in range(HASHES):
                    key = (
                        high * (high_mult[k] << id_bits)
                        + low * (low_mult[k] << id_bits)
                        + (starts[number][k] + name)
                    ) & mask
                    owned = key < limit
                    for level in reversed(range(1, depth)):
                        stack[level] = jnp.where(owned, stack[level - 1], stack[level])
                    stack[0] = jnp.where(owned, key, stack[0])
        return tuple(stack)

    def receive(step, stack):
        across(step).wait_recv()
        over(step).start()
        over(step - 1).wait_recv()
        return consume(me ^ (step - 1), stack)

    stack = (jnp.full((8, LANES), invalid, I32),) * depth
    stack = lax.fori_loop(1, dp - 2, receive, stack)
    over(dp - 3).wait_recv()
    stack = consume(me ^ (dp - 3), stack)
    across(dp - 2).wait_recv()
    direct2.wait_recv()
    stack = consume(me ^ (dp - 2), stack)
    across(dp - 1).wait_recv()
    direct1.wait_recv()
    stack = consume(me ^ (dp - 1), stack)

    spilled = jnp.where(stack[-1] < invalid, 1, 0)
    ends = []
    for b in range(buckets):
        below = jnp.zeros((8, LANES), I32)
        for value in stack:
            below = below + jnp.where(value < (((b + 1) * chunk * LANES) << id_bits), 1, 0)
        ends.append(jnp.broadcast_to(jnp.sum(below, axis=0, keepdims=True), (8, LANES)))
    begins = [jnp.zeros((8, LANES), I32)] + ends[:-1]
    for begin, end in zip(begins, ends):
        spilled = jnp.where(end - begin > cap, 1, spilled)
    spilled = jnp.where(begins[-1] > LANES - 1, 1, spilled)
    values = sort_lanes(list(stack))
    for level in range(depth):
        ranked[pl.ds(level, 8, stride=depth), :] = values[level]
    ordered = [ranked[8 * n : 8 * n + 8] for n in range(depth)]
    for b in range(buckets):
        lifted = lift(ordered, begins[b], cap) if b else ordered[: cap // 8]
        for n, tile in enumerate(lifted):
            codes[b, 8 * n : 8 * n + 8] = tile

    def fetch(b, number):
        rows = [codes[b, pl.ds(number * WIDE + n, 1), :] for n in range(WIDE)]
        code = jnp.concatenate(rows, axis=1)
        return (code >> (7 + id_bits)) - b * chunk, (code >> id_bits) & (LANES - 1), code & (ids - 1)

    def gather(number, total):
        for b in range(buckets):
            row, lane, name = fetch(b, number)
            found = jnp.dot(table[b], one_hot(row, chunk), preferred_element_type=F32)
            value = choose(found[:LANES] + found[LANES:], lane)
            for n in range(WIDE):
                at = slice(n * LANES, (n + 1) * LANES)
                total = total + jnp.where(iota((ids, LANES), 0) == name[:, at], value[:, at], 0.0)
        return total

    margin = lax.fori_loop(0, cap // WIDE, gather, jnp.zeros((ids, LANES), F32), unroll=UNROLL)
    near[column] = margin
    share_out(near, column, [{"table": column ^ n} for n in reversed(range(1, tables))], near_send, near_recv)
    both[...] = jnp.zeros_like(both)

    @pl.when(later == 0)
    def _():
        await_loads()

    lax.fori_loop(later, last, gram, 0)
    margin = collect(near, near_send, near_recv)
    far[me] = margin
    share_out(far, me, [{"dp": me ^ n} for n in reversed(range(1, dp))], far_send, far_recv)
    labels = jnp.concatenate(
        [features[n % 2, n // 2, slots : slots + 1] for n in range(ids)], axis=0
    ).astype(F32)

    for copies in (dp, dp - 1):
        done = features.at[half, pl.ds(0, copies)]
        wire(done, done, send_sem, send_sem, partner).wait_send()
    lax.fori_loop(last, parts_of_gram, gram, 0)
    held[device, 0:1] = gram_line()
    margin = collect(far, far_send, far_recv)
    residual = 1.0 / (1.0 + jnp.exp(-margin)) - labels

    def scatter(number, _):
        for b in range(buckets):
            row, lane, name = fetch(b, number)
            spread = jnp.concatenate([residual] * WIDE, axis=1)
            value = jnp.sum(jnp.where(iota(spread.shape, 0) == name, spread, 0.0), axis=0, keepdims=True)
            top = value.astype(BF16).astype(F32)
            here = stripes(lane, LANES)
            terms = [
                jnp.where(here, jnp.broadcast_to(piece, here.shape).astype(BF16), jnp.array(0, BF16))
                for piece in (top, value - top)
            ]
            both[b * chunk : (b + 1) * chunk] += lax.dot_general(
                one_hot(row, chunk), jnp.concatenate(terms, axis=0), (((1,), (1,)), ((), ())),
                preferred_element_type=F32,
            )
        return 0

    lax.fori_loop(0, cap // WIDE, scatter, 0, unroll=UNROLL)

    def product(number, sums):
        at = pl.ds(pl.multiple_of(number * 8, 8), 8)
        line = both[at, :LANES] + both[at, LANES:] + l2_weight * weights[at]
        gradient[at] = line
        return tuple(
            total + (steps, diffs)[n // mem][n % mem, at] * line for n, total in enumerate(sums)
        )

    sums = (jnp.zeros((8, LANES), F32),) * (2 * mem)
    sums = lax.fori_loop(0, lines // 8, product, sums, unroll=8)
    held[device, 1:2] = to_row([row_sums(list(sums[:mem])), row_sums(list(sums[mem:]))])
    held[device, 2:3] = jnp.max(spilled, axis=0, keepdims=True).astype(F32)
    peers = [
        {"dp": me ^ down, "table": column ^ sideways}
        for down in reversed(range(dp))
        for sideways in reversed(range(tables))
        if down or sideways
    ]
    share_out(held, device, peers, held_send, held_recv)
    total = collect(held, held_send, held_recv)
    scale, on_diffs, on_steps = coefficients(total[0:1], total[1:2], mem)
    factors = [
        jnp.broadcast_to(-group[i : i + 1], (8, LANES)) for group in (on_steps, on_diffs) for i in range(mem)
    ]
    scale = jnp.broadcast_to(-scale[0:1], (8, LANES))

    def body(number, _):
        at = pl.ds(pl.multiple_of(number * 8, 8), 8)
        by_steps = scale * gradient[at]
        by_diffs = factors[mem] * diffs[0, at]
        for i in range(mem):
            by_steps = by_steps + factors[i] * steps[i, at]
            if i:
                by_diffs = by_diffs + factors[mem + i] * diffs[i, at]
        out_ref[at] = by_steps + by_diffs
        return 0

    lax.fori_loop(0, lines // 8, body, 0, unroll=8)
    flag_ref[0] = jnp.max(jnp.where(total[2:3] > 0.0, 1, 0))


def whole(high, low, labels, weights, steps, diffs):
    mem, width = steps.shape
    slots = high.shape[0]
    steps, diffs = (
        array.reshape(mem, width // LANES, LANES).transpose(1, 0, 2) for array in (steps, diffs)
    )
    dp, tables = lax.axis_size("dp"), lax.axis_size("table")
    devices = dp * tables
    rows = width // LANES
    chunk = min(2 * LANES, rows)
    buckets = rows // chunk
    cap = CAP if buckets > 1 else 3 * CAP
    DMA = pltpu.SemaphoreType.DMA
    parts = 8
    return pl.pallas_call(
        functools.partial(whole_kernel, (width * devices, slots, parts)),
        in_specs=[HBM] * 6,
        out_specs=[VMEM, SMEM],
        out_shape=[jax.ShapeDtypeStruct((rows, LANES), F32), jax.ShapeDtypeStruct((1,), I32)],
        scratch_shapes=[
            pltpu.VMEM((mem, rows, LANES), F32),
            pltpu.VMEM((mem, rows, LANES), F32),
            pltpu.VMEM((rows, LANES), F32),
            pltpu.VMEM((buckets, 2 * LANES, chunk), BF16),
            pltpu.VMEM((2, dp, 24 + slots, LANES), I32),
            pltpu.VMEM((8 * DEPTH, LANES), I32),
            pltpu.VMEM((buckets, cap, LANES), I32),
            pltpu.VMEM((rows, 2 * LANES), F32),
            pltpu.VMEM((rows, LANES), F32),
            pltpu.VMEM((tables, 2 * dp, LANES), F32),
            pltpu.VMEM((dp, 2 * dp, LANES), F32),
            pltpu.VMEM((devices, 3, LANES), F32),
            pltpu.VMEM((mem * mem + mem * (mem + 1) // 2, 8, LANES), F32),
            DMA((2,)),
            DMA,
            DMA((3,)),
            DMA,
            DMA((dp - 1,)),
            DMA((dp,)),
            DMA,
            DMA,
            DMA,
            DMA,
            DMA,
            DMA,
        ],
        compiler_params=pltpu.CompilerParams(
            vmem_limit_bytes=ROOM, collective_id=3, has_side_effects=True
        ),
        name="whole",
    )(high, low, labels, weights, steps, diffs)


def quick(feature_high, feature_low, labels, weights, history_steps, history_diffs):
    width = weights.shape[0]
    direction, flag = whole(
        feature_high, feature_low, labels[None, :], weights.reshape(width // LANES, LANES),
        history_steps, history_diffs,
    )
    return lax.cond(
        flag[0] > 0,
        lambda: local(feature_high, feature_low, labels, weights, history_steps, history_diffs),
        lambda: direction.reshape(-1),
    )


def solution(mesh):
    placed = (
        P(None, "dp"),
        P(None, "dp"),
        P("dp"),
        P(("dp", "table")),
        P(None, ("dp", "table")),
        P(None, ("dp", "table")),
    )
    return jax.shard_map(
        quick, mesh=mesh, in_specs=placed, out_specs=P(("dp", "table")), check_vma=False
    )
```

```python
import functools

import jax
import jax.numpy as jnp
from jax import lax
from jax.experimental import pallas as pl
from jax.experimental.pallas import tpu as pltpu
from jax.sharding import PartitionSpec as P

HASHES = 4
LANES = 128
BLOCK = 16
GROUP = 4
DEPTH = 24
CAP = 40
WIDE = 8
UNROLL = 5

high_mult = (40503, 96469, 255361, 362443)
low_mult = (2053, 6151, 12289, 98317)
slot_mult = (1543, 3079, 769, 3457)
shifts = (0, 1048573, 2097143, 3145727)
l2_weight = 1.0
BUDGET = 50 << 20
ROOM = 60 << 20
F32, BF16, I32 = jnp.float32, jnp.bfloat16, jnp.int32
MESH = pl.DeviceIdType.MESH
VMEM = pl.BlockSpec(memory_space=pltpu.VMEM)
HBM = pl.BlockSpec(memory_space=pltpu.HBM)
SMEM = pl.BlockSpec(memory_space=pltpu.SMEM)


def iota(shape, axis):
    return lax.broadcasted_iota(I32, shape, axis)


def split(value):
    top = value.astype(BF16)
    return top, (value - top.astype(F32)).astype(BF16)


def hot(index, count):
    shape = (count, index.shape[1])
    return jnp.where(iota(shape, 0) == index, 1.0, 0.0).astype(BF16)


def greet(peers):
    barrier = pltpu.get_barrier_semaphore()
    for peer in peers:
        pl.semaphore_signal(barrier, inc=1, device_id=peer, device_id_type=MESH)
    pl.semaphore_wait(barrier, len(peers))


def others(axis):
    size, me = lax.axis_size(axis), lax.axis_index(axis)
    return [{axis: lax.rem(me + step, size)} for step in range(1, size)]


def send(source, target, peers, send_sems, recv_sems):
    copies = []
    for number, peer in enumerate(peers):
        copy = pltpu.make_async_remote_copy(
            src_ref=source,
            dst_ref=target,
            send_sem=send_sems.at[number],
            recv_sem=recv_sems.at[number],
            device_id=peer,
            device_id_type=MESH,
        )
        copy.start()
        copies.append(copy)
    return copies


def stage(axis, held, value, sems):
    me = lax.axis_index(axis)
    held[me] = value
    return send(held.at[me], held.at[me], others(axis), *sems)


def finish(copies, held):
    for copy in copies:
        copy.wait()
    total = held[0]
    for number in range(1, held.shape[0]):
        total = total + held[number]
    return total


def sum_scratch(shape):
    near, far = lax.axis_size("table"), lax.axis_size("dp")
    return [
        pltpu.VMEM((near, *shape), F32),
        pltpu.VMEM((far, *shape), F32),
        pltpu.SemaphoreType.DMA((near - 1,)),
        pltpu.SemaphoreType.DMA((near - 1,)),
        pltpu.SemaphoreType.DMA((far - 1,)),
        pltpu.SemaphoreType.DMA((far - 1,)),
    ]


def load(steps_hbm, diffs_hbm, steps, diffs, sems, first=0):
    parts, width = sems.shape[1], steps.shape[1]
    pairs = []
    for part in range(parts):
        size = width // parts
        pair = []
        for kind, (source, target) in enumerate(((steps_hbm, steps), (diffs_hbm, diffs))):
            copy = pltpu.make_async_copy(
                source.at[:, pl.ds(first + part * size, size)],
                target.at[:, pl.ds(part * size, size)],
                sems.at[kind, part],
            )
            copy.start()
            pair.append(copy)
        pairs.append(pair)
    return pairs


def gram_part(steps, diffs, pairs, part, carry):
    mem = steps.shape[0]
    each = steps.shape[1] // len(pairs) // LANES
    for copy in pairs[part]:
        copy.wait()

    def body(number, carry):
        at = pl.ds(pl.multiple_of(number * LANES, LANES), LANES)
        step, diff = steps[:, at], diffs[:, at]
        new = []
        for i in range(mem):
            row = jnp.broadcast_to(diffs[i : i + 1, at], diff.shape)
            new.append(carry[2 * i] + step * row)
            new.append(carry[2 * i + 1] + diff * row)
        return tuple(new)

    return lax.fori_loop(part * each, (part + 1) * each, body, carry, unroll=4)


def to_row(columns):
    mem = columns[0].shape[0]
    total = jnp.zeros((mem, LANES), F32)
    spot = iota((mem, LANES), 1) - iota((mem, LANES), 0)
    for number, column in enumerate(columns):
        total = jnp.where(spot == number * mem, jnp.sum(column, axis=1, keepdims=True), total)
    return jnp.sum(total, axis=0, keepdims=True)


def from_row(row, number, mem):
    spot = iota((mem, LANES), 1) - iota((mem, LANES), 0)
    wide = jnp.broadcast_to(row, (mem, LANES))
    column = jnp.sum(jnp.where(spot == number * mem, wide, 0.0), axis=1, keepdims=True)
    return jnp.broadcast_to(column, (mem, LANES))


def gram_row(carry, mem):
    return to_row([carry[2 * i] for i in range(mem)] + [carry[2 * i + 1] for i in range(mem)])


def share_kernel(mine_ref, steps_hbm, diffs_hbm, every_ref, gram_ref,
                 steps, diffs, send_sems, recv_sems, sems):
    mem = steps.shape[0]
    pairs = load(steps_hbm, diffs_hbm, steps, diffs, sems)
    me = lax.axis_index("dp")
    every_ref[me] = mine_ref[...]
    peers = others("dp")
    greet(peers)
    sent = send(mine_ref, every_ref.at[me], peers, send_sems, recv_sems)
    carry = (jnp.zeros((mem, LANES), F32),) * (2 * mem)
    for part in range(len(pairs)):
        carry = gram_part(steps, diffs, pairs, part, carry)
    gram_ref[...] = gram_row(carry, mem)
    for copy in sent:
        copy.wait()


def share(mine, steps, diffs):
    mem, width = steps.shape
    dp = lax.axis_size("dp")
    return pl.pallas_call(
        share_kernel,
        in_specs=[VMEM] + [HBM] * 2,
        out_specs=[VMEM] * 2,
        out_shape=[
            jax.ShapeDtypeStruct((dp, *mine.shape), I32),
            jax.ShapeDtypeStruct((1, LANES), F32),
        ],
        scratch_shapes=[
            pltpu.VMEM((mem, 3 * width // 4), F32),
            pltpu.VMEM((mem, 3 * width // 4), F32),
            pltpu.SemaphoreType.DMA((dp - 1,)),
            pltpu.SemaphoreType.DMA((dp - 1,)),
            pltpu.SemaphoreType.DMA((2, 3)),
        ],
        compiler_params=pltpu.CompilerParams(
            vmem_limit_bytes=BUDGET, collective_id=0, has_side_effects=True
        ),
        name="share",
    )(mine, steps, diffs)


def reduce_kernel(margin_ref, gram_ref, steps_hbm, diffs_hbm, out_ref, grams_ref,
                  steps, diffs, load_sems, near, far, *sems):
    mem, size = steps.shape
    pairs = load(steps_hbm, diffs_hbm, steps, diffs, load_sems, steps_hbm.shape[1] - size)
    greet(others("table") + others("dp"))
    carry = (jnp.zeros((mem, LANES), F32),) * (2 * mem)
    copies = stage("table", near, margin_ref[...], sems[:2])
    copies = stage("dp", far, finish(copies, near), sems[2:])
    carry = gram_part(steps, diffs, pairs, 0, carry)
    grams_ref[...] = gram_ref[...] + gram_row(carry, mem)
    out_ref[...] = finish(copies, far)


def reduced(margin, grams, steps, diffs):
    mem, width = steps.shape
    return pl.pallas_call(
        reduce_kernel,
        in_specs=[VMEM] * 2 + [HBM] * 2,
        out_specs=[VMEM] * 2,
        out_shape=[
            jax.ShapeDtypeStruct(margin.shape, F32),
            jax.ShapeDtypeStruct((1, LANES), F32),
        ],
        scratch_shapes=[
            pltpu.VMEM((mem, width // 4), F32),
            pltpu.VMEM((mem, width // 4), F32),
            pltpu.SemaphoreType.DMA((2, 1)),
        ]
        + sum_scratch(margin.shape),
        compiler_params=pltpu.CompilerParams(
            vmem_limit_bytes=BUDGET, collective_id=1, has_side_effects=True
        ),
        name="reduce",
    )(margin, grams, steps, diffs)


def margin_kernel(count, subs, bits, slot_total, every_ref, weights_ref, margin_ref, slots_ref, levels_ref, table, features):
    device = lax.axis_index("dp") * lax.axis_size("table") + lax.axis_index("table")
    width = 1 << bits
    for number in range(2 * slot_total):
        features[number] = every_ref[:, number, :]
    tops, rests = split(weights_ref[...].T)
    table[: LANES] = tops
    table[LANES :] = rests

    def one_pass(number, _):
        base = number * BLOCK

        def body(slot, carry):
            seen, outs = carry[0], list(carry[1:])
            for sub in range(subs):
                group, half = sub // 2, sub % 2
                at = (pl.ds(group * 8, 8), pl.ds(half * LANES, LANES))
                high, low = features[(slot, *at)], features[(slot + slot_total, *at)]
                for k in range(HASHES):
                    index = (high * high_mult[k] + low * low_mult[k] + (slot * slot_mult[k] + shifts[k])) & (count - 1)
                    owned = (index >> bits) == device
                    place = jnp.where(owned, seen, -1)
                    code = (index & (width - 1)) | (sub << bits)
                    for level in range(BLOCK):
                        outs[level] = jnp.where(place == level, code, outs[level])
                    seen = seen + owned.astype(I32)
            return (seen, *outs)

        empty = jnp.full((8, LANES), -1, I32)
        final = lax.fori_loop(0, slot_total, body, (jnp.zeros((8, LANES), I32) - base,) + (empty,) * BLOCK)
        for level in range(BLOCK):
            slots_ref[:, base + level, :] = final[1 + level]
        return final[0] + base

    seen = one_pass(0, None)
    most = jnp.max(seen)
    lax.fori_loop(1, (most + BLOCK - 1) // BLOCK, lambda n, c: (one_pass(n, None), c)[1], 0)
    for row in range(8):
        levels_ref[row] = (jnp.max(seen[row : row + 1]) + GROUP - 1) // GROUP

    def rows(row, _):
        def body(number, total):
            codes = slots_ref[row, pl.ds(number * GROUP, GROUP), :]
            code = jnp.concatenate([codes[i : i + 1] for i in range(GROUP)], axis=1)
            local = code & (width - 1)
            found = jnp.dot(table[...], hot(local >> 7, width // LANES), preferred_element_type=F32)
            found = found[:LANES] + found[LANES:]
            chosen = jnp.where(iota(found.shape, 0) == (local & (LANES - 1)), found, 0.0)
            value = jnp.sum(chosen, axis=0, keepdims=True)
            sub = code >> bits
            for i in range(GROUP):
                at = slice(i * LANES, (i + 1) * LANES)
                total = total + jnp.where(iota((subs, LANES), 0) == sub[:, at], value[:, at], 0.0)
            return total

        total = lax.fori_loop(0, levels_ref[row], body, jnp.zeros((subs, LANES), F32))
        for sub in range(subs):
            here = iota((8, LANES), 0) == row
            margin_ref[sub] = jnp.where(here, total[sub : sub + 1], margin_ref[sub])
        return 0

    margin_ref[...] = jnp.zeros_like(margin_ref)
    lax.fori_loop(0, 8, rows, 0)


def margins(every, weights, count, subs, bits, slots):
    levels = -(-subs * HASHES * slots // BLOCK) * BLOCK
    return pl.pallas_call(
        functools.partial(margin_kernel, count, subs, bits, slots),
        in_specs=[VMEM] * 2,
        out_specs=[VMEM, VMEM, SMEM],
        out_shape=[
            jax.ShapeDtypeStruct((subs, 8, LANES), F32),
            jax.ShapeDtypeStruct((8, levels, LANES), I32),
            jax.ShapeDtypeStruct((8,), I32),
        ],
        scratch_shapes=[
            pltpu.VMEM((2 * LANES, (1 << bits) // LANES), BF16),
            pltpu.VMEM((2 * slots, every.shape[0], every.shape[2]), I32),
        ],
        compiler_params=pltpu.CompilerParams(vmem_limit_bytes=BUDGET),
        name="margins",
    )(every, weights)


def gradient_kernel(subs, bits, label_row, total_ref, every_ref, slots_ref, levels_ref, weights_ref,
                    gradient_ref, residual, both):
    width = 1 << bits
    for sub in range(subs):
        label = every_ref[sub // 2 * 8 : sub // 2 * 8 + 8, label_row, sub % 2 * LANES : sub % 2 * LANES + LANES]
        residual[:, sub, :] = 1.0 / (1.0 + jnp.exp(-total_ref[sub])) - label.astype(F32)
    both[...] = jnp.zeros_like(both)

    def rows(row, _):
        value = residual[row]

        def body(number, _):
            codes = slots_ref[row, pl.ds(number * GROUP, GROUP), :]
            code = jnp.concatenate([codes[i : i + 1] for i in range(GROUP)], axis=1)
            local = code & (width - 1)
            sub = code >> bits
            wide = jnp.concatenate([value] * GROUP, axis=1)
            mine = jnp.sum(jnp.where(iota(wide.shape, 0) == sub, wide, 0.0), axis=0, keepdims=True)
            column = iota((LANES, GROUP * LANES), 0) == (local & (LANES - 1))
            top, rest = split(jnp.where(column, mine, 0.0))
            terms = jnp.concatenate([top, rest], axis=0)
            both[...] += lax.dot_general(
                hot(local >> 7, width // LANES), terms, (((1,), (1,)), ((), ())), preferred_element_type=F32
            )
            return 0

        lax.fori_loop(0, levels_ref[row], body, 0)
        return 0

    lax.fori_loop(0, 8, rows, 0)
    gradient_ref[...] = both[:, :LANES] + both[:, LANES:] + l2_weight * weights_ref[...]


def gradients(total, every, slots, levels, weights, subs, bits, label_row):
    return pl.pallas_call(
        functools.partial(gradient_kernel, subs, bits, label_row),
        in_specs=[VMEM, VMEM, VMEM, SMEM, VMEM],
        out_specs=VMEM,
        out_shape=jax.ShapeDtypeStruct(weights.shape, F32),
        scratch_shapes=[
            pltpu.VMEM((8, subs, LANES), F32),
            pltpu.VMEM((weights.shape[0], 2 * LANES), F32),
        ],
        compiler_params=pltpu.CompilerParams(vmem_limit_bytes=BUDGET),
        name="gradient",
    )(total, every, slots, levels, weights)


def coefficients(grams, products, mem):
    place = iota((mem, LANES), 0)

    def pick(array, number):
        return jnp.broadcast_to(array[number : number + 1], (mem, LANES))

    cross = [from_row(grams, i, mem) for i in range(mem)]
    square = [from_row(grams, mem + i, mem) for i in range(mem)]
    pairs = [pick(cross[i], i) for i in range(mem)]
    inverse = [1.0 / pair for pair in pairs]
    by_step, by_diff = from_row(products, 0, mem), from_row(products, 1, mem)
    alphas = [None] * mem
    for i in reversed(range(mem)):
        alphas[i] = inverse[i] * pick(by_step, i)
        by_step = by_step - alphas[i] * cross[i]
        by_diff = by_diff - alphas[i] * square[i]
    scale = pairs[mem - 1] / pick(square[mem - 1], mem - 1)
    by_diff = scale * by_diff
    on_steps = jnp.zeros((mem, LANES), F32)
    on_diffs = jnp.zeros((mem, LANES), F32)
    for i in range(mem):
        extra = jnp.sum(on_steps * cross[i], axis=0, keepdims=True)
        beta = inverse[i] * (pick(by_diff, i) + extra)
        on_steps = jnp.where(place == i, alphas[i] - beta, on_steps)
        on_diffs = jnp.where(place == i, -scale * alphas[i], on_diffs)
    return scale, on_diffs, on_steps


def row_sums(tiles):
    place = iota((8, LANES), 0)
    gap = 1
    while len(tiles) > 1:
        low = (place & gap) == 0
        tiles = [
            jnp.where(low, a, b) + pltpu.roll(jnp.where(low, b, a), 8 - gap, 0)
            for a, b in zip(tiles[::2], tiles[1::2])
        ]
        gap *= 2
    return tiles[0]


def direction_kernel(grams_ref, gradient_ref, steps_hbm, diffs_hbm, out_ref,
                     steps, diffs, load_sems, held, send_sems, recv_sems):
    mem, width = steps.shape
    pairs = load(steps_hbm, diffs_hbm, steps, diffs, load_sems)
    near, far = lax.axis_size("table"), lax.axis_size("dp")
    column, row = lax.axis_index("table"), lax.axis_index("dp")
    peers = [
        {"dp": lax.rem(row + down, far), "table": lax.rem(column + across, near)}
        for down in range(far)
        for across in range(near)
        if down or across
    ]
    barrier = pltpu.get_barrier_semaphore()
    for peer in peers:
        pl.semaphore_signal(barrier, inc=1, device_id=peer, device_id_type=MESH)

    def product(number, carry):
        by_step, by_diff = carry
        for i in range(8):
            at = pl.ds(pl.multiple_of(number * 8 * LANES, LANES) + i * LANES, LANES)
            line = jnp.broadcast_to(gradient_ref[pl.ds(number * 8 + i, 1), :], (mem, LANES))
            by_step = by_step + steps[:, at] * line
            by_diff = by_diff + diffs[:, at] * line
        return by_step, by_diff

    carry = (jnp.zeros((mem, LANES), F32),) * 2
    each = width // len(pairs) // (8 * LANES)
    for part, pair in enumerate(pairs):
        for copy in pair:
            copy.wait()
        carry = lax.fori_loop(part * each, (part + 1) * each, product, carry)
    me = row * near + column
    held[me, 0:1] = grams_ref[...]
    held[me, 1:2] = to_row(carry)
    pl.semaphore_wait(barrier, len(peers))
    total = finish(send(held.at[me], held.at[me], peers, send_sems, recv_sems), held)
    scale, on_diffs, on_steps = coefficients(total[0:1], total[1:2], mem)
    scale, on_diffs, on_steps = -scale, -on_diffs, -on_steps

    def body(number, _):
        rows = []
        for i in range(8):
            at = pl.ds(pl.multiple_of(number * 8 * LANES, LANES) + i * LANES, LANES)
            rows.append(on_diffs * diffs[:, at] + on_steps * steps[:, at])
        at = pl.ds(pl.multiple_of(number * 8, 8), 8)
        out_ref[at, :] = scale * gradient_ref[at, :] + row_sums(rows)
        return 0

    lax.fori_loop(0, out_ref.shape[0] // 8, body, 0, unroll=2)


def directions(grams, gradient, steps, diffs):
    mem, width = steps.shape
    devices = lax.axis_size("dp") * lax.axis_size("table")
    return pl.pallas_call(
        direction_kernel,
        in_specs=[VMEM] * 2 + [HBM] * 2,
        out_specs=VMEM,
        out_shape=jax.ShapeDtypeStruct(gradient.shape, F32),
        scratch_shapes=[
            pltpu.VMEM((mem, width), F32),
            pltpu.VMEM((mem, width), F32),
            pltpu.SemaphoreType.DMA((2, 4)),
            pltpu.VMEM((devices, 2, LANES), F32),
            pltpu.SemaphoreType.DMA((devices - 1,)),
            pltpu.SemaphoreType.DMA((devices - 1,)),
        ],
        compiler_params=pltpu.CompilerParams(
            vmem_limit_bytes=BUDGET, collective_id=2, has_side_effects=True
        ),
        name="direction",
    )(grams, gradient, steps, diffs)


def local(feature_high, feature_low, labels, weights, history_steps, history_diffs):
    width = weights.shape[0]
    parts = lax.axis_size("dp")
    count = width * parts * lax.axis_size("table")
    bits = width.bit_length() - 1
    slots = feature_high.shape[0]
    subs = parts * feature_high.shape[1] // 1024
    table = weights.reshape(width // LANES, LANES)
    mine = jnp.concatenate([feature_high, feature_low, labels[None, :]], axis=0)
    every, partial_gram = share(mine, history_steps, history_diffs)
    margin, listed, levels = margins(every, table, count, subs, bits, slots)
    total, grams = reduced(margin, partial_gram, history_steps, history_diffs)
    gradient = gradients(total, every, listed, levels, table, subs, bits, 2 * slots)
    return directions(grams, gradient, history_steps, history_diffs).reshape(-1)


def wire(source, target, send_sem, recv_sem, peer):
    return pltpu.make_async_remote_copy(
        src_ref=source,
        dst_ref=target,
        send_sem=send_sem,
        recv_sem=recv_sem,
        device_id=peer,
        device_id_type=MESH,
    )


def share_out(array, place, peers, send_sem, recv_sem):
    for peer in peers:
        wire(array.at[place], array.at[place], send_sem, recv_sem, peer).start()


def collect(array, send_sem, recv_sem):
    rest = array.at[pl.ds(0, array.shape[0] - 1)]
    wire(rest, rest, send_sem, recv_sem, others("table")[0]).wait()
    total = array[0]
    for number in range(1, array.shape[0]):
        total = total + array[number]
    return total


def merge_pairs(count):
    pairs = []
    size = 1
    while size < count:
        step = size
        while step >= 1:
            for base in range(step % size, count - step, 2 * step):
                for i in range(base, min(base + step, count - step)):
                    if i // (2 * size) == (i + step) // (2 * size):
                        pairs.append((i, i + step))
            step //= 2
        size *= 2
    return pairs


def settle(values):
    count = len(values)
    if count % 2:
        for i in range(count):
            for j in range(i + 1, count):
                low, high = values[i], values[j]
                values[i], values[j] = jnp.minimum(low, high), jnp.maximum(low, high)
        return values
    half = count // 2
    lows = [jnp.minimum(a, b) for a, b in zip(values[:half], values[half:])]
    highs = [jnp.maximum(a, b) for a, b in zip(values[:half], values[half:])]
    if half == 1:
        return lows + highs
    return settle(lows) + settle(highs)


def sort_lanes(values):
    spot = iota(values[0].shape, 0)
    bits = [(spot >> n) & 1 for n in range(3)]
    flips = -(bits[0] ^ bits[1] ^ bits[2])
    values = [value ^ flips for value in values]
    for i, j in merge_pairs(len(values)):
        low, high = values[i], values[j]
        values[i], values[j] = jnp.minimum(low, high), jnp.maximum(low, high)
    for level in range(3):
        flips = -bits[level]
        values = [value ^ flips for value in values]
        for inner in reversed(range(level + 1)):
            gap = 1 << inner
            upper = bits[inner] == 1
            values = [
                jnp.where(
                    upper,
                    jnp.maximum(value, pltpu.roll(value, gap, 0)),
                    jnp.minimum(value, pltpu.roll(value, 8 - gap, 0)),
                )
                for value in values
            ]
        values = settle(values)
    return values


def lift(tiles, offset, length):
    spot = iota(tiles[0].shape, 0)
    bit = 64
    while bit >= 8:
        keep = (bit - 1 + length + 7) // 8 + (1 if bit > 8 else 0)
        move = bit // 8
        taken = (offset & bit) != 0
        keep = min(keep, len(tiles) - move)
        tiles = [jnp.where(taken, tiles[n + move], tiles[n]) for n in range(keep)]
        bit //= 2
    while bit >= 1:
        taken = (offset & bit) != 0
        rolled = [pltpu.roll(tile, 8 - bit, 0) for tile in tiles]
        moved = [jnp.where(spot < 8 - bit, a, b) for a, b in zip(rolled, rolled[1:] + rolled[-1:])]
        tiles = [jnp.where(taken, a, b) for a, b in zip(moved, tiles)]
        bit //= 2
    return tiles[: length // 8]


def stripes(row, count):
    shape = (count, row.shape[1])
    value = jnp.broadcast_to(row.astype(F32), shape).astype(BF16)
    return iota(shape, 0).astype(BF16) == value


def one_hot(row, count):
    return jnp.where(stripes(row, count), jnp.array(1, BF16), jnp.array(0, BF16))


def choose(found, lane):
    size = found.shape[1]
    lane = jnp.broadcast_to(lane, (8, size))
    parts = [found[n : n + 8] for n in range(0, LANES, 8)]
    bit = 8
    while len(parts) > 1:
        taken = (lane & bit) != 0
        parts = [jnp.where(taken, b, a) for a, b in zip(parts[::2], parts[1::2])]
        bit *= 2
    chosen = jnp.where(iota((8, size), 0) == (lane & 7), parts[0], 0.0)
    return jnp.sum(chosen, axis=0, keepdims=True)


def whole_kernel(dims, high_hbm, low_hbm, labels_hbm, weights_hbm, steps_hbm, diffs_hbm,
                 out_ref, flag_ref,
                 steps, diffs, weights, table, features, ranked, codes, both, gradient,
                 near, far, held, grams,
                 load_sems, weight_sem, local_sems, send_sem, recv_sems, take_sems,
                 near_send, near_recv, far_send, far_recv, held_send, held_recv):
    count, slots, parts_of_gram = dims
    mem, lines = steps.shape[:2]
    width = lines * LANES
    bits = width.bit_length() - 1
    buckets, chunk = table.shape[0], table.shape[2]
    cap = codes.shape[1]
    dp, tables = lax.axis_size("dp"), lax.axis_size("table")
    me, column = lax.axis_index("dp"), lax.axis_index("table")
    ids = 2 * dp
    id_bits = ids.bit_length() - 1
    low_row = 24
    part_lines = lines // parts_of_gram

    loads = [
        pltpu.make_async_copy(source.at[:, i], target.at[i], load_sems.at[kind])
        for i in range(mem)
        for kind, (source, target) in enumerate(((steps_hbm, steps), (diffs_hbm, diffs)))
    ]

    def await_loads():
        pltpu.make_async_copy(steps, steps, load_sems.at[0]).wait()
        pltpu.make_async_copy(diffs, diffs, load_sems.at[1]).wait()

    half = column % 2
    partner = {"table": column + 1 - 2 * half}
    barrier = pltpu.get_barrier_semaphore()
    opposites = [{"dp": me ^ (dp - 1 - q), "table": column + 1 - 2 * half} for q in range(2)]
    friends = opposites + [{"dp": me ^ n} for n in reversed(range(1, dp))] + [{"table": column ^ n} for n in range(1, tables)]
    for peer in friends:
        pl.semaphore_signal(barrier, inc=1, device_id=peer, device_id_type=MESH)
    lanes = pl.ds(pl.multiple_of(half * LANES, LANES), LANES)
    mine = features.at[half, me]
    features[half, me, slots + 1 : low_row] = jnp.zeros((low_row - slots - 1, LANES), I32)
    locals_ = [
        pltpu.make_async_copy(high_hbm.at[:, lanes], mine.at[pl.ds(0, slots)], local_sems.at[0]),
        pltpu.make_async_copy(low_hbm.at[:, lanes], mine.at[pl.ds(low_row, slots)], local_sems.at[1]),
        pltpu.make_async_copy(labels_hbm.at[:, lanes], mine.at[pl.ds(slots, 1)], local_sems.at[2]),
    ]
    for copy in locals_:
        copy.start()

    for copy in loads:
        copy.start()
    weight_copy = pltpu.make_async_copy(weights_hbm, weights, weight_sem)
    weight_copy.start()

    half_mem = mem // 2
    passes = [
        [(steps, i, j) for i in range(0, half_mem) for j in range(mem)],
        [(steps, i, j) for i in range(half_mem, mem) for j in range(mem)],
        [(diffs, i, j) for i in range(mem) for j in range(i, mem)],
    ]

    def gram(part, _):
        first = 0
        for chosen in passes:
            size = len(chosen)

            def body(number, sums):
                at = pl.ds(pl.multiple_of(part * part_lines + number * 8, 8), 8)
                left = {i: chosen[0][0][i, at] for i in {i for _, i, _ in chosen}}
                right = left if chosen[0][0] is diffs else {j: diffs[j, at] for j in range(mem)}
                return tuple(total + left[i] * right[j] for total, (_, i, j) in zip(sums, chosen))

            sums = tuple(grams[first + n] for n in range(size))
            sums = lax.fori_loop(0, part_lines // 8, body, sums, unroll=4)
            for n in range(size):
                grams[first + n] = sums[n]
            first += size
        return 0

    def gram_line():
        where = {}
        for chosen in passes:
            for source, i, j in chosen:
                where[source is diffs, i, j] = len(where)
        columns = [row_sums([grams[where[False, j, i]] for j in range(mem)]) for i in range(mem)]
        columns += [
            row_sums([grams[where[True, min(i, j), max(i, j)]] for j in range(mem)]) for i in range(mem)
        ]
        return to_row(columns)

    later = ((dp - 1 - me) * parts_of_gram) // (2 * dp)
    last = later + (parts_of_gram - later + 2) // 3
    grams[...] = jnp.zeros_like(grams)
    for copy in locals_:
        copy.wait()

    pl.semaphore_wait(barrier, len(friends))

    def across(step):
        return wire(mine, mine, send_sem, recv_sems.at[step - 1], {"dp": me ^ step})

    def over(step):
        source = features.at[half, me ^ step]
        return wire(source, source, send_sem, take_sems.at[step], partner)

    def start_across(step, _):
        across(dp - step).start()
        return 0

    lax.fori_loop(1, dp, start_across, 0)
    direct1 = wire(mine, mine, send_sem, take_sems.at[dp - 1], opposites[0])
    direct1.start()
    direct2 = wire(mine, mine, send_sem, take_sems.at[dp - 2], opposites[1])
    direct2.start()
    over(0).start()
    weight_copy.wait()
    for b in range(buckets):
        tops, rests = split(weights[b * chunk : (b + 1) * chunk].T)
        table[b, :LANES] = tops
        table[b, LANES:] = rests

    @pl.when(later > 0)
    def _():
        await_loads()
        lax.fori_loop(0, later, gram, 0)

    device = me * tables + column
    spot = iota((8, LANES), 0)
    invalid = 1 << 30
    depth = ranked.shape[0] // 8
    mask, limit = (count << id_bits) - 1, width << id_bits
    rests_of = slots % 8
    assert slots % 8 in (0, 4)
    tiles = [(8 * n + spot, True) for n in range(slots // 8)]
    if rests_of:
        tiles.append((slots - 4 + (spot & 3), False))
    starts = [
        [((slot * slot_mult[k] + shifts[k]) - device * width) << id_bits for k in range(HASHES)]
        for slot, _ in tiles
    ]

    def consume(source, stack):
        stack = list(stack)
        for number, (_, full) in enumerate(tiles):
            if full:
                group = [
                    (
                        features[h, source, 8 * number : 8 * number + 8],
                        features[h, source, low_row + 8 * number : low_row + 8 * number + 8],
                        2 * source + h,
                    )
                    for h in range(2)
                ]
            else:
                at = slots - 4
                pair = [
                    jnp.concatenate([features[h, source, at + base : at + base + 4] for h in range(2)], axis=0)
                    for base in (0, low_row)
                ]
                group = [(*pair, 2 * source + (spot >> 2))]
            for high, low, name in group:
                for k in range(HASHES):
                    key = (
                        high * (high_mult[k] << id_bits)
                        + low * (low_mult[k] << id_bits)
                        + (starts[number][k] + name)
                    ) & mask
                    owned = key < limit
                    for level in reversed(range(1, depth)):
                        stack[level] = jnp.where(owned, stack[level - 1], stack[level])
                    stack[0] = jnp.where(owned, key, stack[0])
        return tuple(stack)

    def receive(step, stack):
        across(step).wait_recv()
        over(step).start()
        over(step - 1).wait_recv()
        return consume(me ^ (step - 1), stack)

    stack = (jnp.full((8, LANES), invalid, I32),) * depth
    stack = lax.fori_loop(1, dp - 2, receive, stack)
    over(dp - 3).wait_recv()
    stack = consume(me ^ (dp - 3), stack)
    across(dp - 2).wait_recv()
    direct2.wait_recv()
    stack = consume(me ^ (dp - 2), stack)
    across(dp - 1).wait_recv()
    direct1.wait_recv()
    stack = consume(me ^ (dp - 1), stack)

    spilled = jnp.where(stack[-1] < invalid, 1, 0)
    ends = []
    for b in range(buckets):
        below = jnp.zeros((8, LANES), I32)
        for value in stack:
            below = below + jnp.where(value < (((b + 1) * chunk * LANES) << id_bits), 1, 0)
        ends.append(jnp.broadcast_to(jnp.sum(below, axis=0, keepdims=True), (8, LANES)))
    begins = [jnp.zeros((8, LANES), I32)] + ends[:-1]
    for begin, end in zip(begins, ends):
        spilled = jnp.where(end - begin > cap, 1, spilled)
    spilled = jnp.where(begins[-1] > LANES - 1, 1, spilled)
    values = sort_lanes(list(stack))
    for level in range(depth):
        ranked[pl.ds(level, 8, stride=depth), :] = values[level]
    ordered = [ranked[8 * n : 8 * n + 8] for n in range(depth)]
    for b in range(buckets):
        lifted = lift(ordered, begins[b], cap) if b else ordered[: cap // 8]
        for n, tile in enumerate(lifted):
            codes[b, 8 * n : 8 * n + 8] = tile

    def fetch(b, number):
        rows = [codes[b, pl.ds(number * WIDE + n, 1), :] for n in range(WIDE)]
        code = jnp.concatenate(rows, axis=1)
        return (code >> (7 + id_bits)) - b * chunk, (code >> id_bits) & (LANES - 1), code & (ids - 1)

    def gather(number, total):
        for b in range(buckets):
            row, lane, name = fetch(b, number)
            found = jnp.dot(table[b], one_hot(row, chunk), preferred_element_type=F32)
            value = choose(found[:LANES] + found[LANES:], lane)
            for n in range(WIDE):
                at = slice(n * LANES, (n + 1) * LANES)
                total = total + jnp.where(iota((ids, LANES), 0) == name[:, at], value[:, at], 0.0)
        return total

    margin = lax.fori_loop(0, cap // WIDE, gather, jnp.zeros((ids, LANES), F32), unroll=UNROLL)
    near[column] = margin
    share_out(near, column, [{"table": column ^ n} for n in reversed(range(1, tables))], near_send, near_recv)
    both[...] = jnp.zeros_like(both)

    @pl.when(later == 0)
    def _():
        await_loads()

    lax.fori_loop(later, last, gram, 0)
    margin = collect(near, near_send, near_recv)
    far[me] = margin
    share_out(far, me, [{"dp": me ^ n} for n in reversed(range(1, dp))], far_send, far_recv)
    labels = jnp.concatenate(
        [features[n % 2, n // 2, slots : slots + 1] for n in range(ids)], axis=0
    ).astype(F32)

    for copies in (dp, dp - 1):
        done = features.at[half, pl.ds(0, copies)]
        wire(done, done, send_sem, send_sem, partner).wait_send()
    lax.fori_loop(last, parts_of_gram, gram, 0)
    held[device, 0:1] = gram_line()
    margin = collect(far, far_send, far_recv)
    residual = 1.0 / (1.0 + jnp.exp(-margin)) - labels

    def scatter(number, _):
        for b in range(buckets):
            row, lane, name = fetch(b, number)
            spread = jnp.concatenate([residual] * WIDE, axis=1)
            value = jnp.sum(jnp.where(iota(spread.shape, 0) == name, spread, 0.0), axis=0, keepdims=True)
            top = value.astype(BF16).astype(F32)
            here = stripes(lane, LANES)
            terms = [
                jnp.where(here, jnp.broadcast_to(piece, here.shape).astype(BF16), jnp.array(0, BF16))
                for piece in (top, value - top)
            ]
            both[b * chunk : (b + 1) * chunk] += lax.dot_general(
                one_hot(row, chunk), jnp.concatenate(terms, axis=0), (((1,), (1,)), ((), ())),
                preferred_element_type=F32,
            )
        return 0

    lax.fori_loop(0, cap // WIDE, scatter, 0, unroll=UNROLL)

    def product(number, sums):
        at = pl.ds(pl.multiple_of(number * 8, 8), 8)
        line = both[at, :LANES] + both[at, LANES:] + l2_weight * weights[at]
        gradient[at] = line
        return tuple(
            total + (steps, diffs)[n // mem][n % mem, at] * line for n, total in enumerate(sums)
        )

    sums = (jnp.zeros((8, LANES), F32),) * (2 * mem)
    sums = lax.fori_loop(0, lines // 8, product, sums, unroll=8)
    held[device, 1:2] = to_row([row_sums(list(sums[:mem])), row_sums(list(sums[mem:]))])
    held[device, 2:3] = jnp.max(spilled, axis=0, keepdims=True).astype(F32)
    peers = [
        {"dp": me ^ down, "table": column ^ sideways}
        for down in reversed(range(dp))
        for sideways in reversed(range(tables))
        if down or sideways
    ]
    share_out(held, device, peers, held_send, held_recv)
    total = collect(held, held_send, held_recv)
    scale, on_diffs, on_steps = coefficients(total[0:1], total[1:2], mem)
    factors = [
        jnp.broadcast_to(-group[i : i + 1], (8, LANES)) for group in (on_steps, on_diffs) for i in range(mem)
    ]
    scale = jnp.broadcast_to(-scale[0:1], (8, LANES))

    def body(number, _):
        at = pl.ds(pl.multiple_of(number * 8, 8), 8)
        by_steps = scale * gradient[at]
        by_diffs = factors[mem] * diffs[0, at]
        for i in range(mem):
            by_steps = by_steps + factors[i] * steps[i, at]
            if i:
                by_diffs = by_diffs + factors[mem + i] * diffs[i, at]
        out_ref[at] = by_steps + by_diffs
        return 0

    lax.fori_loop(0, lines // 8, body, 0, unroll=8)
    flag_ref[0] = jnp.max(jnp.where(total[2:3] > 0.0, 1, 0))


def whole(high, low, labels, weights, steps, diffs):
    mem, width = steps.shape
    slots = high.shape[0]
    steps, diffs = (
        array.reshape(mem, width // LANES, LANES).transpose(1, 0, 2) for array in (steps, diffs)
    )
    dp, tables = lax.axis_size("dp"), lax.axis_size("table")
    devices = dp * tables
    rows = width // LANES
    chunk = min(2 * LANES, rows)
    buckets = rows // chunk
    cap = CAP if buckets > 1 else 3 * CAP
    DMA = pltpu.SemaphoreType.DMA
    parts = 8
    return pl.pallas_call(
        functools.partial(whole_kernel, (width * devices, slots, parts)),
        in_specs=[HBM] * 6,
        out_specs=[VMEM, SMEM],
        out_shape=[jax.ShapeDtypeStruct((rows, LANES), F32), jax.ShapeDtypeStruct((1,), I32)],
        scratch_shapes=[
            pltpu.VMEM((mem, rows, LANES), F32),
            pltpu.VMEM((mem, rows, LANES), F32),
            pltpu.VMEM((rows, LANES), F32),
            pltpu.VMEM((buckets, 2 * LANES, chunk), BF16),
            pltpu.VMEM((2, dp, 24 + slots, LANES), I32),
            pltpu.VMEM((8 * DEPTH, LANES), I32),
            pltpu.VMEM((buckets, cap, LANES), I32),
            pltpu.VMEM((rows, 2 * LANES), F32),
            pltpu.VMEM((rows, LANES), F32),
            pltpu.VMEM((tables, 2 * dp, LANES), F32),
            pltpu.VMEM((dp, 2 * dp, LANES), F32),
            pltpu.VMEM((devices, 3, LANES), F32),
            pltpu.VMEM((mem * mem + mem * (mem + 1) // 2, 8, LANES), F32),
            DMA((2,)),
            DMA,
            DMA((3,)),
            DMA,
            DMA((dp - 1,)),
            DMA((dp,)),
            DMA,
            DMA,
            DMA,
            DMA,
            DMA,
            DMA,
        ],
        compiler_params=pltpu.CompilerParams(
            vmem_limit_bytes=ROOM, collective_id=3, has_side_effects=True
        ),
        name="whole",
    )(high, low, labels, weights, steps, diffs)


def quick(feature_high, feature_low, labels, weights, history_steps, history_diffs):
    width = weights.shape[0]
    direction, flag = whole(
        feature_high, feature_low, labels[None, :], weights.reshape(width // LANES, LANES),
        history_steps, history_diffs,
    )
    return lax.cond(
        flag[0] > 0,
        lambda: local(feature_high, feature_low, labels, weights, history_steps, history_diffs),
        lambda: direction.reshape(-1),
    )


def solution(mesh):
    placed = (
        P(None, "dp"),
        P(None, "dp"),
        P("dp"),
        P(("dp", "table")),
        P(None, ("dp", "table")),
        P(None, ("dp", "table")),
    )
    return jax.shard_map(
        quick, mesh=mesh, in_specs=placed, out_specs=P(("dp", "table")), check_vma=False
    )
```
